32 devices in a mesh: dp: 8 (over z, y), tensor: 4 (over x, core).
Axes of the slice: x: 2, y: 2, z: 4, core: 2. Of those that a mesh axis runs over, the one named last changes fastest.
Arguments:
- tokens: bfloat16 [16384, 768], P(('dp', 'tensor')), may hold values from -6 to 6
- gene_counts: int32 [16], P('dp'), may hold values from 300 to 1024, as said below
- in_proj: bfloat16 [3, 768, 768], P(None, None, 'tensor'), may hold values from -0.21875 to 0.21875
- out_proj: bfloat16 [768, 768], P('tensor'), may hold values from -0.875 to 0.875
- up_proj: bfloat16 [768, 3072], P(None, 'tensor'), may hold values from -0.21875 to 0.21875
- down_proj: bfloat16 [3072, 768], P('tensor'), may hold values from -0.109375 to 0.109375
- gains: float32 [2, 768], replicated, may hold values from 0.1 to 1.9
- biases: float32 [2, 768], replicated, may hold values from -3 to 3
- cotangent: bfloat16 [16384, 768], P(('dp', 'tensor')), may hold values from -6 to 6
Outputs:
- block_out: bfloat16 [16384, 768], P(('dp', 'tensor'))
- input_grad: bfloat16 [16384, 768], P(('dp', 'tensor'))
- grad_in_proj: float32 [3, 768, 768], P(None, 'dp', 'tensor')
- grad_out_proj: float32 [768, 768], P('tensor', 'dp')
- grad_up_proj: float32 [768, 3072], P('dp', 'tensor')
- grad_down_proj: float32 [3072, 768], P('tensor', 'dp')
- grad_gains: float32 [2, 768], replicated
- grad_biases: float32 [2, 768], replicated
The draws below stay inside these ranges and needn't reach their ends.
Inputs may be any that keep to these rules, and one draw needn't show every extreme that they name: Cell c holds genes at its first gene_counts[c] positions and padding at the rest of its 1024 positions; in every draw one cell holds 1024 genes and one holds 300; most cells are short.
All inputs are finite; a program needn't handle non-finite values.
Results may differ from the reference program's by a relative error of at most 0.013.
The reference program's roundings to bfloat16 on the way count: a program that leaves them out, or rounds other values in their place, can miss the bound.
Values may be sent and summed in bfloat16 or wider, within the bound.
A program may use at most 128 MiB of HBM per device.

```python
import jax
import jax.numpy as jnp
from jax import lax

D = 768
HEADS = 12
HEAD_DIM = 64
FF = 3072
LEN = 1024
MINLEN = 300
CELLS = 16
TOKENS = 16384


def draw_gene_counts(key, part):
    keys = jax.random.split(key, 4)
    span = LEN - MINLEN + 1
    first = jax.random.randint(keys[0], (CELLS,), 0, span)
    second = jax.random.randint(keys[1], (CELLS,), 0, span)
    counts = MINLEN + jnp.minimum(first, second)
    longest = jax.random.randint(keys[2], (), 0, CELLS)
    shortest = (longest + 1 + jax.random.randint(keys[3], (), 0, CELLS - 1)) % CELLS
    counts = counts.at[shortest].set(MINLEN).at[longest].set(LEN)
    return counts.astype(jnp.int32)


def level_of(own_key, shape, cuts, smallest, largest):
    factor_of, own = 1.0, jax.random.fold_in(own_key, 6)
    for axis_at, blocks in cuts:
        draws = jnp.exp(jax.random.uniform(jax.random.fold_in(own, axis_at), (blocks,), jnp.float32, smallest / len(cuts), largest / len(cuts)))
        factor_of = factor_of * jnp.repeat(draws, shape[axis_at] // blocks).reshape([-1 if axis == axis_at else 1 for axis in range(len(shape))])
    return factor_of


def bell_draw(rng, shape, scale, bound, cuts=(), dtype=jnp.bfloat16):
    values = scale * jax.random.normal(rng, shape, jnp.float32)
    if cuts:
        values = values * level_of(rng, shape, cuts, -0.22, 0.18)
    return jnp.clip(values, -bound, bound).astype(dtype)


def setup_inputs(seed: int = 0) -> dict:
    streams_of = jax.random.split(jax.random.key(seed), 10)
    tokens = bell_draw(streams_of[0], (TOKENS, D), 1.0, 6.0, ((0, 32),))
    gene_counts = draw_gene_counts(jax.random.fold_in(streams_of[9], 71), 0)
    in_proj = bell_draw(streams_of[2], (3, D, D), D ** -0.5, 0.21875, ((2, 4),))
    out_proj = bell_draw(streams_of[3], (D, D), (D // 16) ** -0.5, 0.875, ((0, 4),))
    up_proj = bell_draw(streams_of[4], (D, FF), D ** -0.5, 0.21875, ((1, 4),))
    down_proj = bell_draw(streams_of[5], (FF, D), FF ** -0.5, 0.109375, ((0, 4),))
    gains = jnp.clip(1.0 + 0.18 * jax.random.normal(streams_of[6], (2, D), jnp.float32), 0.1, 1.9)
    biases = bell_draw(streams_of[7], (2, D), 0.5, 3.0, (), jnp.float32)
    cotangent = bell_draw(streams_of[8], (TOKENS, D), 1.0, 6.0, ((0, 32),))
    return {"tokens": tokens, "gene_counts": gene_counts, "in_proj": in_proj, "out_proj": out_proj, "up_proj": up_proj, "down_proj": down_proj, "gains": gains, "biases": biases, "cotangent": cotangent}


HIGH = lax.Precision.HIGHEST
EPS = 1e-05
NEG = -1e+30

@jax.custom_vjp
def low(v):
    return lax.optimization_barrier(v.astype(jnp.bfloat16)).astype(jnp.float32)

@jax.custom_vjp
def low_back(v):
    return v

def low_keep(v):
    return (low(v), None)

def low_pass(kept, grad):
    return (grad,)

def back_keep(v):
    return (v, None)

def back_low(kept, grad):
    return (low(grad),)
low.defvjp(low_keep, low_pass)
low_back.defvjp(back_keep, back_low)

def layer_norm(values, gain, offset):
    center = values - lax.optimization_barrier(jnp.mean(values, axis=-1, keepdims=True))
    spread = lax.optimization_barrier(jnp.mean(center * center, axis=-1, keepdims=True))
    return center * lax.rsqrt(spread + EPS) * gain + offset

def gelu_exact(values):
    return jax.nn.gelu(values, approximate=False)

def matmul(left, right):
    return jnp.dot(left, right, precision=HIGH)

def cell_forward(params, cell_rows, count):
    in_proj, out_proj, up_proj, down_proj, gains, biases = params
    length = cell_rows.shape[0]
    normed = low(layer_norm(cell_rows, gains[0], biases[0]))
    query_rows = low(low_back(matmul(normed, in_proj[0]))).reshape(length, HEADS, HEAD_DIM)
    key_rows = low(low_back(matmul(normed, in_proj[1]))).reshape(length, HEADS, HEAD_DIM)
    value_rows = low(low_back(matmul(normed, in_proj[2]))).reshape(length, HEADS, HEAD_DIM)
    scores = jnp.einsum('qhd,khd->hqk', query_rows, key_rows, precision=HIGH) * HEAD_DIM ** (-0.5)
    scores = low_back(scores)
    live = jnp.arange(length) < count
    scores = jnp.where(live[None, None, :], scores, NEG)
    top = lax.optimization_barrier(jnp.max(scores, axis=-1, keepdims=True))
    expo = jnp.exp(scores - top)
    attn_probs = expo / lax.optimization_barrier(jnp.sum(expo, axis=-1, keepdims=True))
    attended = jnp.einsum('hqk,khd->qhd', low(attn_probs), value_rows, precision=HIGH)
    attended = low(low_back(attended.reshape(length, HEADS * HEAD_DIM)))
    mid = cell_rows + low_back(matmul(attended, out_proj))
    normed_mid = low(layer_norm(mid, gains[1], biases[1]))
    hidden = low_back(matmul(normed_mid, up_proj))
    active = low(gelu_exact(hidden))
    return mid + low_back(matmul(active, down_proj))

def reference(tokens, gene_counts, in_proj, out_proj, up_proj, down_proj, gains, biases, cotangent):
    rows = tokens.astype(jnp.float32).reshape(CELLS, LEN, D)
    params = (in_proj.astype(jnp.float32), out_proj.astype(jnp.float32), up_proj.astype(jnp.float32), down_proj.astype(jnp.float32), gains.astype(jnp.float32), biases.astype(jnp.float32))
    cell_fn = jax.checkpoint(cell_forward)

    def forward(all_rows, weights):

        def per_cell(item):
            return cell_fn(weights, item[0], item[1])
        return lax.map(per_cell, (all_rows, gene_counts))
    result, pullback = jax.vjp(forward, rows, params)
    grad_rows, grad_params = pullback(cotangent.astype(jnp.float32).reshape(CELLS, LEN, D))
    return (result.reshape(TOKENS, D).astype(jnp.bfloat16), grad_rows.reshape(TOKENS, D).astype(jnp.bfloat16), grad_params[0], grad_params[1], grad_params[2], grad_params[3], grad_params[4], grad_params[5])
```

```python
import functools
import math

import jax
import jax.numpy as jnp
from jax import lax
from jax.experimental import pallas as pl
from jax.experimental.pallas import tpu as pltpu
from jax.sharding import PartitionSpec as P

HEAD_DIM = 64
EPS = 1e-05
NEG = -1e30
F32 = jnp.float32
BF16 = jnp.bfloat16
MESH = pl.DeviceIdType.MESH
LOG2E = math.log2(math.e)
LN2 = math.log(2.0)
ROWS = 512
WIDTH = 768
PART = 192
CHUNK = 96
SLAB = 256
ORDERS = (("c", "x", "y", "l", "h"), ("c", "y", "l", "x", "h"), ("c", "l", "x", "y", "h"))


def dot_nn(left, right):
    return lax.dot_general(left, right, (((1,), (0,)), ((), ())), preferred_element_type=F32)


def dot_nt(left, right):
    return lax.dot_general(left, right, (((1,), (1,)), ((), ())), preferred_element_type=F32)


def dot_tn(left, right):
    return lax.dot_general(left, right, (((0,), (0,)), ((), ())), preferred_element_type=F32)


def span(start, size):
    return pl.ds(pl.multiple_of(start, size), size)


def normalize(values):
    center = values - jnp.mean(values, axis=-1, keepdims=True)
    spread = jnp.mean(center * center, axis=-1, keepdims=True)
    rstd = lax.rsqrt(spread + EPS)
    return center * rstd, rstd


def pieces(values):
    high = values.astype(BF16)
    rest = values - high.astype(F32)
    middle = rest.astype(BF16)
    low = (rest - middle.astype(F32)).astype(BF16)
    return high, middle, low


class Mover:
    def __init__(self, where, send, recv):
        self.where, self.send, self.recv = where, send, recv
        self.count, self.started = 0, []

    def slot(self):
        self.count += 1
        return self.count - 1

    def remote(self, source, target, slot, to):
        copy = pltpu.make_async_remote_copy(
            src_ref=source,
            dst_ref=target,
            send_sem=self.send.at[slot],
            recv_sem=self.recv.at[slot],
            device_id=self.where[to],
            device_id_type=MESH,
        )
        copy.start()
        self.started.append(copy)
        return copy

    def local(self, source, target):
        copy = pltpu.make_async_copy(source, target, self.recv.at[self.slot()])
        copy.start()
        return copy

    def finish(self):
        for copy in self.started:
            copy.wait_send()
        self.started = []


class Gather:
    def __init__(self, mover, place, shard, full, view, halves):
        self.m, self.p, self.shard, self.full, self.view = mover, place, shard, full, view
        self.halves = halves
        self.slots = {k: mover.slot() for k in ("x0", "x1", "y", "z", "yf", "zf", "own", "c0", "c1", "c2", "c3")}
        self.copies = {}
        q, qy, qz = place["q"], place["qy"], place["qz"]
        self.quarter = {"q": q, "qy": qy, "qz": qz, "qd": place["qd"]}

    def go(self, key, source, target, to):
        self.copies[key] = self.m.remote(source, target, self.slots[key], to)

    def start_own(self):
        p = self.p
        mine = self.view(self.full, p["t"], 0, 4)
        self.load = self.m.local(self.view(self.shard, None, 0, 4), mine)
        self.go("own", self.view(self.shard, None, 0, 4), mine, "c")

    def start_x(self):
        p = self.p
        self.go("x0", self.view(self.shard, None, p["q"], 1), self.view(self.full, p["t"], p["q"], 1), "x")
        if not self.halves:
            self.go("x1", self.view(self.shard, None, p["qd"], 1), self.view(self.full, p["t"], p["qd"], 1), "x")

    def pass_on(self, key, quarter, to, half=None):
        part = self.view(self.full, self.p["t2"], self.quarter[quarter], 1, half)
        self.go(key, part, part, to)

    def step1(self):
        self.copies["x0"].wait_recv()
        self.pass_on("y", "q", "y")
        self.pass_on("z", "q", "l")
        self.pass_on("c0", "q", "c")

    def step2(self):
        self.copies["y"].wait_recv()
        if self.halves:
            self.pass_on("zf", "qy", "l", 0)
        self.pass_on("c1", "qy", "c")
        self.copies["z"].wait_recv()
        if self.halves:
            self.pass_on("yf", "qz", "y", 1)
        self.pass_on("c2", "qz", "c")

    def step3(self):
        if self.halves:
            self.copies["zf"].wait_recv()
            self.copies["yf"].wait_recv()
        else:
            self.copies["x1"].wait_recv()
        self.pass_on("c3", "qd", "c")

    def ready(self, i):
        if i == 0:
            self.load.wait()
        if i == 1:
            self.copies["own"].wait_recv()
        if i == 3:
            for key in ("c0", "c1", "c2", "c3"):
                self.copies[key].wait_recv()


class Reduce:
    def __init__(self, mover, place, grad, inbox, result):
        self.m, self.p, self.grad, self.inbox, self.result = mover, place, grad, inbox, result
        self.slots = [[mover.slot() for _ in range(3)] for _ in range(5)]
        self.copies = [[None] * 3 for _ in range(5)]

    def put(self, value, first, x, c):
        for k in range(value.shape[0] // CHUNK):
            r = first + k
            bits = {"x": x, "c": c, "y": r % 2, "l": (r // 2) % 2, "h": r // 4}
            for s in range(3):
                at = 0
                for name in ORDERS[s]:
                    at = at * 2 + bits[name]
                self.grad[s, span(at * CHUNK, CHUNK), :] = value[
                    k * CHUNK : (k + 1) * CHUNK, s * SLAB : (s + 1) * SLAB
                ].astype(BF16)

    def ranges(self, stage, s):
        base = 0
        size = 32
        for k in range(stage):
            size //= 2
            base = base + self.p[ORDERS[s][k]] * size
        size //= 2
        bit = self.p[ORDERS[s][stage]]
        return (base + bit * size) * CHUNK, (base + (1 - bit) * size) * CHUNK, size * CHUNK

    def inbox_at(self, stage, s, size):
        start = (0, 16, 24, 28, 30)[stage] * CHUNK
        return self.inbox.at[s, pl.ds(start, size), :]

    def send(self, stage):
        for s in range(3):
            _, away, size = self.ranges(stage, s)
            self.copies[stage][s] = self.m.remote(
                self.grad.at[s, span(away, size), :],
                self.inbox_at(stage, s, size),
                self.slots[stage][s],
                ORDERS[s][stage],
            )

    def add(self, stage):
        start = (0, 16, 24, 28, 30)[stage] * CHUNK
        for s in range(3):
            self.copies[stage][s].wait_recv()
            keep, _, size = self.ranges(stage, s)
            if stage == 4:
                self.result[:, s * SLAB : (s + 1) * SLAB] = self.grad[s, span(keep, CHUNK), :].astype(
                    F32
                ) + self.inbox[s, pl.ds(start, CHUNK), :].astype(F32)
            else:

                @pl.loop(0, size // CHUNK)
                def _(k):
                    at = span(keep + k * CHUNK, CHUNK)
                    total = self.grad[s, at, :].astype(F32) + self.inbox[
                        s, span(start + k * CHUNK, CHUNK), :
                    ].astype(F32)
                    self.grad[s, at, :] = total.astype(BF16)

    def step(self, stage):
        self.add(stage)
        if stage < 4:
            self.send(stage + 1)


def kernel(
    counts,
    tokens_in,
    cot_in,
    win_in,
    wout_in,
    wup_in,
    wdown_in,
    gains,
    biases,
    block_out,
    input_grad,
    grad_in,
    grad_out,
    grad_up,
    grad_down,
    grad_norm,
    tokens,
    normed,
    cot,
    win,
    wout,
    wup,
    wdown,
    qs,
    kvs,
    att,
    mid,
    mid_low,
    act,
    hid_grad,
    acc_a,
    acc_b,
    dqs,
    dks,
    dvs,
    g_down,
    g_up,
    in_down,
    in_up,
    in_io,
    res_io,
    norm_box,
    norm_sum,
    send,
    recv,
):
    d = lax.axis_index("dp")
    t = lax.axis_index("tensor")
    x = lax.div(t, 2)
    c = t - 2 * x
    y = lax.rem(d, 2)
    l = lax.rem(lax.div(d, 2), 2)
    h = lax.div(d, 4)
    where = {
        "c": (d, t + 1 - 2 * c),
        "x": (d, t + 2 - 4 * x),
        "y": (d + 1 - 2 * y, t),
        "l": (d + 2 - 4 * l, t),
        "h": (d + 4 - 8 * h, t),
    }
    place = {"x": x, "c": c, "y": y, "l": l, "h": h, "t": t, "t2": t + 2 - 4 * x}
    place["q"] = 2 * l + y
    place["qy"] = 2 * l + 1 - y
    place["qz"] = 2 * (1 - l) + y
    place["qd"] = 2 * (1 - l) + 1 - y
    barrier = pltpu.get_barrier_semaphore()
    for to in where:
        pl.semaphore_signal(barrier, inc=1, device_id=where[to], device_id_type=MESH)
    pl.semaphore_wait(barrier, len(where))

    m = Mover(where, send, recv)
    own_rows = span(c * ROWS, ROWS)
    other_rows = span((1 - c) * ROWS, ROWS)

    def view_in(ref, dev, first, parts, half=None):
        start, size = first * PART, parts * PART
        if half is not None:
            start, size = start + half * CHUNK, CHUNK
        rows = pl.ds(pl.multiple_of(start, CHUNK), size)
        return ref.at[:, rows, :] if dev is None else ref.at[dev, :, rows, :]

    def view_out(ref, dev, first, parts, half=None):
        start = first * 48
        rows = pl.ds(pl.multiple_of(start if dev is None else dev * PART + start, 48), parts * 48)
        return ref.at[rows, :]

    def view_up(ref, dev, first, parts, half=None):
        start, size = first * PART, parts * PART
        if half is not None:
            start, size = start + half * CHUNK, CHUNK
        rows = pl.ds(pl.multiple_of(start, CHUNK), size)
        return ref.at[rows, :] if dev is None else ref.at[dev, rows, :]

    def view_down(slab):
        def view(ref, dev, first, parts, half=None):
            start, size = first * PART, parts * PART
            if half is not None:
                start, size = start + half * CHUNK, CHUNK
            if dev is None:
                rows = pl.ds(pl.multiple_of(start, CHUNK), size)
                return ref.at[rows, pl.ds(slab * SLAB, SLAB)]
            rows = pl.ds(pl.multiple_of(dev * WIDTH + start, CHUNK), size)
            return ref.at[slab, rows, :]

        return view

    tok_load = m.local(tokens_in, tokens)
    tok_slot = m.slot()
    tok_copy = m.remote(tokens_in, mid_low, tok_slot, "c")
    gat_in = Gather(m, place, win_in, win, view_in, False)
    gat_out = Gather(m, place, wout_in, wout, view_out, False)
    gat_up = Gather(m, place, wup_in, wup, view_up, True)
    gat_down = [Gather(m, place, wdown_in, wdown, view_down(s), True) for s in range(3)]
    ff_weights = [gat_up, *gat_down]
    gat_in.start_x()
    gat_in.start_own()
    cot_load = m.local(cot_in, cot)
    for gat in (gat_out, *ff_weights):
        gat.start_own()

    gain0, bias0 = gains[0:1, :], biases[0:1, :]
    gain1, bias1 = gains[1:2, :], biases[1:2, :]

    def norm_rows(source, first):
        @pl.loop(0, ROWS // 64)
        def _(k):
            hat, _ = normalize(source[span(k * 64, 64), :].astype(F32))
            normed[span(first + k * 64, 64), :] = (hat * gain0 + bias0).astype(BF16)

    tok_load.wait()
    norm_rows(tokens, c * ROWS)
    tok_copy.wait_recv()
    norm_rows(mid_low, (1 - c) * ROWS)

    count = counts[x]
    key_at = lax.broadcasted_iota(jnp.int32, (2 * ROWS, 2 * HEAD_DIM), 0)
    key_lane = lax.broadcasted_iota(jnp.int32, (2 * ROWS, 2 * HEAD_DIM), 1)
    key_tail = jnp.where(
        key_lane == HEAD_DIM,
        jnp.where(key_at < count, 0.0, NEG),
        jnp.where(key_lane < HEAD_DIM + 4, 1.0, 0.0),
    ).astype(BF16)
    value_tail = jnp.where(key_lane < 3, 1.0, 0.0).astype(BF16)
    row_lane = lax.broadcasted_iota(jnp.int32, (SLAB, 2 * HEAD_DIM), 1)
    query_tail = jnp.where(
        lax.broadcasted_iota(jnp.int32, (ROWS, HEAD_DIM), 1) == 0, 1.0, 0.0
    ).astype(BF16)

    def keys_of(head):
        return jnp.where(key_lane < HEAD_DIM, kvs[head], key_tail)

    def values_of(head):
        return jnp.where(key_lane < HEAD_DIM, value_tail, kvs[head])

    def peer(i):
        xi = x if i < 2 else 1 - x
        ci = c if i % 2 == 0 else 1 - c
        return xi, ci, 2 * xi + ci

    def forward_heads(i):
        _, _, ti = peer(i)
        q = dot_nn(normed[own_rows, :], win[ti, 0]) * (HEAD_DIM ** (-0.5) * LOG2E)
        q = q.astype(BF16)
        k = dot_nn(normed[...], win[ti, 1]).astype(BF16)
        v = dot_nn(normed[...], win[ti, 2]).astype(BF16)
        for j in range(3):
            lanes = slice(j * HEAD_DIM, (j + 1) * HEAD_DIM)
            qs[3 * i + j] = jnp.concatenate([q[:, lanes], query_tail], axis=1)
            kvs[3 * i + j] = jnp.concatenate([k[:, lanes], v[:, lanes]], axis=1)
        for j in range(3):
            head = 3 * i + j
            keys, vals = keys_of(head), values_of(head)
            for b in range(ROWS // SLAB):
                rows = slice(b * SLAB, (b + 1) * SLAB)
                query = qs[head, rows, :]
                scores = dot_nt(query, keys)
                top = jnp.max(scores, axis=-1, keepdims=True)
                expo = jnp.exp2(scores - top).astype(BF16)
                mixed = dot_nn(expo, vals)
                total = mixed[:, 0:1]
                att[i, rows, j * HEAD_DIM : (j + 1) * HEAD_DIM] = (mixed * (1.0 / total))[
                    :, HEAD_DIM:
                ].astype(BF16)
                high, middle, low = pieces(-(top + jnp.log2(total)))
                qs[head, rows, :] = jnp.where(
                    row_lane == HEAD_DIM + 1,
                    high,
                    jnp.where(
                        row_lane == HEAD_DIM + 2,
                        middle,
                        jnp.where(row_lane == HEAD_DIM + 3, low, query),
                    ),
                )

    gat_in.ready(0)
    forward_heads(0)
    gat_in.step1()
    gat_out.start_x()
    gat_up.start_x()
    gat_in.ready(1)
    forward_heads(1)
    gat_in.step2()
    gat_in.step3()
    for gat in gat_down:
        gat.start_x()
    gat_out.step1()
    gat_up.step1()
    forward_heads(2)
    gat_out.step2()
    gat_out.step3()
    for gat in gat_down:
        gat.step1()
    gat_in.ready(3)
    forward_heads(3)
    gat_up.step2()
    for i in range(4):
        gat_out.ready(i)
    for b in range(2):
        at = slice(b * SLAB, (b + 1) * SLAB)
        total = tokens[at, :].astype(F32)
        for i in range(4):
            _, _, ti = peer(i)
            total = total + dot_nn(att[i, at, :], wout[span(ti * PART, PART), :])
        mid[at, :] = total
        hat, _ = normalize(total)
        mid_low[at, :] = (hat * gain1 + bias1).astype(BF16)
    cot_load.wait()

    red_down = Reduce(m, place, g_down, in_down, grad_down)
    red_up = Reduce(m, place, g_up, in_up, grad_up)
    red_io = Reduce(m, place, wdown, in_io, res_io)

    def feed_forward(i):
        xi, ci, ti = peer(i)
        for f in range(3):
            lanes = slice(f * SLAB, (f + 1) * SLAB)
            hidden = dot_nn(mid_low[...], wup[ti, :, lanes])
            back = jnp.zeros((ROWS, SLAB), F32)
            for s in range(3):
                back = back + dot_nt(
                    cot[:, s * SLAB : (s + 1) * SLAB], wdown[s, span(ti * WIDTH + f * SLAB, SLAB), :]
                )
            cdf = 0.5 + 0.5 * lax.erf(hidden * math.sqrt(0.5))
            pdf = jnp.exp2(hidden * hidden * (-0.5 * LOG2E)) * (1.0 / math.sqrt(2.0 * math.pi))
            act[:, lanes] = (hidden * cdf).astype(BF16)
            hid_grad[:, lanes] = (back * (cdf + hidden * pdf)).astype(BF16)
        for s in range(3):
            lanes = slice(s * SLAB, (s + 1) * SLAB)
            down = dot_nn(act[...], wdown[s, span(ti * WIDTH, WIDTH), :])
            up = dot_nt(hid_grad[...], wup[ti, lanes, :])
            if i == 0:
                acc_a[:, lanes] = mid[:, lanes] + down
                acc_b[:, lanes] = up
            else:
                acc_a[:, lanes] += down
                acc_b[:, lanes] += up
        for b in range(2):
            lanes = slice(b * 384, (b + 1) * 384)
            red_down.put(dot_tn(cot[:, lanes], act[...]), 4 * b, xi, ci)
            red_up.put(dot_tn(mid_low[:, lanes], hid_grad[...]), 4 * b, xi, ci)

    for gat in ff_weights:
        gat.ready(0)
    feed_forward(0)
    for gat in gat_down:
        gat.step2()
    gat_up.step3()
    for gat in ff_weights:
        gat.ready(1)
    feed_forward(1)
    for gat in gat_down:
        gat.step3()
    feed_forward(2)
    for gat in ff_weights:
        gat.ready(3)
    feed_forward(3)
    m.finish()
    red_down.send(0)
    red_up.send(0)
    block_out[...] = acc_a[...].astype(BF16)

    def norm_back(grad, hat, rstd, gain):
        e = grad * gain
        mean_e = jnp.mean(e, axis=-1, keepdims=True)
        mean_eh = jnp.mean(e * hat, axis=-1, keepdims=True)
        return rstd * (e - mean_e - hat * mean_eh)

    def column_sum(values):
        return jnp.sum(values, axis=0, keepdims=True)

    gain_sum = jnp.zeros((1, WIDTH), F32)
    bias_sum = jnp.zeros((1, WIDTH), F32)
    for b in range(4):
        at = slice(b * 128, (b + 1) * 128)
        grad = acc_b[at, :]
        hat, rstd = normalize(mid[at, :])
        total = cot[at, :].astype(F32) + norm_back(grad, hat, rstd, gain1)
        gain_sum = gain_sum + column_sum(grad * hat)
        bias_sum = bias_sum + column_sum(grad)
        mid[at, :] = total
        mid_low[at, :] = total.astype(BF16)
    norm_sum[1:2, :] = gain_sum
    norm_sum[3:4, :] = bias_sum

    def attention_back(i):
        _, _, ti = peer(i)
        hid_grad[:, :PART] = dot_nt(mid_low[...], wout[span(ti * PART, PART), :]).astype(BF16)
        for j in range(3):
            head = 3 * i + j
            lanes = slice(j * HEAD_DIM, (j + 1) * HEAD_DIM)
            keys, vals = keys_of(head), values_of(head)
            key_sum = value_sum = None
            for b in range(ROWS // SLAB):
                rows = slice(b * SLAB, (b + 1) * SLAB)
                grad = hid_grad[rows, lanes]
                inner = jnp.sum(
                    grad.astype(F32) * att[i, rows, lanes].astype(F32), axis=-1, keepdims=True
                )
                high, middle, low = pieces(-inner)
                both = jnp.concatenate([grad, grad], axis=1)
                zero = jnp.zeros_like(both)
                both = jnp.where(
                    row_lane >= HEAD_DIM,
                    both,
                    jnp.where(
                        row_lane == 0,
                        high,
                        jnp.where(row_lane == 1, middle, jnp.where(row_lane == 2, low, zero)),
                    ),
                )
                query = qs[head, rows, :]
                probs = jnp.exp2(dot_nt(query, keys))
                score_grads = (probs * dot_nt(both, vals)).astype(BF16)
                probs = probs.astype(BF16)
                dqs[i, rows, lanes] = (dot_nn(score_grads, keys)[:, :HEAD_DIM] * HEAD_DIM ** (-0.5)).astype(BF16)
                key_part = dot_tn(score_grads, query)
                value_part = dot_tn(probs, both)
                key_sum = key_part if b == 0 else key_sum + key_part
                value_sum = value_part if b == 0 else value_sum + value_part
            dks[i, :, lanes] = (key_sum[:, :HEAD_DIM] * LN2).astype(BF16)
            dvs[i, :, lanes] = value_sum[:, HEAD_DIM:].astype(BF16)

    def projection_grads(i):
        xi, ci, _ = peer(i)
        for b in range(2):
            lanes = slice(b * 384, (b + 1) * 384)
            everyone, own = normed[:, lanes], normed[own_rows, lanes]
            red_io.put(
                jnp.concatenate(
                    [
                        dot_tn(own, dqs[i]),
                        dot_tn(everyone, dks[i]),
                        dot_tn(everyone, dvs[i]),
                        dot_tn(mid_low[:, lanes], att[i]),
                    ],
                    axis=1,
                ),
                4 * b,
                xi,
                ci,
            )

    red_down.step(0)
    attention_back(0)
    projection_grads(0)
    red_up.step(0)
    red_down.step(1)
    attention_back(1)
    projection_grads(1)
    red_up.step(1)
    red_down.step(2)
    attention_back(2)
    projection_grads(2)
    red_up.step(2)
    red_down.step(3)
    attention_back(3)
    projection_grads(3)
    red_io.send(0)
    red_up.step(3)
    red_down.step(4)

    for n in range(3):
        lanes = slice(n * SLAB, (n + 1) * SLAB)
        total = None
        for i in range(4):
            _, _, ti = peer(i)
            part = dot_nt(dks[i, other_rows, :], win[ti, 1, lanes, :]) + dot_nt(
                dvs[i, other_rows, :], win[ti, 2, lanes, :]
            )
            total = part if i == 0 else total + part
        mid_low[:, lanes] = total.astype(BF16)
    dn_copy = m.remote(mid_low, act, m.slot(), "c")
    red_io.step(0)
    for n in range(3):
        lanes = slice(n * SLAB, (n + 1) * SLAB)
        total = None
        for i in range(4):
            _, _, ti = peer(i)
            part = (
                dot_nt(dqs[i], win[ti, 0, lanes, :])
                + dot_nt(dks[i, own_rows, :], win[ti, 1, lanes, :])
                + dot_nt(dvs[i, own_rows, :], win[ti, 2, lanes, :])
            )
            total = part if i == 0 else total + part
        acc_b[:, lanes] = total
    red_up.step(4)
    red_io.step(1)
    dn_copy.wait_recv()
    gain_sum = jnp.zeros((1, WIDTH), F32)
    bias_sum = jnp.zeros((1, WIDTH), F32)
    for b in range(4):
        at = slice(b * 128, (b + 1) * 128)
        grad = acc_b[at, :] + act[at, :].astype(F32)
        hat, rstd = normalize(tokens[at, :].astype(F32))
        hid_grad[at, :] = (mid[at, :] + norm_back(grad, hat, rstd, gain0)).astype(BF16)
        gain_sum = gain_sum + column_sum(grad * hat)
        bias_sum = bias_sum + column_sum(grad)
    store = m.local(hid_grad, input_grad)
    norm_sum[0:1, :] = gain_sum
    norm_sum[2:3, :] = bias_sum

    def share(stage):
        grad_norm[...] = norm_sum[0:4, :]
        norm_box[2 * stage, 0:4, :] = grad_norm[...]
        return m.remote(norm_box.at[2 * stage], norm_box.at[2 * stage + 1], m.slot(), "cxylh"[stage])

    copy = share(0)
    red_io.step(2)
    for stage in range(5):
        copy.wait_recv()
        norm_sum[0:4, :] = norm_box[2 * stage, 0:4, :] + norm_box[2 * stage + 1, 0:4, :]
        if stage < 4:
            copy = share(stage + 1)
        if stage == 1:
            red_io.step(3)
        if stage == 3:
            red_io.step(4)
    grad_norm[...] = norm_sum[0:4, :]
    for k in range(3):
        grad_in[k] = res_io[:, k * PART : (k + 1) * PART]
    grad_out[...] = res_io[:, 3 * PART :]
    store.wait()
    m.finish()


def fused(tokens, gene_counts, in_proj, out_proj, up_proj, down_proj, gains, biases, cotangent):
    vmem = pl.BlockSpec(memory_space=pltpu.VMEM)
    hbm = pl.BlockSpec(memory_space=pl.ANY)
    shape = jax.ShapeDtypeStruct
    outs = pl.pallas_call(
        kernel,
        out_shape=(
            shape((ROWS, WIDTH), BF16),
            shape((ROWS, WIDTH), BF16),
            shape((3, CHUNK, PART), F32),
            shape((CHUNK, PART), F32),
            shape((CHUNK, WIDTH), F32),
            shape((CHUNK, WIDTH), F32),
            shape((4, WIDTH), F32),
        ),
        in_specs=[pl.BlockSpec(memory_space=pltpu.SMEM)] + [hbm] * 6 + [vmem] * 2,
        out_specs=[vmem, hbm] + [vmem] * 5,
        scratch_shapes=[
            pltpu.VMEM((ROWS, WIDTH), BF16),
            pltpu.VMEM((2 * ROWS, WIDTH), BF16),
            pltpu.VMEM((ROWS, WIDTH), BF16),
            pltpu.VMEM((4, 3, WIDTH, PART), BF16),
            pltpu.VMEM((WIDTH, WIDTH), BF16),
            pltpu.VMEM((4, WIDTH, WIDTH), BF16),
            pltpu.VMEM((3, 4 * WIDTH, SLAB), BF16),
            pltpu.VMEM((12, ROWS, 2 * HEAD_DIM), BF16),
            pltpu.VMEM((12, 2 * ROWS, 2 * HEAD_DIM), BF16),
            pltpu.VMEM((4, ROWS, PART), BF16),
            pltpu.VMEM((ROWS, WIDTH), F32),
            pltpu.VMEM((ROWS, WIDTH), BF16),
            pltpu.VMEM((ROWS, WIDTH), BF16),
            pltpu.VMEM((ROWS, WIDTH), BF16),
            pltpu.VMEM((ROWS, WIDTH), F32),
            pltpu.VMEM((ROWS, WIDTH), F32),
            pltpu.VMEM((4, ROWS, PART), BF16),
            pltpu.VMEM((4, 2 * ROWS, PART), BF16),
            pltpu.VMEM((4, 2 * ROWS, PART), BF16),
            pltpu.VMEM((3, 4 * WIDTH, SLAB), BF16),
            pltpu.VMEM((3, 4 * WIDTH, SLAB), BF16),
            pltpu.VMEM((3, 31 * CHUNK, SLAB), BF16),
            pltpu.VMEM((3, 31 * CHUNK, SLAB), BF16),
            pltpu.VMEM((3, 31 * CHUNK, SLAB), BF16),
            pltpu.VMEM((CHUNK, WIDTH), F32),
            pltpu.VMEM((10, 8, WIDTH), F32),
            pltpu.VMEM((8, WIDTH), F32),
            pltpu.SemaphoreType.DMA((140,)),
            pltpu.SemaphoreType.DMA((140,)),
        ],
        compiler_params=pltpu.CompilerParams(
            collective_id=0, has_side_effects=True, vmem_limit_bytes=64 * 2**20
        ),
    )(
        gene_counts,
        tokens,
        cotangent,
        in_proj,
        out_proj,
        up_proj,
        down_proj,
        gains,
        biases,
    )
    block_out, input_grad, grad_in, grad_out, grad_up, grad_down, norms = outs
    return (
        block_out,
        input_grad,
        grad_in,
        grad_out.T,
        grad_up,
        grad_down.T,
        norms[0:2],
        norms[2:4],
    )


def layer_norm(values, gain, offset):
    center = values - jnp.mean(values, axis=-1, keepdims=True)
    spread = jnp.mean(center * center, axis=-1, keepdims=True)
    return center * lax.rsqrt(spread + EPS) * gain + offset


def gelu_exact(values):
    return jax.nn.gelu(values, approximate=False)


def per_device(
    tokens, gene_counts, in_proj, out_proj, up_proj, down_proj, gains, biases, cotangent
):
    rows = tokens.shape[0]
    cells = gene_counts.shape[0]
    group = rows * lax.axis_size("tensor")
    length = group // cells
    local_width = out_proj.shape[0]
    heads = local_width // HEAD_DIM
    block = min(length, 512)
    blocks = length // block
    scale = HEAD_DIM ** (-0.5)
    positions = jnp.arange(length, dtype=jnp.int32)
    resid = tokens.astype(jnp.float32)
    normed, first_back = jax.vjp(layer_norm, resid, gains[0], biases[0])
    normed_all = lax.all_gather(normed.astype(jnp.bfloat16), "tensor", axis=0, tiled=True)
    projected = jnp.einsum(
        "td,cde->cte", normed_all, in_proj, preferred_element_type=jnp.float32
    ).astype(jnp.bfloat16)
    query_cells = projected[0].reshape(cells, blocks, block, local_width)
    key_cells = projected[1].reshape(cells, length, local_width)
    value_cells = projected[2].reshape(cells, length, local_width)

    def block_scores(query_block, key_rows, count):
        query_heads = query_block.reshape(block, heads, HEAD_DIM)
        key_heads = key_rows.reshape(length, heads, HEAD_DIM)
        scores = (
            jnp.einsum("qhd,khd->hqk", query_heads, key_heads, preferred_element_type=jnp.float32)
            * scale
        )
        return jnp.where((positions < count)[None, None, :], scores, NEG)

    def cell_forward(item):
        queries, key_rows, value_rows, count = item
        value_heads = value_rows.reshape(length, heads, HEAD_DIM)

        def one_block(query_block):
            scores = block_scores(query_block, key_rows, count)
            top = jnp.max(scores, axis=-1, keepdims=True)
            expo = jnp.exp(scores - top)
            total = jnp.sum(expo, axis=-1, keepdims=True)
            probs = (expo / total).astype(jnp.bfloat16)
            result = jnp.einsum(
                "hqk,khd->qhd", probs, value_heads, preferred_element_type=jnp.float32
            )
            return (
                result.reshape(block, local_width).astype(jnp.bfloat16),
                (top + jnp.log(total))[..., 0],
            )

        return lax.map(one_block, queries)

    attended, log_totals = lax.map(cell_forward, (query_cells, key_cells, value_cells, gene_counts))
    attended = attended.reshape(group, local_width)
    piece = attended
    mid = resid + lax.psum_scatter(
        jnp.dot(piece, out_proj, preferred_element_type=jnp.float32),
        "tensor",
        scatter_dimension=0,
        tiled=True,
    )
    normed_mid, second_back = jax.vjp(layer_norm, mid, gains[1], biases[1])
    mid_low = normed_mid.astype(jnp.bfloat16)
    mid_all = lax.all_gather(mid_low, "tensor", axis=0, tiled=True)
    hidden = jnp.dot(mid_all, up_proj, preferred_element_type=jnp.float32)
    active = gelu_exact(hidden).astype(jnp.bfloat16)
    piece = active
    block_out = (
        mid
        + lax.psum_scatter(
            jnp.dot(piece, down_proj, preferred_element_type=jnp.float32).astype(jnp.bfloat16),
            "tensor",
            scatter_dimension=0,
            tiled=True,
        ).astype(jnp.float32)
    ).astype(jnp.bfloat16)
    out_grads = lax.all_gather(cotangent, "tensor", axis=0, tiled=True)
    _, gelu_back = jax.vjp(gelu_exact, hidden)
    active_grad = jnp.einsum("td,fd->tf", out_grads, down_proj, preferred_element_type=jnp.float32)
    hidden_grad = gelu_back(active_grad)[0].astype(jnp.bfloat16)
    grad_down = jnp.einsum("tf,td->fd", active, out_grads, preferred_element_type=jnp.float32)
    grad_up = jnp.einsum("td,tf->df", mid_all, hidden_grad, preferred_element_type=jnp.float32)
    piece = hidden_grad
    mid_grad = lax.psum_scatter(
        jnp.einsum("tf,df->td", piece, up_proj, preferred_element_type=jnp.float32),
        "tensor",
        scatter_dimension=0,
        tiled=True,
    )
    resid_part, gain_second, bias_second = second_back(mid_grad)
    mid_total = cotangent.astype(jnp.float32) + resid_part
    branch_all = lax.all_gather(mid_total.astype(jnp.bfloat16), "tensor", axis=0, tiled=True)
    attended_grad = jnp.einsum(
        "td,ed->te", branch_all, out_proj, preferred_element_type=jnp.float32
    ).astype(jnp.bfloat16)
    grad_out = jnp.einsum("te,td->ed", attended, branch_all, preferred_element_type=jnp.float32)

    def cell_backward(item):
        queries, key_rows, value_rows, count, grad_rows, totals = item
        key_heads = key_rows.reshape(length, heads, HEAD_DIM)
        value_heads = value_rows.reshape(length, heads, HEAD_DIM)

        def one_block(carry, part):
            key_sum, value_sum = carry
            query_block, grad_block, total_block = part
            scores = block_scores(query_block, key_rows, count)
            probs = jnp.exp(scores - total_block[..., None])
            grad_heads = grad_block.reshape(block, heads, HEAD_DIM)
            query_heads = query_block.reshape(block, heads, HEAD_DIM)
            prob_grads = jnp.einsum(
                "qhd,khd->hqk", grad_heads, value_heads, preferred_element_type=jnp.float32
            )
            inner = jnp.sum(probs * prob_grads, axis=-1, keepdims=True)
            score_grads = (probs * (prob_grads - inner)).astype(jnp.bfloat16)
            query_grad = (
                jnp.einsum(
                    "hqk,khd->qhd", score_grads, key_heads, preferred_element_type=jnp.float32
                )
                * scale
            )
            key_sum = (
                key_sum
                + jnp.einsum(
                    "hqk,qhd->khd", score_grads, query_heads, preferred_element_type=jnp.float32
                )
                * scale
            )
            value_sum = value_sum + jnp.einsum(
                "hqk,qhd->khd",
                probs.astype(jnp.bfloat16),
                grad_heads,
                preferred_element_type=jnp.float32,
            )
            return (
                (key_sum, value_sum),
                query_grad.reshape(block, local_width).astype(jnp.bfloat16),
            )

        zeros = jnp.zeros((length, heads, HEAD_DIM), jnp.float32)
        (key_sum, value_sum), query_grads = lax.scan(
            one_block, (zeros, zeros), (queries, grad_rows, totals)
        )
        return (
            query_grads.reshape(length, local_width),
            key_sum.reshape(length, local_width).astype(jnp.bfloat16),
            value_sum.reshape(length, local_width).astype(jnp.bfloat16),
        )

    grad_cells = attended_grad.reshape(cells, blocks, block, local_width)
    query_grads, key_grads, value_grads = lax.map(
        cell_backward, (query_cells, key_cells, value_cells, gene_counts, grad_cells, log_totals)
    )
    proj_grads = jnp.stack(
        [
            query_grads.reshape(group, local_width),
            key_grads.reshape(group, local_width),
            value_grads.reshape(group, local_width),
        ]
    )
    grad_in = jnp.einsum("td,cte->cde", normed_all, proj_grads, preferred_element_type=jnp.float32)
    piece = proj_grads
    normed_grad = lax.psum_scatter(
        jnp.einsum("cte,cde->td", piece, in_proj, preferred_element_type=jnp.float32),
        "tensor",
        scatter_dimension=0,
        tiled=True,
    )
    resid_grad, gain_first, bias_first = first_back(normed_grad)
    input_grad = (mid_total + resid_grad).astype(jnp.bfloat16)
    grad_gains, grad_biases = lax.psum(
        (jnp.stack([gain_first, gain_second]), jnp.stack([bias_first, bias_second])),
        ("dp", "tensor"),
    )
    grad_in_part, grad_out_part, grad_up_part, grad_down_part = (
        lax.psum_scatter(grad_in, "dp", scatter_dimension=1, tiled=True),
        lax.psum_scatter(grad_out, "dp", scatter_dimension=1, tiled=True),
        lax.psum_scatter(grad_up, "dp", scatter_dimension=0, tiled=True),
        lax.psum_scatter(grad_down, "dp", scatter_dimension=1, tiled=True),
    )
    return (
        block_out,
        input_grad,
        grad_in_part,
        grad_out_part,
        grad_up_part,
        grad_down_part,
        grad_gains,
        grad_biases,
    )


def solution(mesh):
    placed = (
        P(("dp", "tensor"), None),
        P("dp"),
        P(None, None, "tensor"),
        P("tensor", None),
        P(None, "tensor"),
        P("tensor", None),
        P(),
        P(),
        P(("dp", "tensor"), None),
    )
    halves = mesh.shape["dp"] == 8 and mesh.shape["tensor"] == 4
    return jax.shard_map(
        fused if halves else per_device,
        mesh=mesh,
        in_specs=placed,
        out_specs=(
            P(("dp", "tensor"), None),
            P(("dp", "tensor"), None),
            P(None, "dp", "tensor"),
            P("tensor", "dp"),
            P("dp", "tensor"),
            P("tensor", "dp"),
            P(),
            P(),
        ),
        check_vma=False,
    )
```

```python
import itertools
import math

import jax
import jax.numpy as jnp
from jax import lax
from jax.experimental import pallas as pl
from jax.experimental.pallas import tpu as pltpu
from jax.sharding import PartitionSpec as P

HEAD_DIM = 64
EPS = 1e-05
NEG = -1e30
F32 = jnp.float32
BF16 = jnp.bfloat16
MESH = pl.DeviceIdType.MESH
LOG2E = math.log2(math.e)
LN2 = math.log(2.0)
ROWS = 512
WIDTH = 768
PART = 192
CHUNK = 96
SLAB = 256
THIRD = 32
ORDERS = ("xylh", "ylxh", "lxyh")
WEIGHT = {"x": 8, "y": 4, "l": 2, "h": 1}
BOX = (0, 16, 24, 28, 30)


def dot_nn(left, right):
    return lax.dot_general(left, right, (((1,), (0,)), ((), ())), preferred_element_type=F32)


def dot_nt(left, right):
    return lax.dot_general(left, right, (((1,), (1,)), ((), ())), preferred_element_type=F32)


def dot_tn(left, right):
    return lax.dot_general(left, right, (((0,), (0,)), ((), ())), preferred_element_type=F32)


def span(start, size):
    return pl.ds(pl.multiple_of(start, size), size)


def normalize(values):
    center = values - jnp.mean(values, axis=-1, keepdims=True)
    spread = jnp.mean(center * center, axis=-1, keepdims=True)
    rstd = lax.rsqrt(spread + EPS)
    return center * rstd, rstd


def pieces(values):
    high = values.astype(BF16)
    rest = values - high.astype(F32)
    middle = rest.astype(BF16)
    low = (rest - middle.astype(F32)).astype(BF16)
    return high, middle, low


class Mover:
    def __init__(self, where, send, recv):
        self.where, self.send, self.recv = where, send, recv
        self.count, self.started = 0, []

    def slot(self):
        self.count += 1
        return self.count - 1

    def remote(self, source, target, slot, to):
        copy = pltpu.make_async_remote_copy(
            src_ref=source,
            dst_ref=target,
            send_sem=self.send.at[slot],
            recv_sem=self.recv.at[slot],
            device_id=self.where[to],
            device_id_type=MESH,
        )
        copy.start()
        self.started.append(copy)
        return copy

    def local(self, source, target):
        copy = pltpu.make_async_copy(source, target, self.recv.at[self.slot()])
        copy.start()
        return copy

    def finish(self):
        for copy in self.started:
            copy.wait_send()
        self.started = []


class Gather:
    def __init__(self, mover, place, shard, full, view, halves):
        self.m, self.p, self.shard, self.full, self.view = mover, place, shard, full, view
        self.halves = halves
        self.slots = {k: mover.slot() for k in ("x0", "x1", "y", "z", "yf", "zf", "own", "c0", "c1", "c2", "c3")}
        self.copies = {}
        q, qy, qz = place["q"], place["qy"], place["qz"]
        self.quarter = {"q": q, "qy": qy, "qz": qz, "qd": place["qd"]}

    def go(self, key, source, target, to):
        self.copies[key] = self.m.remote(source, target, self.slots[key], to)

    def start_own(self):
        p = self.p
        mine = self.view(self.full, p["t"], 0, 4)
        self.load = self.m.local(self.view(self.shard, None, 0, 4), mine)
        self.go("own", self.view(self.shard, None, 0, 4), mine, "c")

    def start_x(self):
        p = self.p
        self.go("x0", self.view(self.shard, None, p["q"], 1), self.view(self.full, p["t"], p["q"], 1), "x")
        if not self.halves:
            self.go("x1", self.view(self.shard, None, p["qd"], 1), self.view(self.full, p["t"], p["qd"], 1), "x")

    def pass_on(self, key, quarter, to, half=None):
        part = self.view(self.full, self.p["t2"], self.quarter[quarter], 1, half)
        self.go(key, part, part, to)

    def step1(self):
        self.copies["x0"].wait_recv()
        self.pass_on("y", "q", "y")
        self.pass_on("z", "q", "l")
        self.pass_on("c0", "q", "c")

    def step2(self):
        self.copies["y"].wait_recv()
        if self.halves:
            self.pass_on("zf", "qy", "l", 0)
        self.pass_on("c1", "qy", "c")
        self.copies["z"].wait_recv()
        if self.halves:
            self.pass_on("yf", "qz", "y", 1)
        self.pass_on("c2", "qz", "c")

    def step3(self):
        if self.halves:
            self.copies["zf"].wait_recv()
            self.copies["yf"].wait_recv()
        else:
            self.copies["x1"].wait_recv()
        self.pass_on("c3", "qd", "c")

    def finish(self):
        done = list(self.copies.values())
        for copy in done:
            copy.wait_send()
        self.m.started = [copy for copy in self.m.started if all(copy is not other for other in done)]

    def ready(self, i):
        if i == 0:
            self.load.wait()
        if i == 1:
            self.copies["own"].wait_recv()
        if i == 3:
            for key in ("c0", "c1", "c2", "c3"):
                self.copies[key].wait_recv()


class Reduce:
    def __init__(self, mover, place, grad, inbox, result):
        self.m, self.p, self.grad, self.inbox, self.result = mover, place, grad, inbox, result
        self.copies = {}

    def rows(self, third, chunk, count):
        return pl.ds(pl.multiple_of((third * 32 + chunk) * THIRD, THIRD), count * THIRD)

    def box(self, third, at, count):
        return pl.ds((third * 31 + at) * THIRD, count * THIRD)

    def put(self, value, first, x, c):
        for k in range(value.shape[0] // CHUNK):
            r = first + k
            chunk = 16 * c + 8 * x + 4 * (r % 2) + 2 * ((r // 2) % 2) + r // 4
            for third in range(3):
                start = k * CHUNK + third * THIRD
                self.grad[self.rows(third, chunk, 1), :] = value[start : start + THIRD, :].astype(BF16)

    def go(self, key, third, chunk, count, at, to):
        self.copies[key] = self.m.remote(
            self.grad.at[self.rows(third, chunk, count), :],
            self.inbox.at[self.box(third, at, count), :],
            self.m.slot(),
            to,
        )

    def halves(self, side):
        return (self.p["x"], 0) if side == "near" else (1 - self.p["x"], 8)

    def send_core(self, side):
        x, at = self.halves(side)
        for third in range(3):
            self.go((third, 0, side), third, 16 * (1 - self.p["c"]) + 8 * x, 8, at, "c")

    def add(self, key, third, chunk, count, at):
        self.copies[key].wait_recv()
        here, there = self.rows(third, chunk, count), self.box(third, at, count)
        self.grad[here, :] = self.grad[here, :] + self.inbox[there, :]

    def add_core(self, side):
        x, at = self.halves(side)
        for third in range(3):
            self.add((third, 0, side), third, 16 * self.p["c"] + 8 * x, 8, at)
            self.send(third, 1, side)

    def runs(self, third, stage):
        order = ORDERS[third]
        dim, fixed = order[stage - 1], order[: stage - 1]
        rest, count = list("xylh"), 1
        while rest and rest[-1] != dim and rest[-1] not in fixed:
            rest.pop()
            count *= 2
        free = [name for name in rest if name != dim and name not in fixed]
        found = []
        for values in itertools.product((0, 1), repeat=len(free)):
            flip = dict(zip(free, values))
            base = 16 * self.p["c"]
            for name in rest:
                if name != dim:
                    own = self.p[name]
                    base = base + WEIGHT[name] * (1 - own if flip.get(name) else own)
            own = WEIGHT[dim] * self.p[dim]
            side = "far" if flip.get("x", dim == "x") else "near"
            found.append((base + own, base + WEIGHT[dim] - own, count, BOX[stage] + len(found) * count, side))
        return found

    def send(self, third, stage, side=None):
        for n, (_, away, count, at, where) in enumerate(self.runs(third, stage)):
            if side in (None, where):
                self.go((third, stage, n), third, away, count, at, ORDERS[third][stage - 1])

    def step(self, third, stage):
        for n, (keep, _, count, at, _) in enumerate(self.runs(third, stage)):
            if stage < 4:
                self.add((third, stage, n), third, keep, count, at)
            else:
                self.copies[third, stage, n].wait_recv()
                total = self.grad[self.rows(third, keep, 1), :].astype(F32) + self.inbox[
                    self.box(third, at, 1), :
                ].astype(F32)
                self.result[third * THIRD : (third + 1) * THIRD, :] = total
        if stage < 4:
            self.send(third, stage + 1)


def kernel(
    counts,
    tokens_in,
    cot_in,
    win_in,
    wout_in,
    wup_in,
    wdown_in,
    gains,
    biases,
    block_out,
    input_grad,
    grad_in,
    grad_up,
    grad_down,
    grad_out,
    grad_norm,
    tokens,
    normed,
    cot,
    win,
    wout,
    wup,
    wdown,
    qs,
    kvs,
    att,
    mid,
    mid_low,
    act,
    hid_grad,
    stage,
    acc_b,
    dqs,
    dks,
    dvs,
    g_down,
    g_up,
    in_down,
    in_up,
    res_io,
    norm_box,
    norm_sum,
    send,
    recv,
):
    d = lax.axis_index("dp")
    t = lax.axis_index("tensor")
    x = lax.div(t, 2)
    c = t - 2 * x
    y = lax.rem(d, 2)
    l = lax.rem(lax.div(d, 2), 2)
    h = lax.div(d, 4)
    where = {
        "c": (d, t + 1 - 2 * c),
        "x": (d, t + 2 - 4 * x),
        "y": (d + 1 - 2 * y, t),
        "l": (d + 2 - 4 * l, t),
        "h": (d + 4 - 8 * h, t),
    }
    place = {"x": x, "c": c, "y": y, "l": l, "h": h, "t": t, "t2": t + 2 - 4 * x}
    place["q"] = 2 * l + y
    place["qy"] = 2 * l + 1 - y
    place["qz"] = 2 * (1 - l) + y
    place["qd"] = 2 * (1 - l) + 1 - y
    m = Mover(where, send, recv)
    own_rows = span(c * ROWS, ROWS)
    other_rows = span((1 - c) * ROWS, ROWS)

    def view_in(ref, dev, first, parts, half=None):
        start = first * 48
        rows = pl.ds(pl.multiple_of(start if dev is None else dev * PART + start, 48), parts * 48)
        return ref.at[:, rows, :]

    def view_out(ref, dev, first, parts, half=None):
        start = first * 48
        rows = pl.ds(pl.multiple_of(start if dev is None else dev * PART + start, 48), parts * 48)
        return ref.at[rows, :]

    def view_up(ref, dev, first, parts, half=None):
        start, size = first * PART, parts * PART
        if half is not None:
            start, size = start + half * CHUNK, CHUNK
        start = start if dev is None else dev * WIDTH + start
        return ref.at[pl.ds(pl.multiple_of(start, CHUNK), size), :]

    def view_down(slab):
        def view(ref, dev, first, parts, half=None):
            start, size = first * PART, parts * PART
            if half is not None:
                start, size = start + half * CHUNK, CHUNK
            if dev is None:
                rows = pl.ds(pl.multiple_of(start, CHUNK), size)
                return ref.at[rows, pl.ds(slab * SLAB, SLAB)]
            rows = pl.ds(pl.multiple_of(dev * WIDTH + start, CHUNK), size)
            return ref.at[slab, rows, :]

        return view

    barrier = pltpu.get_barrier_semaphore()
    for to in where:
        pl.semaphore_signal(barrier, inc=1, device_id=where[to], device_id_type=MESH)
    tok_load = m.local(tokens_in, tokens)
    pl.semaphore_wait(barrier, len(where))
    gat_in = Gather(m, place, win_in, win, view_in, False)
    gat_out = Gather(m, place, wout_in, wout, view_out, False)
    gat_up = Gather(m, place, wup_in, wup, view_up, True)
    gat_down = [Gather(m, place, wdown_in, wdown, view_down(s), False) for s in range(3)]
    ff_weights = [gat_up, *gat_down]
    gat_in.start_x()
    tok_copy = m.remote(tokens_in, mid_low, m.slot(), "c")
    gat_in.start_own()
    gat_out.start_x()
    for gat in ff_weights:
        gat.start_x()
    cot_load = m.local(cot_in, cot)
    for gat in (gat_out, *ff_weights):
        gat.start_own()

    gain0, bias0 = gains[0:1, :], biases[0:1, :]
    gain1, bias1 = gains[1:2, :], biases[1:2, :]

    def norm_rows(source, first):
        @pl.loop(0, ROWS // 64)
        def _(k):
            hat, _ = normalize(source[span(k * 64, 64), :].astype(F32))
            normed[span(first + k * 64, 64), :] = (hat * gain0 + bias0).astype(BF16)

    tok_load.wait()
    norm_rows(tokens, c * ROWS)
    tok_copy.wait_recv()
    norm_rows(mid_low, (1 - c) * ROWS)

    count = counts[x]
    key_at = lax.broadcasted_iota(jnp.int32, (2 * ROWS, 2 * HEAD_DIM), 0)
    key_lane = lax.broadcasted_iota(jnp.int32, (2 * ROWS, 2 * HEAD_DIM), 1)
    key_tail = jnp.where(
        key_lane == HEAD_DIM,
        jnp.where(key_at < count, 0.0, NEG),
        jnp.where(key_lane < HEAD_DIM + 4, 1.0, 0.0),
    ).astype(BF16)
    value_tail = jnp.where(key_lane < 3, 1.0, 0.0).astype(BF16)
    row_lane = lax.broadcasted_iota(jnp.int32, (SLAB, 2 * HEAD_DIM), 1)
    query_tail = jnp.where(
        lax.broadcasted_iota(jnp.int32, (ROWS, HEAD_DIM), 1) == 0, 1.0, 0.0
    ).astype(BF16)

    def keys_of(head):
        return jnp.where(key_lane < HEAD_DIM, kvs[head], key_tail)

    def values_of(head):
        return jnp.where(key_lane < HEAD_DIM, value_tail, kvs[head])

    def peer(i):
        xi = x if i < 2 else 1 - x
        ci = c if i % 2 == 0 else 1 - c
        return xi, ci, 2 * xi + ci

    def project(i):
        _, _, ti = peer(i)
        part = span(ti * PART, PART)
        q = dot_nt(normed[own_rows, :], win[0, part, :]) * (HEAD_DIM ** (-0.5) * LOG2E)
        q = q.astype(BF16)
        k = dot_nt(normed[...], win[1, part, :]).astype(BF16)
        v = dot_nt(normed[...], win[2, part, :]).astype(BF16)
        for j in range(3):
            lanes = slice(j * HEAD_DIM, (j + 1) * HEAD_DIM)
            qs[3 * i + j] = jnp.concatenate([q[:, lanes], query_tail], axis=1)
            kvs[3 * i + j] = jnp.concatenate([k[:, lanes], v[:, lanes]], axis=1)

    def out_step1():
        gat_in.step3()
        gat_out.step1()

    def out_step2():
        gat_out.step2()
        gat_out.step3()

    items = [(i, j, b) for i in range(4) for j in range(3) for b in range(2)]
    hooks = {
        0: [lambda: gat_in.ready(0)],
        3: [gat_in.step1],
        6: [lambda: gat_in.ready(1)],
        10: [gat_in.step2],
        12: [out_step1],
        16: [out_step2],
        18: [lambda: gat_in.ready(3)],
        21: [gat_up.step1],
    }
    scores, tops, expos, keys = {}, {}, {}, None
    for n in range(len(items) + 2):
        for hook in hooks.get(n, ()):
            hook()
        if n < len(items):
            i, j, b = items[n]
            if n % 6 == 0:
                project(i)
            if b == 0:
                keys = keys_of(3 * i + j)
            scores[n] = dot_nt(qs[3 * i + j, b * SLAB : (b + 1) * SLAB, :], keys)
        if n >= 2:
            i, j, b = items[n - 2]
            head, rows = 3 * i + j, slice(b * SLAB, (b + 1) * SLAB)
            mixed = dot_nn(expos.pop(n - 2), values_of(head))
            total = mixed[:, 0:1]
            att[i, rows, j * HEAD_DIM : (j + 1) * HEAD_DIM] = (mixed * (1.0 / total))[
                :, HEAD_DIM:
            ].astype(BF16)
            high, middle, low = pieces(-(tops.pop(n - 2) + jnp.log2(total)))
            qs[head, rows, :] = jnp.where(
                row_lane == HEAD_DIM + 1,
                high,
                jnp.where(
                    row_lane == HEAD_DIM + 2,
                    middle,
                    jnp.where(row_lane == HEAD_DIM + 3, low, qs[head, rows, :]),
                ),
            )
        if 1 <= n <= len(items):
            score = scores.pop(n - 1)
            tops[n - 1] = jnp.max(score, axis=-1, keepdims=True)
            expos[n - 1] = jnp.exp2(score - tops[n - 1]).astype(BF16)
    for i in (0, 1, 3):
        gat_out.ready(i)
    for b in range(2):
        at = slice(b * SLAB, (b + 1) * SLAB)
        total = tokens[at, :].astype(F32)
        for i in range(4):
            _, _, ti = peer(i)
            total = total + dot_nn(att[i, at, :], wout[span(ti * PART, PART), :])
        mid[at, :] = total
        hat, _ = normalize(total)
        mid_low[at, :] = (hat * gain1 + bias1).astype(BF16)
    cot_load.wait()

    red_down = Reduce(m, place, g_down, in_down, grad_down)
    red_up = Reduce(m, place, g_up, in_up, grad_up)
    red_io = [
        Reduce(m, place, wdown.at[j], wup.at[:, j * SLAB : (j + 1) * SLAB], res_io.at[j]) for j in range(3)
    ]

    def feed_forward(i, hooks):
        xi, ci, ti = peer(i)
        for f in range(3):
            if f in hooks:
                hooks[f]()
            lanes = slice(f * SLAB, (f + 1) * SLAB)
            hidden = dot_nn(mid_low[...], wup[span(ti * WIDTH, WIDTH), lanes])
            back = jnp.zeros((ROWS, SLAB), F32)
            for s in range(3):
                back = back + dot_nt(
                    cot[:, s * SLAB : (s + 1) * SLAB], wdown[s, span(ti * WIDTH + f * SLAB, SLAB), :]
                )
            cdf = 0.5 + 0.5 * lax.erf(hidden * math.sqrt(0.5))
            pdf = jnp.exp2(hidden * hidden * (-0.5 * LOG2E)) * (1.0 / math.sqrt(2.0 * math.pi))
            act[i, :, lanes] = (hidden * cdf).astype(BF16)
            hid_grad[:, lanes] = (back * (cdf + hidden * pdf)).astype(BF16)
        for s in range(3):
            lanes = slice(s * SLAB, (s + 1) * SLAB)
            up = dot_nt(hid_grad[...], wup[span(ti * WIDTH + s * SLAB, SLAB), :])
            if i == 1:
                acc_b[:, lanes] = up
            else:
                acc_b[:, lanes] += up
        for b in range(2):
            lanes = slice(b * 384, (b + 1) * 384)
            red_down.put(dot_tn(cot[:, lanes], act[i]), 4 * b, xi, ci)
            red_up.put(dot_tn(mid_low[:, lanes], hid_grad[...]), 4 * b, xi, ci)

    def down_step1():
        for gat in gat_down:
            gat.step1()

    for gat in ff_weights:
        gat.ready(0)
        gat.ready(1)
    feed_forward(1, {1: down_step1})
    red_down.send_core("near")
    red_up.send_core("near")
    feed_forward(0, {0: gat_up.step2, 2: gat_up.step3})
    red_down.add_core("near")
    red_up.add_core("near")
    for gat in gat_down:
        gat.step2()
        gat.step3()
    feed_forward(2, {})
    for gat in ff_weights:
        gat.ready(3)
    feed_forward(3, {})
    for gat in ff_weights:
        gat.finish()
    red_down.send_core("far")
    red_up.send_core("far")
    for s in range(3):
        lanes = slice(s * SLAB, (s + 1) * SLAB)
        for b in range(2):
            rows = slice(b * SLAB, (b + 1) * SLAB)
            total = None
            for i in range(4):
                _, _, ti = peer(i)
                part = dot_nn(act[i, rows, :], wdown[s, span(ti * WIDTH, WIDTH), :])
                total = part if i == 0 else total + part
            stage[rows, lanes] = (mid[rows, lanes] + total).astype(BF16)
    block_store = m.local(stage, block_out)

    def norm_back(grad, hat, rstd, gain):
        e = grad * gain
        mean_e = jnp.mean(e, axis=-1, keepdims=True)
        mean_eh = jnp.mean(e * hat, axis=-1, keepdims=True)
        return rstd * (e - mean_e - hat * mean_eh)

    def column_sum(values):
        return jnp.sum(values, axis=0, keepdims=True)

    gain_sum = jnp.zeros((1, WIDTH), F32)
    bias_sum = jnp.zeros((1, WIDTH), F32)
    for b in range(4):
        at = slice(b * 128, (b + 1) * 128)
        grad = acc_b[at, :]
        hat, rstd = normalize(mid[at, :])
        total = cot[at, :].astype(F32) + norm_back(grad, hat, rstd, gain1)
        gain_sum = gain_sum + column_sum(grad * hat)
        bias_sum = bias_sum + column_sum(grad)
        mid[at, :] = total
        mid_low[at, :] = total.astype(BF16)
    norm_sum[1:2, :] = gain_sum
    norm_sum[3:4, :] = bias_sum

    red_down.add_core("far")
    for i in range(4):
        _, _, ti = peer(i)
        hid_grad[:, i * PART : (i + 1) * PART] = dot_nt(
            mid_low[...], wout[span(ti * PART, PART), :]
        ).astype(BF16)
    red_up.add_core("far")

    def grads_of(i, j, rows):
        lanes = slice(j * HEAD_DIM, (j + 1) * HEAD_DIM)
        grad = hid_grad[rows, i * PART + j * HEAD_DIM : i * PART + (j + 1) * HEAD_DIM]
        inner = jnp.sum(grad.astype(F32) * att[i, rows, lanes].astype(F32), axis=-1, keepdims=True)
        high, middle, low = pieces(-inner)
        both = jnp.concatenate([grad, grad], axis=1)
        head_lanes = jnp.where(
            row_lane == 0,
            high,
            jnp.where(row_lane == 1, middle, jnp.where(row_lane == 2, low, jnp.zeros_like(both))),
        )
        return jnp.where(row_lane >= HEAD_DIM, both, head_lanes)

    def projection_grads(j, pair):
        def lanes_of(ref, rows):
            return [ref[i, rows, j * HEAD_DIM : (j + 1) * HEAD_DIM] for i in pair]

        every, low_lane = slice(None), lax.broadcasted_iota(jnp.int32, (384, 2 * HEAD_DIM), 1) < HEAD_DIM
        query = jnp.concatenate(lanes_of(dqs, every), axis=1)
        mixed = jnp.concatenate(lanes_of(att, every), axis=1)
        k, v = lanes_of(dks, every), lanes_of(dvs, every)
        both = jnp.concatenate([k[0], v[0], k[1], v[1]], axis=1)
        for b in range(2):
            lanes = slice(b * 384, (b + 1) * 384)
            q = dot_tn(normed[own_rows, lanes], query)
            o = dot_tn(mid_low[:, lanes], mixed)
            kv = dot_tn(normed[:, lanes], both)
            first = jnp.where(low_lane, q, pltpu.roll(o, HEAD_DIM, 1))
            second = jnp.where(low_lane, pltpu.roll(q, HEAD_DIM, 1), o)
            for n, qo in enumerate((first, second)):
                xi, ci, _ = peer(pair[n])
                value = jnp.concatenate([qo, kv[:, n * 128 : (n + 1) * 128]], axis=1)
                red_io[j].put(value, 4 * b, xi, ci)

    def far(j):
        projection_grads(j, (3, 2))
        if j == 0:
            block_store.wait()
        red_io[j].send_core("far")

    def near(j):
        projection_grads(j, (1, 0))
        red_io[j].send_core("near")

    def step(red, *what):
        for third, stage in what:
            red.step(third, stage)

    plan = {
        3: [lambda: step(red_down, (1, 1), (2, 1))],
        5: [lambda: far(0), lambda: step(red_down, (0, 1))],
        7: [lambda: red_io[0].add_core("far"), lambda: step(red_up, (1, 1), (2, 1))],
        9: [lambda: near(0)],
        11: [lambda: red_io[0].add_core("near"), lambda: step(red_down, (1, 2), (0, 2))],
        13: [lambda: far(1), lambda: step(red_up, (0, 1))],
        15: [lambda: red_io[1].add_core("far"), lambda: step(red_up, (1, 2)), lambda: step(red_down, (2, 2))],
        17: [lambda: near(1), lambda: step(red_down, (0, 3))],
        19: [lambda: red_io[1].add_core("near"), lambda: step(red_up, (0, 2))],
        21: [lambda: far(2), lambda: step(red_down, (1, 3)), lambda: step(red_up, (2, 2))],
        23: [lambda: red_io[2].add_core("far"), lambda: step(red_down, (2, 3))],
        25: [lambda: near(2), lambda: step(red_io[0], (1, 1), (2, 1), (0, 1))],
    }
    items = [(i, j, b) for j in range(3) for i in (3, 2, 1, 0) for b in range(2)]
    raw, ready, sums = {}, {}, None
    for n in range(len(items) + 2):
        if n < len(items):
            i, j, b = items[n]
            head, rows = 3 * i + j, slice(b * SLAB, (b + 1) * SLAB)
            both = grads_of(i, j, rows)
            raw[n] = dot_nt(qs[head, rows, :], keys_of(head)), dot_nt(both, values_of(head)), both
        if n >= 2:
            i, j, b = items[n - 2]
            head, rows = 3 * i + j, slice(b * SLAB, (b + 1) * SLAB)
            lanes = slice(j * HEAD_DIM, (j + 1) * HEAD_DIM)
            probs, score_grads, both = ready.pop(n - 2)
            dqs[i, rows, lanes] = (
                dot_nn(score_grads, keys_of(head))[:, :HEAD_DIM] * HEAD_DIM ** (-0.5)
            ).astype(BF16)
            key_part = dot_tn(score_grads, qs[head, rows, :])
            value_part = dot_tn(probs, both)
            if b == 0:
                sums = key_part, value_part
            else:
                dks[i, :, lanes] = ((sums[0] + key_part)[:, :HEAD_DIM] * LN2).astype(BF16)
                dvs[i, :, lanes] = (sums[1] + value_part)[:, HEAD_DIM:].astype(BF16)
        if 1 <= n <= len(items):
            score, prob_grad, both = raw.pop(n - 1)
            probs = jnp.exp2(score)
            ready[n - 1] = probs.astype(BF16), (probs * prob_grad).astype(BF16), both
        for event in plan.get(n, ()):
            event()

    for n in range(3):
        lanes = slice(n * SLAB, (n + 1) * SLAB)
        total = None
        for i in range(4):
            _, _, ti = peer(i)
            at = span(ti * PART, PART)
            part = dot_nn(dks[i, other_rows, :], win[1, at, lanes]) + dot_nn(
                dvs[i, other_rows, :], win[2, at, lanes]
            )
            total = part if i == 0 else total + part
        mid_low[:, lanes] = total.astype(BF16)
    dn_copy = m.remote(mid_low, act.at[0], m.slot(), "c")
    red_io[2].add_core("near")
    step(red_io[1], (1, 1), (2, 1), (0, 1))
    for n in range(3):
        lanes = slice(n * SLAB, (n + 1) * SLAB)
        total = None
        for i in range(4):
            _, _, ti = peer(i)
            at = span(ti * PART, PART)
            part = (
                dot_nn(dqs[i], win[0, at, lanes])
                + dot_nn(dks[i, own_rows, :], win[1, at, lanes])
                + dot_nn(dvs[i, own_rows, :], win[2, at, lanes])
            )
            total = part if i == 0 else total + part
        acc_b[:, lanes] = total
    step(red_up, (0, 3), (1, 3), (2, 3))
    step(red_io[0], (1, 2), (0, 2), (2, 2))
    step(red_io[2], (1, 1), (2, 1), (0, 1))
    step(red_io[1], (1, 2), (0, 2), (2, 2))
    dn_copy.wait_recv()
    gain_sum = jnp.zeros((1, WIDTH), F32)
    bias_sum = jnp.zeros((1, WIDTH), F32)
    for b in range(4):
        at = slice(b * 128, (b + 1) * 128)
        grad = acc_b[at, :] + act[0, at, :].astype(F32)
        hat, rstd = normalize(tokens[at, :].astype(F32))
        hid_grad[at, :] = (mid[at, :] + norm_back(grad, hat, rstd, gain0)).astype(BF16)
        gain_sum = gain_sum + column_sum(grad * hat)
        bias_sum = bias_sum + column_sum(grad)
    store = m.local(hid_grad, input_grad)
    norm_sum[0:1, :] = gain_sum
    norm_sum[2:3, :] = bias_sum

    def share(stage):
        grad_norm[...] = norm_sum[0:4, :]
        norm_box[2 * stage, 0:4, :] = grad_norm[...]
        return m.remote(norm_box.at[2 * stage], norm_box.at[2 * stage + 1], m.slot(), "cxylh"[stage])

    copy = share(0)
    step(red_down, (0, 4), (1, 4), (2, 4))
    step(red_io[0], (0, 3), (1, 3), (2, 3))
    step(red_io[2], (1, 2), (0, 2), (2, 2))
    step(red_io[1], (0, 3), (1, 3), (2, 3))
    last = [
        lambda: step(red_io[2], (0, 3), (1, 3), (2, 3)),
        lambda: step(red_up, (0, 4), (1, 4), (2, 4)),
        lambda: None,
        lambda: [step(red_io[j], (0, 4), (1, 4), (2, 4)) for j in (0, 1)],
        lambda: step(red_io[2], (0, 4), (1, 4), (2, 4)),
    ]
    for stage in range(5):
        copy.wait_recv()
        norm_sum[0:4, :] = norm_box[2 * stage, 0:4, :] + norm_box[2 * stage + 1, 0:4, :]
        if stage < 4:
            copy = share(stage + 1)
        last[stage]()
    grad_norm[...] = norm_sum[0:4, :]
    for j in range(3):
        lanes = slice(j * HEAD_DIM, (j + 1) * HEAD_DIM)
        block = res_io[j]
        for k, part in enumerate((0, 2, 3)):
            grad_in[k, :, lanes] = block[:, part * HEAD_DIM : (part + 1) * HEAD_DIM]
        grad_out[:, lanes] = block[:, HEAD_DIM : 2 * HEAD_DIM]
    store.wait()
    m.finish()


def write_results(*refs):
    sources, grad_out, norms = refs[:5], refs[5], refs[6]
    targets, out, gains, biases = refs[7:12], refs[12], refs[13], refs[14]
    stages, sems = refs[15:20], refs[20]
    loads = [pltpu.make_async_copy(a, b, sems.at[k]) for k, (a, b) in enumerate(zip(sources, stages))]
    stores = [pltpu.make_async_copy(a, b, sems.at[5 + k]) for k, (a, b) in enumerate(zip(stages, targets))]
    for copy in loads:
        copy.start()
    out[...] = grad_out[...].T
    gains[...] = norms[0:2, :]
    biases[...] = norms[2:4, :]
    for load, store in zip(loads, stores):
        load.wait()
        store.start()
    for copy in stores:
        copy.wait()


def fused(tokens, gene_counts, in_proj, out_proj, up_proj, down_proj, gains, biases, cotangent):
    vmem = pl.BlockSpec(memory_space=pltpu.VMEM)
    hbm = pl.BlockSpec(memory_space=pl.ANY)
    shape = jax.ShapeDtypeStruct
    outs = pl.pallas_call(
        kernel,
        out_shape=(
            shape((ROWS, WIDTH), BF16),
            shape((ROWS, WIDTH), BF16),
            shape((3, CHUNK, PART), F32),
            shape((CHUNK, WIDTH), F32),
            shape((CHUNK, WIDTH), F32),
            shape((CHUNK, PART), F32),
            shape((4, WIDTH), F32),
        ),
        in_specs=[pl.BlockSpec(memory_space=pltpu.SMEM)] + [hbm] * 6 + [vmem] * 2,
        out_specs=[hbm, hbm] + [vmem] * 5,
        scratch_shapes=[
            pltpu.VMEM((ROWS, WIDTH), BF16),
            pltpu.VMEM((2 * ROWS, WIDTH), BF16),
            pltpu.VMEM((ROWS, WIDTH), BF16),
            pltpu.VMEM((3, WIDTH, WIDTH), BF16),
            pltpu.VMEM((WIDTH, WIDTH), BF16),
            pltpu.VMEM((4 * WIDTH, WIDTH), BF16),
            pltpu.VMEM((3, 4 * WIDTH, SLAB), BF16),
            pltpu.VMEM((12, ROWS, 2 * HEAD_DIM), BF16),
            pltpu.VMEM((12, 2 * ROWS, 2 * HEAD_DIM), BF16),
            pltpu.VMEM((4, ROWS, PART), BF16),
            pltpu.VMEM((ROWS, WIDTH), F32),
            pltpu.VMEM((ROWS, WIDTH), BF16),
            pltpu.VMEM((4, ROWS, WIDTH), BF16),
            pltpu.VMEM((ROWS, WIDTH), BF16),
            pltpu.VMEM((ROWS, WIDTH), BF16),
            pltpu.VMEM((ROWS, WIDTH), F32),
            pltpu.VMEM((4, ROWS, PART), BF16),
            pltpu.VMEM((4, 2 * ROWS, PART), BF16),
            pltpu.VMEM((4, 2 * ROWS, PART), BF16),
            pltpu.VMEM((4 * WIDTH, WIDTH), BF16),
            pltpu.VMEM((4 * WIDTH, WIDTH), BF16),
            pltpu.VMEM((31 * CHUNK, WIDTH), BF16),
            pltpu.VMEM((31 * CHUNK, WIDTH), BF16),
            pltpu.VMEM((3, CHUNK, SLAB), F32),
            pltpu.VMEM((10, 8, WIDTH), F32),
            pltpu.VMEM((8, WIDTH), F32),
            pltpu.SemaphoreType.DMA((224,)),
            pltpu.SemaphoreType.DMA((224,)),
        ],
        compiler_params=pltpu.CompilerParams(
            collective_id=0, has_side_effects=True, vmem_limit_bytes=64 * 2**20
        ),
    )(
        gene_counts,
        tokens,
        cotangent,
        jnp.swapaxes(in_proj, 1, 2),
        out_proj,
        up_proj,
        down_proj,
        gains,
        biases,
    )
    results = pl.pallas_call(
        write_results,
        out_shape=(
            *(shape(o.shape, o.dtype) for o in outs[:5]),
            shape((PART, CHUNK), F32),
            shape((2, WIDTH), F32),
            shape((2, WIDTH), F32),
        ),
        in_specs=[hbm] * 5 + [vmem] * 2,
        out_specs=[hbm] * 5 + [vmem] * 3,
        scratch_shapes=[
            *(pltpu.VMEM(o.shape, o.dtype) for o in outs[:5]),
            pltpu.SemaphoreType.DMA((10,)),
        ],
    )(*outs)
    block_out, input_grad, grad_in, grad_up, grad_down, grad_out, grad_gains, grad_biases = results
    return (
        block_out,
        input_grad,
        grad_in,
        grad_out,
        grad_up,
        grad_down.T,
        grad_gains,
        grad_biases,
    )


def layer_norm(values, gain, offset):
    center = values - jnp.mean(values, axis=-1, keepdims=True)
    spread = jnp.mean(center * center, axis=-1, keepdims=True)
    return center * lax.rsqrt(spread + EPS) * gain + offset


def gelu_exact(values):
    return jax.nn.gelu(values, approximate=False)


def per_device(
    tokens, gene_counts, in_proj, out_proj, up_proj, down_proj, gains, biases, cotangent
):
    rows = tokens.shape[0]
    cells = gene_counts.shape[0]
    group = rows * lax.axis_size("tensor")
    length = group // cells
    local_width = out_proj.shape[0]
    heads = local_width // HEAD_DIM
    block = min(length, 512)
    blocks = length // block
    scale = HEAD_DIM ** (-0.5)
    positions = jnp.arange(length, dtype=jnp.int32)
    resid = tokens.astype(jnp.float32)
    normed, first_back = jax.vjp(layer_norm, resid, gains[0], biases[0])
    normed_all = lax.all_gather(normed.astype(jnp.bfloat16), "tensor", axis=0, tiled=True)
    projected = jnp.einsum(
        "td,cde->cte", normed_all, in_proj, preferred_element_type=jnp.float32
    ).astype(jnp.bfloat16)
    query_cells = projected[0].reshape(cells, blocks, block, local_width)
    key_cells = projected[1].reshape(cells, length, local_width)
    value_cells = projected[2].reshape(cells, length, local_width)

    def block_scores(query_block, key_rows, count):
        query_heads = query_block.reshape(block, heads, HEAD_DIM)
        key_heads = key_rows.reshape(length, heads, HEAD_DIM)
        scores = (
            jnp.einsum("qhd,khd->hqk", query_heads, key_heads, preferred_element_type=jnp.float32)
            * scale
        )
        return jnp.where((positions < count)[None, None, :], scores, NEG)

    def cell_forward(item):
        queries, key_rows, value_rows, count = item
        value_heads = value_rows.reshape(length, heads, HEAD_DIM)

        def one_block(query_block):
            scores = block_scores(query_block, key_rows, count)
            top = jnp.max(scores, axis=-1, keepdims=True)
            expo = jnp.exp(scores - top)
            total = jnp.sum(expo, axis=-1, keepdims=True)
            probs = (expo / total).astype(jnp.bfloat16)
            result = jnp.einsum(
                "hqk,khd->qhd", probs, value_heads, preferred_element_type=jnp.float32
            )
            return (
                result.reshape(block, local_width).astype(jnp.bfloat16),
                (top + jnp.log(total))[..., 0],
            )

        return lax.map(one_block, queries)

    attended, log_totals = lax.map(cell_forward, (query_cells, key_cells, value_cells, gene_counts))
    attended = attended.reshape(group, local_width)
    piece = attended
    mid = resid + lax.psum_scatter(
        jnp.dot(piece, out_proj, preferred_element_type=jnp.float32),
        "tensor",
        scatter_dimension=0,
        tiled=True,
    )
    normed_mid, second_back = jax.vjp(layer_norm, mid, gains[1], biases[1])
    mid_low = normed_mid.astype(jnp.bfloat16)
    mid_all = lax.all_gather(mid_low, "tensor", axis=0, tiled=True)
    hidden = jnp.dot(mid_all, up_proj, preferred_element_type=jnp.float32)
    active = gelu_exact(hidden).astype(jnp.bfloat16)
    piece = active
    block_out = (
        mid
        + lax.psum_scatter(
            jnp.dot(piece, down_proj, preferred_element_type=jnp.float32).astype(jnp.bfloat16),
            "tensor",
            scatter_dimension=0,
            tiled=True,
        ).astype(jnp.float32)
    ).astype(jnp.bfloat16)
    out_grads = lax.all_gather(cotangent, "tensor", axis=0, tiled=True)
    _, gelu_back = jax.vjp(gelu_exact, hidden)
    active_grad = jnp.einsum("td,fd->tf", out_grads, down_proj, preferred_element_type=jnp.float32)
    hidden_grad = gelu_back(active_grad)[0].astype(jnp.bfloat16)
    grad_down = jnp.einsum("tf,td->fd", active, out_grads, preferred_element_type=jnp.float32)
    grad_up = jnp.einsum("td,tf->df", mid_all, hidden_grad, preferred_element_type=jnp.float32)
    piece = hidden_grad
    mid_grad = lax.psum_scatter(
        jnp.einsum("tf,df->td", piece, up_proj, preferred_element_type=jnp.float32),
        "tensor",
        scatter_dimension=0,
        tiled=True,
    )
    resid_part, gain_second, bias_second = second_back(mid_grad)
    mid_total = cotangent.astype(jnp.float32) + resid_part
    branch_all = lax.all_gather(mid_total.astype(jnp.bfloat16), "tensor", axis=0, tiled=True)
    attended_grad = jnp.einsum(
        "td,ed->te", branch_all, out_proj, preferred_element_type=jnp.float32
    ).astype(jnp.bfloat16)
    grad_out = jnp.einsum("te,td->ed", attended, branch_all, preferred_element_type=jnp.float32)

    def cell_backward(item):
        queries, key_rows, value_rows, count, grad_rows, totals = item
        key_heads = key_rows.reshape(length, heads, HEAD_DIM)
        value_heads = value_rows.reshape(length, heads, HEAD_DIM)

        def one_block(carry, part):
            key_sum, value_sum = carry
            query_block, grad_block, total_block = part
            scores = block_scores(query_block, key_rows, count)
            probs = jnp.exp(scores - total_block[..., None])
            grad_heads = grad_block.reshape(block, heads, HEAD_DIM)
            query_heads = query_block.reshape(block, heads, HEAD_DIM)
            prob_grads = jnp.einsum(
                "qhd,khd->hqk", grad_heads, value_heads, preferred_element_type=jnp.float32
            )
            inner = jnp.sum(probs * prob_grads, axis=-1, keepdims=True)
            score_grads = (probs * (prob_grads - inner)).astype(jnp.bfloat16)
            query_grad = (
                jnp.einsum(
                    "hqk,khd->qhd", score_grads, key_heads, preferred_element_type=jnp.float32
                )
                * scale
            )
            key_sum = (
                key_sum
                + jnp.einsum(
                    "hqk,qhd->khd", score_grads, query_heads, preferred_element_type=jnp.float32
                )
                * scale
            )
            value_sum = value_sum + jnp.einsum(
                "hqk,qhd->khd",
                probs.astype(jnp.bfloat16),
                grad_heads,
                preferred_element_type=jnp.float32,
            )
            return (
                (key_sum, value_sum),
                query_grad.reshape(block, local_width).astype(jnp.bfloat16),
            )

        zeros = jnp.zeros((length, heads, HEAD_DIM), jnp.float32)
        (key_sum, value_sum), query_grads = lax.scan(
            one_block, (zeros, zeros), (queries, grad_rows, totals)
        )
        return (
            query_grads.reshape(length, local_width),
            key_sum.reshape(length, local_width).astype(jnp.bfloat16),
            value_sum.reshape(length, local_width).astype(jnp.bfloat16),
        )

    grad_cells = attended_grad.reshape(cells, blocks, block, local_width)
    query_grads, key_grads, value_grads = lax.map(
        cell_backward, (query_cells, key_cells, value_cells, gene_counts, grad_cells, log_totals)
    )
    proj_grads = jnp.stack(
        [
            query_grads.reshape(group, local_width),
            key_grads.reshape(group, local_width),
            value_grads.reshape(group, local_width),
        ]
    )
    grad_in = jnp.einsum("td,cte->cde", normed_all, proj_grads, preferred_element_type=jnp.float32)
    piece = proj_grads
    normed_grad = lax.psum_scatter(
        jnp.einsum("cte,cde->td", piece, in_proj, preferred_element_type=jnp.float32),
        "tensor",
        scatter_dimension=0,
        tiled=True,
    )
    resid_grad, gain_first, bias_first = first_back(normed_grad)
    input_grad = (mid_total + resid_grad).astype(jnp.bfloat16)
    grad_gains, grad_biases = lax.psum(
        (jnp.stack([gain_first, gain_second]), jnp.stack([bias_first, bias_second])),
        ("dp", "tensor"),
    )
    grad_in_part, grad_out_part, grad_up_part, grad_down_part = (
        lax.psum_scatter(grad_in, "dp", scatter_dimension=1, tiled=True),
        lax.psum_scatter(grad_out, "dp", scatter_dimension=1, tiled=True),
        lax.psum_scatter(grad_up, "dp", scatter_dimension=0, tiled=True),
        lax.psum_scatter(grad_down, "dp", scatter_dimension=1, tiled=True),
    )
    return (
        block_out,
        input_grad,
        grad_in_part,
        grad_out_part,
        grad_up_part,
        grad_down_part,
        grad_gains,
        grad_biases,
    )


def solution(mesh):
    placed = (
        P(("dp", "tensor"), None),
        P("dp"),
        P(None, None, "tensor"),
        P("tensor", None),
        P(None, "tensor"),
        P("tensor", None),
        P(),
        P(),
        P(("dp", "tensor"), None),
    )
    halves = mesh.shape["dp"] == 8 and mesh.shape["tensor"] == 4
    return jax.shard_map(
        fused if halves else per_device,
        mesh=mesh,
        in_specs=placed,
        out_specs=(
            P(("dp", "tensor"), None),
            P(("dp", "tensor"), None),
            P(None, "dp", "tensor"),
            P("tensor", "dp"),
            P("dp", "tensor"),
            P("tensor", "dp"),
            P(),
            P(),
        ),
        check_vma=False,
    )
```

```python
import itertools
import math

import jax
import jax.numpy as jnp
from jax import lax
from jax.experimental import pallas as pl
from jax.experimental.pallas import tpu as pltpu
from jax.sharding import PartitionSpec as P

HEAD_DIM = 64
EPS = 1e-05
NEG = -1e30
F32 = jnp.float32
BF16 = jnp.bfloat16
MESH = pl.DeviceIdType.MESH
LOG2E = math.log2(math.e)
LN2 = math.log(2.0)
ROWS = 512
WIDTH = 768
PART = 192
CHUNK = 96
SLAB = 256
THIRD = 32
ORDERS = ("xylh", "ylxh", "lxyh")
WEIGHT = {"x": 8, "y": 4, "l": 2, "h": 1}
BOX = (0, 16, 24, 28, 30)
SEMAPHORES = 146


def dot_nn(left, right):
    return lax.dot_general(left, right, (((1,), (0,)), ((), ())), preferred_element_type=F32)


def dot_nt(left, right):
    return lax.dot_general(left, right, (((1,), (1,)), ((), ())), preferred_element_type=F32)


def dot_tn(left, right):
    return lax.dot_general(left, right, (((0,), (0,)), ((), ())), preferred_element_type=F32)


def span(start, size):
    return pl.ds(pl.multiple_of(start, size), size)


def normalize(values):
    center = values - jnp.mean(values, axis=-1, keepdims=True)
    spread = jnp.mean(center * center, axis=-1, keepdims=True)
    rstd = lax.rsqrt(spread + EPS)
    return center * rstd, rstd


def pieces(values):
    high = values.astype(BF16)
    rest = values - high.astype(F32)
    middle = rest.astype(BF16)
    low = (rest - middle.astype(F32)).astype(BF16)
    return high, middle, low


class Mover:
    def __init__(self, where, sems):
        self.where, self.sems, self.count = where, sems, 0

    def slot(self):
        self.count += 1
        assert self.count <= SEMAPHORES
        return self.count - 1

    def remote(self, source, target, sent, arrived, to):
        copy = pltpu.make_async_remote_copy(
            src_ref=source,
            dst_ref=target,
            send_sem=self.sems.at[sent],
            recv_sem=self.sems.at[arrived],
            device_id=self.where[to],
            device_id_type=MESH,
        )
        copy.start()
        return copy

    def local(self, source, target):
        copy = pltpu.make_async_copy(source, target, self.sems.at[self.slot()])
        copy.start()
        return copy

    def wait(self, slot, like):
        pltpu.make_async_copy(like, like, self.sems.at[slot]).wait()


class Gather:
    def __init__(self, mover, place, shard, full, view, halves):
        self.m, self.p, self.shard, self.full, self.view = mover, place, shard, full, view
        self.halves = halves
        forward = ("yf", "zf") if halves else ("x1",)
        self.slots = {k: mover.slot() for k in ("x0", "y", "z", "own", "core", *forward)}
        self.sent = mover.slot()
        self.copies = {}
        self.quarter = {k: place[k] for k in ("q", "qy", "qz", "qd")}

    def go(self, key, source, target, to):
        arrived = self.slots["core" if key[0] == "c" else key]
        self.copies[key] = self.m.remote(source, target, self.sent, arrived, to)

    def start_own(self):
        p = self.p
        mine = self.view(self.full, p["t"], 0, 4)
        self.load = self.m.local(self.view(self.shard, None, 0, 4), mine)
        self.go("own", self.view(self.shard, None, 0, 4), mine, "c")

    def start_x(self, key="x0", quarter="q"):
        p = self.p
        self.go(key, self.view(self.shard, None, p[quarter], 1), self.view(self.full, p["t"], p[quarter], 1), "x")

    def start_x1(self):
        self.start_x("x1", "qd")

    def pass_on(self, key, quarter, to, half=None):
        part = self.view(self.full, self.p["t2"], self.quarter[quarter], 1, half)
        self.go(key, part, part, to)

    def step1(self):
        self.copies["x0"].wait_recv()
        self.pass_on("y", "q", "y")
        self.pass_on("z", "q", "l")
        self.pass_on("c0", "q", "c")

    def step2(self):
        self.copies["y"].wait_recv()
        if self.halves:
            self.pass_on("zf", "qy", "l", 0)
        self.pass_on("c1", "qy", "c")
        self.copies["z"].wait_recv()
        if self.halves:
            self.pass_on("yf", "qz", "y", 1)
        self.pass_on("c2", "qz", "c")

    def step3(self):
        if self.halves:
            self.copies["zf"].wait_recv()
            self.copies["yf"].wait_recv()
        else:
            self.copies["x1"].wait_recv()
        self.pass_on("c3", "qd", "c")

    def finish(self):
        self.m.wait(self.sent, self.view(self.full, 0, 0, 12))

    def ready(self, i):
        if i == 0:
            self.load.wait()
        if i == 1:
            self.copies["own"].wait_recv()
        if i == 3:
            self.m.wait(self.slots["core"], self.view(self.full, self.p["t"], 0, 4))


class Reduce:
    def __init__(self, mover, place, own, away, inbox, result):
        self.m, self.p, self.own, self.away = mover, place, own, away
        self.inbox, self.result = inbox, result
        self.slots = {key: mover.slot() for key in ("near", "far", "last")}
        self.slots |= {(third, stage): mover.slot() for third in range(3) for stage in (1, 2, 3)}
        self.sent, self.core_sent = mover.slot(), mover.slot()

    def at(self, place, third, chunk, count):
        ref, half = place
        start = third * 32 * THIRD + half * 16 * THIRD + chunk * THIRD
        return ref.at[pl.ds(pl.multiple_of(start, THIRD), count * THIRD), :]

    def box(self, third, at, count):
        return pl.ds((third * 31 + at) * THIRD, count * THIRD)

    def put(self, value, first, x, away):
        for k in range(value.shape[0] // CHUNK):
            r = first + k
            chunk = 8 * x + 4 * (r % 2) + 2 * ((r // 2) % 2) + r // 4
            for third in range(3):
                start = k * CHUNK + third * THIRD
                target = self.at(self.away if away else self.own, third, chunk, 1)
                target[...] = value[start : start + THIRD, :].astype(BF16)

    def go(self, slot, third, source, at, count, to):
        self.m.remote(
            source,
            self.inbox.at[self.box(third, at, count), :],
            self.core_sent if to == "c" else self.sent,
            self.slots[slot],
            to,
        )

    def arrived(self, slot, count):
        self.m.wait(self.slots[slot], self.inbox.at[pl.ds(0, count * THIRD), :])

    def finish_core(self):
        self.m.wait(self.core_sent, self.inbox.at[pl.ds(0, 48 * THIRD), :])

    def finish(self):
        self.m.wait(self.sent, self.inbox.at[pl.ds(0, 45 * THIRD), :])

    def halves(self, side):
        return (self.p["x"], 0) if side == "near" else (1 - self.p["x"], 8)

    def send_core(self, side):
        x, at = self.halves(side)
        for third in range(3):
            self.go(side, third, self.at(self.away, third, 8 * x, 8), at, 8, "c")

    def add(self, third, chunk, count, at):
        here = self.at(self.own, third, chunk, count)
        here[...] = here[...] + self.inbox[self.box(third, at, count), :]

    def add_core(self, side):
        x, at = self.halves(side)
        self.arrived(side, 24)
        for third in range(3):
            self.add(third, 8 * x, 8, at)
            self.send(third, 1, side)

    def runs(self, third, stage):
        order = ORDERS[third]
        dim, fixed = order[stage - 1], order[: stage - 1]
        rest, count = list("xylh"), 1
        while rest and rest[-1] != dim and rest[-1] not in fixed:
            rest.pop()
            count *= 2
        free = [name for name in rest if name != dim and name not in fixed]
        found = []
        for values in itertools.product((0, 1), repeat=len(free)):
            flip = dict(zip(free, values))
            base = 0
            for name in rest:
                if name != dim:
                    own = self.p[name]
                    base = base + WEIGHT[name] * (1 - own if flip.get(name) else own)
            own = WEIGHT[dim] * self.p[dim]
            side = "far" if flip.get("x", dim == "x") else "near"
            found.append((base + own, base + WEIGHT[dim] - own, count, BOX[stage] + len(found) * count, side))
        return found

    def send(self, third, stage, side=None):
        slot = (third, stage) if stage < 4 else "last"
        for _, away, count, at, where in self.runs(third, stage):
            if side in (None, where):
                source = self.at(self.own, third, away, count)
                self.go(slot, third, source, at, count, ORDERS[third][stage - 1])

    def step(self, third, stage):
        self.arrived((third, stage), 16 >> stage)
        for keep, _, count, at, _ in self.runs(third, stage):
            self.add(third, keep, count, at)
        self.send(third, stage + 1)

    def last(self):
        self.arrived("last", 3)
        for third in range(3):
            ((keep, _, _, at, _),) = self.runs(third, 4)
            total = self.at(self.own, third, keep, 1)[...].astype(F32) + self.inbox[
                self.box(third, at, 1), :
            ].astype(F32)
            self.result[third * THIRD : (third + 1) * THIRD, :] = total


def kernel(
    counts,
    tokens_in,
    cot_in,
    win_in,
    wout_in,
    wup_in,
    wdown_in,
    gains,
    biases,
    block_out,
    input_grad,
    grad_in,
    grad_up,
    grad_down,
    grad_out,
    grad_norm,
    tokens,
    normed,
    cot,
    win,
    wout,
    wup,
    wdown,
    qs,
    kvs,
    key_tail,
    att,
    mid,
    mid_low,
    act,
    hid_grad,
    acc_b,
    dkvs,
    g_down,
    g_up,
    in_down,
    in_up,
    res_io,
    res_ff,
    res_in,
    res_out,
    norm_box,
    norm_sum,
    free,
    sems,
):
    d = lax.axis_index("dp")
    t = lax.axis_index("tensor")
    x = lax.div(t, 2)
    c = t - 2 * x
    y = lax.rem(d, 2)
    l = lax.rem(lax.div(d, 2), 2)
    h = lax.div(d, 4)
    where = {
        "c": (d, t + 1 - 2 * c),
        "x": (d, t + 2 - 4 * x),
        "y": (d + 1 - 2 * y, t),
        "l": (d + 2 - 4 * l, t),
        "h": (d + 4 - 8 * h, t),
        "xc": (d, 3 - t),
        "lh": (d + 2 - 4 * l + 4 - 8 * h, t),
    }
    place = {"x": x, "c": c, "y": y, "l": l, "h": h, "t": t, "t2": t + 2 - 4 * x}
    place["q"] = 2 * l + y
    place["qy"] = 2 * l + 1 - y
    place["qz"] = 2 * (1 - l) + y
    place["qd"] = 2 * (1 - l) + 1 - y
    m = Mover(where, sems)
    own_rows = span(c * ROWS, ROWS)
    other_rows = span((1 - c) * ROWS, ROWS)

    def view_in(lane):
        def view(ref, dev, first, parts, half=None):
            start, size = first * 48, parts * 48
            if half is not None:
                size = 32 if half == lane else 16
                start = start + (48 - size if half else 0)
            start = start if dev is None else dev * PART + start
            return ref.at[:, pl.ds(pl.multiple_of(start, 16), size), pl.ds(lane * 384, 384)]

        return view

    def view_out(ref, dev, first, parts, half=None):
        start = first * 48
        rows = pl.ds(pl.multiple_of(start if dev is None else dev * PART + start, 48), parts * 48)
        return ref.at[rows, :]

    def view_up(lane):
        def view(ref, dev, first, parts, half=None):
            start, size = first * PART, parts * PART
            if half is not None:
                start, size = start + half * CHUNK, CHUNK
            start = start if dev is None else dev * WIDTH + start
            return ref.at[pl.ds(pl.multiple_of(start, CHUNK), size), pl.ds(lane * 384, 384)]

        return view

    barrier = pltpu.get_barrier_semaphore()
    for to in where:
        pl.semaphore_signal(barrier, inc=1, device_id=where[to], device_id_type=MESH)
    tok_load = m.local(tokens_in, tokens)
    pl.semaphore_wait(barrier, len(where))
    gat_in = [Gather(m, place, win_in, win, view_in(k), True) for k in range(2)]
    gat_out = Gather(m, place, wout_in, wout, view_out, False)
    gat_up = [Gather(m, place, wup_in, wup, view_up(k), True) for k in range(2)]
    gat_down = [Gather(m, place, wdown_in, wdown, view_up(k), False) for k in range(2)]
    ff_weights = [*gat_up, *gat_down]
    for gat in gat_in:
        gat.start_x()
    core_sent = m.slot()
    tok_copy = m.remote(tokens_in, mid_low, core_sent, m.slot(), "c")
    for gat in gat_in:
        gat.start_own()
    gat_out.start_x()
    gat_out.start_x1()
    for gat in ff_weights:
        gat.start_x()
    for gat in gat_down:
        gat.start_x1()
    cot_load = m.local(cot_in, cot)
    for gat in (gat_out, *ff_weights):
        gat.start_own()

    gain0, bias0 = gains[0:1, :], biases[0:1, :]
    gain1, bias1 = gains[1:2, :], biases[1:2, :]

    def norm_rows(source, first):
        @pl.loop(0, ROWS // 64)
        def _(k):
            hat, _ = normalize(source[span(k * 64, 64), :].astype(F32))
            normed[span(first + k * 64, 64), :] = (hat * gain0 + bias0).astype(BF16)

    tok_load.wait()
    norm_rows(tokens, c * ROWS)
    tok_copy.wait_recv()
    norm_rows(mid_low, (1 - c) * ROWS)

    count = counts[x]
    lane = lax.broadcasted_iota(jnp.int32, (1, 2 * HEAD_DIM), 1)
    low_lane = lane < HEAD_DIM

    @pl.loop(0, 2 * ROWS // 128)
    def _(k):
        at = k * 128 + lax.broadcasted_iota(jnp.int32, (128, 2 * HEAD_DIM), 0)
        column = lax.broadcasted_iota(jnp.int32, (128, 2 * HEAD_DIM), 1)
        key_tail[span(k * 128, 128), :] = jnp.where(
            column == HEAD_DIM,
            jnp.where(at < count, 0.0, NEG),
            jnp.where(column < HEAD_DIM + 4, 1.0, 0.0),
        ).astype(BF16)

    value_tail = jnp.where(lane < 3, 1.0, 0.0).astype(BF16)
    query_tail = jnp.where(lane[:, :HEAD_DIM] == 0, 1.0, 0.0).astype(BF16)

    def keys_of(head):
        return jnp.where(low_lane, kvs[head], key_tail[...])

    def values_of(head):
        return jnp.where(low_lane, value_tail, kvs[head])

    def peer(i):
        xi = x if i < 2 else 1 - x
        ci = c if i % 2 == 0 else 1 - c
        return xi, ci, 2 * xi + ci

    def project(i):
        _, _, ti = peer(i)
        part = span(ti * PART, PART)
        q = dot_nt(normed[own_rows, :], win[0, part, :]) * (HEAD_DIM ** (-0.5) * LOG2E)
        q = q.astype(BF16)
        k = dot_nt(normed[...], win[1, part, :]).astype(BF16)
        v = dot_nt(normed[...], win[2, part, :]).astype(BF16)
        for j in range(3):
            lanes = slice(j * HEAD_DIM, (j + 1) * HEAD_DIM)
            qs[3 * i + j] = jnp.concatenate(
                [q[:, lanes], jnp.broadcast_to(query_tail, (ROWS, HEAD_DIM))], axis=1
            )
            kvs[3 * i + j] = jnp.concatenate([k[:, lanes], v[:, lanes]], axis=1)

    items = [(i, j, b) for i in range(4) for j in range(3) for b in range(2)]
    hooks = {
        0: [lambda: gat_in[0].ready(0), lambda: gat_in[1].ready(0)],
        1: [gat_in[0].step1],
        3: [gat_in[1].step1],
        6: [gat_in[0].step2, lambda: gat_in[0].ready(1), lambda: gat_in[1].ready(1)],
        8: [gat_in[1].step2, gat_out.step1],
        12: [gat_in[0].step3, gat_in[1].step3, gat_up[0].step1],
        13: [gat_out.step2, gat_out.step3],
        15: [gat_up[1].step1],
        17: [gat_up[0].step2],
        18: [gat_down[0].step1, lambda: gat_in[0].ready(3), lambda: gat_in[1].ready(3)],
        20: [gat_up[1].step2],
        22: [gat_down[1].step1, gat_up[0].step3],
    }
    scores, tops, expos, keys = {}, {}, {}, None
    for n in range(len(items) + 2):
        for hook in hooks.get(n, ()):
            hook()
        if n < len(items):
            i, j, b = items[n]
            if n % 6 == 0:
                project(i)
            if b == 0:
                keys = keys_of(3 * i + j)
            scores[n] = dot_nt(qs[3 * i + j, b * SLAB : (b + 1) * SLAB, :], keys)
        if n >= 2:
            i, j, b = items[n - 2]
            head, rows = 3 * i + j, slice(b * SLAB, (b + 1) * SLAB)
            mixed = dot_nn(expos.pop(n - 2), values_of(head))
            total = mixed[:, 0:1]
            att[i, rows, j * HEAD_DIM : (j + 1) * HEAD_DIM] = (mixed * (1.0 / total))[
                :, HEAD_DIM:
            ].astype(BF16)
            high, middle, low = pieces(-(tops.pop(n - 2) + jnp.log2(total)))
            qs[head, rows, :] = jnp.where(
                lane == HEAD_DIM + 1,
                high,
                jnp.where(
                    lane == HEAD_DIM + 2,
                    middle,
                    jnp.where(lane == HEAD_DIM + 3, low, qs[head, rows, :]),
                ),
            )
        if 1 <= n <= len(items):
            score = scores.pop(n - 1)
            tops[n - 1] = jnp.max(score, axis=-1, keepdims=True)
            expos[n - 1] = jnp.exp2(score - tops[n - 1]).astype(BF16)
    for i in (0, 1, 3):
        gat_out.ready(i)
    for b in range(2):
        at = slice(b * SLAB, (b + 1) * SLAB)
        total = tokens[at, :].astype(F32)
        for i in range(4):
            _, _, ti = peer(i)
            total = total + dot_nn(att[i, at, :PART], wout[span(ti * PART, PART), :])
        mid[at, :] = total
        hat, _ = normalize(total)
        mid_low[at, :] = (hat * gain1 + bias1).astype(BF16)
    cot_load.wait()

    red_down = Reduce(m, place, (g_down, c), (g_down, 1 - c), in_down, res_ff)
    red_up = Reduce(m, place, (g_up, c), (g_up, 1 - c), in_up, res_ff)
    red_io = []
    for j in range(3):
        lanes = slice(j * SLAB, (j + 1) * SLAB)
        red_io.append(
            Reduce(
                m, place, (g_down.at[:, lanes], 1 - c), (g_up.at[:, lanes], 1 - c), wup.at[:, lanes], res_io
            )
        )

    def feed_forward(i, hooks):
        xi, _, ti = peer(i)
        for f in range(3):
            if f in hooks:
                hooks[f]()
            lanes = slice(f * SLAB, (f + 1) * SLAB)
            hidden = dot_nn(mid_low[...], wup[span(ti * WIDTH, WIDTH), lanes])
            back = dot_nt(cot[...], wdown[span(ti * WIDTH + f * SLAB, SLAB), :])
            cdf = 0.5 + 0.5 * lax.erf(hidden * math.sqrt(0.5))
            pdf = jnp.exp2(hidden * hidden * (-0.5 * LOG2E)) * (1.0 / math.sqrt(2.0 * math.pi))
            act[i, :, lanes] = (hidden * cdf).astype(BF16)
            hid_grad[:, lanes] = (back * (cdf + hidden * pdf)).astype(BF16)
        for s in range(3):
            lanes = slice(s * SLAB, (s + 1) * SLAB)
            up = dot_nt(hid_grad[...], wup[span(ti * WIDTH + s * SLAB, SLAB), :])
            if i == 1:
                acc_b[:, lanes] = up
            else:
                acc_b[:, lanes] += up
        for b in range(2):
            lanes = slice(b * 384, (b + 1) * 384)
            red_down.put(dot_tn(cot[:, lanes], act[i]), 4 * b, xi, i % 2)
            red_up.put(dot_tn(mid_low[:, lanes], hid_grad[...]), 4 * b, xi, i % 2)

    for gat in ff_weights:
        gat.ready(0)
        gat.ready(1)
    feed_forward(1, {0: gat_down[0].step2, 2: gat_down[1].step2})
    red_down.send_core("near")
    red_up.send_core("near")
    feed_forward(0, {2: lambda: [gat.step3() for gat in gat_down]})
    red_down.add_core("near")
    red_up.add_core("near")
    gat_up[1].step3()
    for gat in ff_weights:
        gat.ready(3)
    feed_forward(3, {})
    red_down.send_core("far")
    red_up.send_core("far")
    feed_forward(2, {})
    for gat in ff_weights:
        gat.finish()
    pl.semaphore_signal(free, inc=1, device_id=where["c"], device_id_type=MESH)
    red_down.add_core("far")

    def finish_block(s):
        lanes = slice(s * SLAB, (s + 1) * SLAB)
        for b in range(2):
            rows = slice(b * SLAB, (b + 1) * SLAB)
            total = None
            for i in range(4):
                _, _, ti = peer(i)
                part = dot_nn(act[i, rows, :], wdown[span(ti * WIDTH, WIDTH), lanes])
                total = part if i == 0 else total + part
            tokens[rows, lanes] = (mid[rows, lanes] + total).astype(BF16)

    def norm_back(grad, hat, rstd, gain):
        e = grad * gain
        mean_e = jnp.mean(e, axis=-1, keepdims=True)
        mean_eh = jnp.mean(e * hat, axis=-1, keepdims=True)
        return rstd * (e - mean_e - hat * mean_eh)

    def column_sum(values):
        return jnp.sum(values, axis=0, keepdims=True)

    gain_sum = jnp.zeros((1, WIDTH), F32)
    bias_sum = jnp.zeros((1, WIDTH), F32)
    for b in range(4):
        at = slice(b * 128, (b + 1) * 128)
        grad = acc_b[at, :]
        hat, rstd = normalize(mid[at, :])
        total = cot[at, :].astype(F32) + norm_back(grad, hat, rstd, gain1)
        gain_sum = gain_sum + column_sum(grad * hat)
        bias_sum = bias_sum + column_sum(grad)
        acc_b[at, :] = total
        mid_low[at, :] = total.astype(BF16)
    red_up.add_core("far")
    norm_sum[...] = jnp.zeros((8, WIDTH), F32)
    norm_sum[1:2, :] = gain_sum
    norm_sum[3:4, :] = bias_sum

    for i in range(4):
        _, _, ti = peer(i)
        hid_grad[:, i * PART : (i + 1) * PART] = dot_nt(
            mid_low[...], wout[span(ti * PART, PART), :]
        ).astype(BF16)

    def grads_of(i, j, rows):
        lanes = slice(j * HEAD_DIM, (j + 1) * HEAD_DIM)
        grad = hid_grad[rows, i * PART + j * HEAD_DIM : i * PART + (j + 1) * HEAD_DIM]
        inner = jnp.sum(grad.astype(F32) * att[i, rows, lanes].astype(F32), axis=-1, keepdims=True)
        high, middle, low = pieces(-inner)
        both = jnp.concatenate([grad, grad], axis=1)
        head_lanes = jnp.where(
            lane == 0,
            high,
            jnp.where(lane == 1, middle, jnp.where(lane == 2, low, jnp.zeros_like(both))),
        )
        return jnp.where(low_lane, head_lanes, both)

    def projection_grads(j, groups):
        def lanes_of(first):
            return [att[i, :, first : first + HEAD_DIM] for i in groups]

        query = jnp.concatenate(lanes_of(PART + j * HEAD_DIM), axis=1)
        mixed = jnp.concatenate(lanes_of(j * HEAD_DIM), axis=1)
        both = jnp.concatenate([dkvs[i, :, j * 128 : (j + 1) * 128] for i in groups], axis=1)
        for b in range(2):
            lanes = slice(b * 384, (b + 1) * 384)
            qs_grad = dot_tn(normed[own_rows, lanes], query)
            out_grad = dot_tn(mid_low[:, lanes], mixed)
            kv = dot_tn(normed[:, lanes], both)
            for n, i in enumerate(groups):
                pair = slice(n // 2 * 128, n // 2 * 128 + 128)
                q, o = qs_grad[:, pair], out_grad[:, pair]
                if n % 2 == 0:
                    qo = jnp.where(low_lane, q, pltpu.roll(o, HEAD_DIM, 1))
                else:
                    qo = jnp.where(low_lane, pltpu.roll(q, HEAD_DIM, 1), o)
                xi, _, _ = peer(i)
                value = jnp.concatenate([qo, kv[:, n * 128 : (n + 1) * 128]], axis=1)
                red_io[j].put(value, 4 * b, xi, i % 2)

    def far(j):
        projection_grads(j, (3, 2))
        red_io[j].send_core("far")

    def near(j):
        projection_grads(j, (1, 0))
        red_io[j].send_core("near")

    def both_sides(j):
        if j == 0:
            red_down.finish_core()
            red_up.finish_core()
            pl.semaphore_wait(free, 1)
        projection_grads(j, (3, 2, 1, 0))
        red_io[j].send_core("far")
        red_io[j].send_core("near")

    def add_both(j):
        red_io[j].add_core("far")
        red_io[j].add_core("near")

    def step(red, *what):
        for third, stage in what:
            red.step(third, stage)

    plan = {
        4: [lambda: step(red_down, (1, 1), (2, 1))],
        8: [lambda: step(red_down, (0, 1))],
        9: [lambda: both_sides(0)],
        10: [lambda: step(red_up, (1, 1), (2, 1))],
        11: [lambda: add_both(0)],
        13: [lambda: step(red_down, (1, 2), (0, 2))],
        15: [lambda: step(red_up, (0, 1))],
        16: [lambda: step(red_up, (1, 2))],
        17: [lambda: both_sides(1)],
        18: [lambda: step(red_down, (2, 2))],
        19: [lambda: add_both(1)],
        20: [lambda: step(red_up, (0, 2)), lambda: step(red_down, (0, 3))],
        21: [lambda: far(2)],
        22: [lambda: step(red_up, (2, 2)), lambda: step(red_down, (1, 3))],
        23: [lambda: red_io[2].add_core("far"), lambda: step(red_io[0], (1, 1), (2, 1))],
        25: [lambda: near(2), lambda: step(red_down, (2, 3))],
    }
    items = [(i, j, b) for j in range(3) for i in (3, 2, 1, 0) for b in range(2)]
    raw, ready, sums = {}, {}, None
    for n in range(len(items) + 2):
        if n < len(items):
            i, j, b = items[n]
            head, rows = 3 * i + j, slice(b * SLAB, (b + 1) * SLAB)
            both = grads_of(i, j, rows)
            raw[n] = dot_nt(qs[head, rows, :], keys_of(head)), dot_nt(both, values_of(head)), both
        if n >= 2:
            i, j, b = items[n - 2]
            head, rows = 3 * i + j, slice(b * SLAB, (b + 1) * SLAB)
            probs, score_grads, both = ready.pop(n - 2)
            att[i, rows, PART + j * HEAD_DIM : PART + (j + 1) * HEAD_DIM] = (
                dot_nn(score_grads, keys_of(head))[:, :HEAD_DIM] * HEAD_DIM ** (-0.5)
            ).astype(BF16)
            key_part = dot_tn(score_grads, qs[head, rows, :])
            value_part = dot_tn(probs, both)
            if b == 0:
                sums = key_part, value_part
            else:
                dkvs[i, :, j * 128 : (j + 1) * 128] = jnp.where(
                    low_lane, (sums[0] + key_part) * LN2, sums[1] + value_part
                ).astype(BF16)
        if 1 <= n <= len(items):
            score, prob_grad, both = raw.pop(n - 1)
            probs = jnp.exp2(score)
            ready[n - 1] = probs.astype(BF16), (probs * prob_grad).astype(BF16), both
        for event in plan.get(n, ()):
            event()

    def key_value_weights(ti, lanes):
        parts = []
        for j in range(3):
            rows = pl.ds(pl.multiple_of(ti * PART + j * HEAD_DIM, HEAD_DIM), HEAD_DIM)
            parts += [win[1, rows, lanes], win[2, rows, lanes]]
        return jnp.concatenate(parts, axis=0)

    def share_rows(n):
        lanes = slice(n * SLAB, (n + 1) * SLAB)
        total = None
        for i in range(4):
            _, _, ti = peer(i)
            part = dot_nn(dkvs[i, other_rows, :], key_value_weights(ti, lanes))
            total = part if i == 0 else total + part
        mid_low[:, lanes] = total.astype(BF16)

    share_rows(0)
    step(red_io[0], (0, 1))
    step(red_up, (0, 3), (1, 3))
    share_rows(1)
    red_io[2].add_core("near")
    share_rows(2)
    dn_copy = m.remote(mid_low, cot, core_sent, m.slot(), "c")
    step(red_io[1], (1, 1), (2, 1), (0, 1))
    step(red_io[0], (1, 2), (0, 2))

    sums = [jnp.zeros((1, WIDTH), F32), jnp.zeros((1, WIDTH), F32)]

    def finish_rows(b):
        at = slice(b * SLAB, (b + 1) * SLAB)
        rows = pl.ds(pl.multiple_of(c * ROWS + b * SLAB, SLAB), SLAB)
        grad = None
        for i in range(4):
            _, _, ti = peer(i)
            part = span(ti * PART, PART)
            total = dot_nn(att[i, at, PART:], win[0, part, :]) + dot_nn(
                dkvs[i, rows, :], key_value_weights(ti, slice(None))
            )
            grad = total if i == 0 else grad + total
        grad = grad + cot[at, :].astype(F32)
        hat, rstd = normalize(tokens[at, :].astype(F32))
        hid_grad[at, :] = (acc_b[at, :] + norm_back(grad, hat, rstd, gain0)).astype(BF16)
        sums[0] = sums[0] + column_sum(grad * hat)
        sums[1] = sums[1] + column_sum(grad)

    dn_copy.wait_recv()
    finish_rows(0)
    step(red_io[2], (1, 1), (2, 1))
    step(red_up, (2, 3))
    step(red_io[0], (2, 2))
    step(red_io[1], (1, 2), (0, 2))
    finish_rows(1)
    norm_sum[0:1, :] = sums[0]
    norm_sum[2:3, :] = sums[1]
    share_sent = m.slot()
    rounds = (
        (0, 4, t, ("c", "x", "xc"), m.slot()),
        (4, 2, y, ("y",), m.slot()),
        (6, 4, 2 * h + l, ("l", "h", "lh"), m.slot()),
    )

    def share(n):
        if n > 0:
            first, size, _, peers, slot = rounds[n - 1]
            m.wait(slot, norm_box.at[pl.ds(0, len(peers))])
            total = norm_box[first]
            for k in range(1, size):
                total = total + norm_box[first + k]
            norm_sum[...] = total
        if n < 3:
            first, _, mine, peers, slot = rounds[n]
            norm_box[first + mine] = norm_sum[...]
            for to in peers:
                m.remote(norm_box.at[first + mine], norm_box.at[first + mine], share_sent, slot, to)

    share(0)
    stores = [m.local(hid_grad, input_grad)]
    step(red_io[2], (0, 1))
    step(red_io[1], (2, 2))
    red_down.last()
    down_store = m.local(res_ff, grad_down)
    step(red_io[0], (0, 3), (1, 3), (2, 3))
    finish_block(0)
    share(1)
    step(red_io[2], (1, 2), (0, 2))
    finish_block(1)
    step(red_io[1], (0, 3), (1, 3))
    step(red_io[2], (2, 2))
    step(red_io[1], (2, 3))
    down_store.wait()
    red_up.last()
    stores.append(m.local(res_ff, grad_up))
    share(2)
    finish_block(2)
    stores.append(m.local(tokens, block_out))
    step(red_io[2], (0, 3), (1, 3), (2, 3))
    for j in range(3):
        red_io[j].last()
        lanes = slice(j * HEAD_DIM, (j + 1) * HEAD_DIM)
        block = res_io[...]
        for k, part in enumerate((0, 2, 3)):
            res_in[k, :, lanes] = block[:, part * HEAD_DIM : (part + 1) * HEAD_DIM]
        res_out[:, lanes] = block[:, HEAD_DIM : 2 * HEAD_DIM]
        if j == 1:
            share(3)
            stores.append(m.local(norm_sum, grad_norm))
    stores.append(m.local(res_in, grad_in))
    stores.append(m.local(res_out, grad_out))
    gat_out.finish()
    for gat in gat_in:
        gat.finish()
    for red in red_io:
        red.finish_core()
    for red in (red_down, red_up, *red_io):
        red.finish()
    m.wait(share_sent, norm_box.at[pl.ds(0, 7)])
    m.wait(core_sent, normed)
    for store in stores:
        store.wait()


def write_results(*refs):
    sources, targets, stages = refs[:7], refs[7:15], refs[15:22]
    out, gains, biases, sems = refs[22], refs[23], refs[24], refs[25]
    loads = [pltpu.make_async_copy(a, b, sems.at[k]) for k, (a, b) in enumerate(zip(sources, stages))]
    for copy in loads:
        copy.start()
    loads[5].wait()
    out[...] = stages[5][...].T
    loads[6].wait()
    gains[...] = stages[6][0:2, :]
    biases[...] = stages[6][2:4, :]
    done = [*stages[:5], out, gains, biases]
    stores = [pltpu.make_async_copy(a, b, sems.at[7 + k]) for k, (a, b) in enumerate(zip(done, targets))]
    for k in (5, 6, 7):
        stores[k].start()
    for k in range(5):
        loads[k].wait()
        stores[k].start()
    for copy in stores:
        copy.wait()


def fused(tokens, gene_counts, in_proj, out_proj, up_proj, down_proj, gains, biases, cotangent):
    vmem = pl.BlockSpec(memory_space=pltpu.VMEM)
    hbm = pl.BlockSpec(memory_space=pl.ANY)
    shape = jax.ShapeDtypeStruct
    outs = pl.pallas_call(
        kernel,
        out_shape=(
            shape((ROWS, WIDTH), BF16),
            shape((ROWS, WIDTH), BF16),
            shape((3, CHUNK, PART), F32),
            shape((CHUNK, WIDTH), F32),
            shape((CHUNK, WIDTH), F32),
            shape((CHUNK, PART), F32),
            shape((8, WIDTH), F32),
        ),
        in_specs=[pl.BlockSpec(memory_space=pltpu.SMEM)] + [hbm] * 6 + [vmem] * 2,
        out_specs=[hbm] * 7,
        scratch_shapes=[
            pltpu.VMEM((ROWS, WIDTH), BF16),
            pltpu.VMEM((2 * ROWS, WIDTH), BF16),
            pltpu.VMEM((ROWS, WIDTH), BF16),
            pltpu.VMEM((3, WIDTH, WIDTH), BF16),
            pltpu.VMEM((WIDTH, WIDTH), BF16),
            pltpu.VMEM((4 * WIDTH, WIDTH), BF16),
            pltpu.VMEM((4 * WIDTH, WIDTH), BF16),
            pltpu.VMEM((12, ROWS, 2 * HEAD_DIM), BF16),
            pltpu.VMEM((12, 2 * ROWS, 2 * HEAD_DIM), BF16),
            pltpu.VMEM((2 * ROWS, 2 * HEAD_DIM), BF16),
            pltpu.VMEM((4, ROWS, 2 * PART), BF16),
            pltpu.VMEM((ROWS, WIDTH), F32),
            pltpu.VMEM((ROWS, WIDTH), BF16),
            pltpu.VMEM((4, ROWS, WIDTH), BF16),
            pltpu.VMEM((ROWS, WIDTH), BF16),
            pltpu.VMEM((ROWS, WIDTH), F32),
            pltpu.VMEM((4, 2 * ROWS, 2 * PART), BF16),
            pltpu.VMEM((4 * WIDTH, WIDTH), BF16),
            pltpu.VMEM((4 * WIDTH, WIDTH), BF16),
            pltpu.VMEM((31 * CHUNK, WIDTH), BF16),
            pltpu.VMEM((31 * CHUNK, WIDTH), BF16),
            pltpu.VMEM((CHUNK, SLAB), F32),
            pltpu.VMEM((CHUNK, WIDTH), F32),
            pltpu.VMEM((3, CHUNK, PART), F32),
            pltpu.VMEM((CHUNK, PART), F32),
            pltpu.VMEM((10, 8, WIDTH), F32),
            pltpu.VMEM((8, WIDTH), F32),
            pltpu.SemaphoreType.REGULAR,
            pltpu.SemaphoreType.DMA((SEMAPHORES,)),
        ],
        compiler_params=pltpu.CompilerParams(
            collective_id=0, has_side_effects=True, vmem_limit_bytes=64 * 2**20
        ),
    )(
        gene_counts,
        tokens,
        cotangent,
        jnp.swapaxes(in_proj, 1, 2),
        out_proj,
        up_proj,
        down_proj,
        gains,
        biases,
    )
    results = pl.pallas_call(
        write_results,
        out_shape=(
            *(shape(o.shape, o.dtype) for o in outs[:5]),
            shape((PART, CHUNK), F32),
            shape((2, WIDTH), F32),
            shape((2, WIDTH), F32),
        ),
        in_specs=[hbm] * 7,
        out_specs=[hbm] * 8,
        scratch_shapes=[
            *(pltpu.VMEM(o.shape, o.dtype) for o in outs),
            pltpu.VMEM((PART, CHUNK), F32),
            pltpu.VMEM((2, WIDTH), F32),
            pltpu.VMEM((2, WIDTH), F32),
            pltpu.SemaphoreType.DMA((15,)),
        ],
    )(*outs)
    block_out, input_grad, grad_in, grad_up, grad_down, grad_out, grad_gains, grad_biases = results
    return (
        block_out,
        input_grad,
        grad_in,
        grad_out,
        grad_up,
        grad_down.T,
        grad_gains,
        grad_biases,
    )


def layer_norm(values, gain, offset):
    center = values - jnp.mean(values, axis=-1, keepdims=True)
    spread = jnp.mean(center * center, axis=-1, keepdims=True)
    return center * lax.rsqrt(spread + EPS) * gain + offset


def gelu_exact(values):
    return jax.nn.gelu(values, approximate=False)


def per_device(
    tokens, gene_counts, in_proj, out_proj, up_proj, down_proj, gains, biases, cotangent
):
    rows = tokens.shape[0]
    cells = gene_counts.shape[0]
    group = rows * lax.axis_size("tensor")
    length = group // cells
    local_width = out_proj.shape[0]
    heads = local_width // HEAD_DIM
    block = min(length, 512)
    blocks = length // block
    scale = HEAD_DIM ** (-0.5)
    positions = jnp.arange(length, dtype=jnp.int32)
    resid = tokens.astype(jnp.float32)
    normed, first_back = jax.vjp(layer_norm, resid, gains[0], biases[0])
    normed_all = lax.all_gather(normed.astype(jnp.bfloat16), "tensor", axis=0, tiled=True)
    projected = jnp.einsum(
        "td,cde->cte", normed_all, in_proj, preferred_element_type=jnp.float32
    ).astype(jnp.bfloat16)
    query_cells = projected[0].reshape(cells, blocks, block, local_width)
    key_cells = projected[1].reshape(cells, length, local_width)
    value_cells = projected[2].reshape(cells, length, local_width)

    def block_scores(query_block, key_rows, count):
        query_heads = query_block.reshape(block, heads, HEAD_DIM)
        key_heads = key_rows.reshape(length, heads, HEAD_DIM)
        scores = (
            jnp.einsum("qhd,khd->hqk", query_heads, key_heads, preferred_element_type=jnp.float32)
            * scale
        )
        return jnp.where((positions < count)[None, None, :], scores, NEG)

    def cell_forward(item):
        queries, key_rows, value_rows, count = item
        value_heads = value_rows.reshape(length, heads, HEAD_DIM)

        def one_block(query_block):
            scores = block_scores(query_block, key_rows, count)
            top = jnp.max(scores, axis=-1, keepdims=True)
            expo = jnp.exp(scores - top)
            total = jnp.sum(expo, axis=-1, keepdims=True)
            probs = (expo / total).astype(jnp.bfloat16)
            result = jnp.einsum(
                "hqk,khd->qhd", probs, value_heads, preferred_element_type=jnp.float32
            )
            return (
                result.reshape(block, local_width).astype(jnp.bfloat16),
                (top + jnp.log(total))[..., 0],
            )

        return lax.map(one_block, queries)

    attended, log_totals = lax.map(cell_forward, (query_cells, key_cells, value_cells, gene_counts))
    attended = attended.reshape(group, local_width)
    piece = attended
    mid = resid + lax.psum_scatter(
        jnp.dot(piece, out_proj, preferred_element_type=jnp.float32),
        "tensor",
        scatter_dimension=0,
        tiled=True,
    )
    normed_mid, second_back = jax.vjp(layer_norm, mid, gains[1], biases[1])
    mid_low = normed_mid.astype(jnp.bfloat16)
    mid_all = lax.all_gather(mid_low, "tensor", axis=0, tiled=True)
    hidden = jnp.dot(mid_all, up_proj, preferred_element_type=jnp.float32)
    active = gelu_exact(hidden).astype(jnp.bfloat16)
    piece = active
    block_out = (
        mid
        + lax.psum_scatter(
            jnp.dot(piece, down_proj, preferred_element_type=jnp.float32).astype(jnp.bfloat16),
            "tensor",
            scatter_dimension=0,
            tiled=True,
        ).astype(jnp.float32)
    ).astype(jnp.bfloat16)
    out_grads = lax.all_gather(cotangent, "tensor", axis=0, tiled=True)
    _, gelu_back = jax.vjp(gelu_exact, hidden)
    active_grad = jnp.einsum("td,fd->tf", out_grads, down_proj, preferred_element_type=jnp.float32)
    hidden_grad = gelu_back(active_grad)[0].astype(jnp.bfloat16)
    grad_down = jnp.einsum("tf,td->fd", active, out_grads, preferred_element_type=jnp.float32)
    grad_up = jnp.einsum("td,tf->df", mid_all, hidden_grad, preferred_element_type=jnp.float32)
    piece = hidden_grad
    mid_grad = lax.psum_scatter(
        jnp.einsum("tf,df->td", piece, up_proj, preferred_element_type=jnp.float32),
        "tensor",
        scatter_dimension=0,
        tiled=True,
    )
    resid_part, gain_second, bias_second = second_back(mid_grad)
    mid_total = cotangent.astype(jnp.float32) + resid_part
    branch_all = lax.all_gather(mid_total.astype(jnp.bfloat16), "tensor", axis=0, tiled=True)
    attended_grad = jnp.einsum(
        "td,ed->te", branch_all, out_proj, preferred_element_type=jnp.float32
    ).astype(jnp.bfloat16)
    grad_out = jnp.einsum("te,td->ed", attended, branch_all, preferred_element_type=jnp.float32)

    def cell_backward(item):
        queries, key_rows, value_rows, count, grad_rows, totals = item
        key_heads = key_rows.reshape(length, heads, HEAD_DIM)
        value_heads = value_rows.reshape(length, heads, HEAD_DIM)

        def one_block(carry, part):
            key_sum, value_sum = carry
            query_block, grad_block, total_block = part
            scores = block_scores(query_block, key_rows, count)
            probs = jnp.exp(scores - total_block[..., None])
            grad_heads = grad_block.reshape(block, heads, HEAD_DIM)
            query_heads = query_block.reshape(block, heads, HEAD_DIM)
            prob_grads = jnp.einsum(
                "qhd,khd->hqk", grad_heads, value_heads, preferred_element_type=jnp.float32
            )
            inner = jnp.sum(probs * prob_grads, axis=-1, keepdims=True)
            score_grads = (probs * (prob_grads - inner)).astype(jnp.bfloat16)
            query_grad = (
                jnp.einsum(
                    "hqk,khd->qhd", score_grads, key_heads, preferred_element_type=jnp.float32
                )
                * scale
            )
            key_sum = (
                key_sum
                + jnp.einsum(
                    "hqk,qhd->khd", score_grads, query_heads, preferred_element_type=jnp.float32
                )
                * scale
            )
            value_sum = value_sum + jnp.einsum(
                "hqk,qhd->khd",
                probs.astype(jnp.bfloat16),
                grad_heads,
                preferred_element_type=jnp.float32,
            )
            return (
                (key_sum, value_sum),
                query_grad.reshape(block, local_width).astype(jnp.bfloat16),
            )

        zeros = jnp.zeros((length, heads, HEAD_DIM), jnp.float32)
        (key_sum, value_sum), query_grads = lax.scan(
            one_block, (zeros, zeros), (queries, grad_rows, totals)
        )
        return (
            query_grads.reshape(length, local_width),
            key_sum.reshape(length, local_width).astype(jnp.bfloat16),
            value_sum.reshape(length, local_width).astype(jnp.bfloat16),
        )

    grad_cells = attended_grad.reshape(cells, blocks, block, local_width)
    query_grads, key_grads, value_grads = lax.map(
        cell_backward, (query_cells, key_cells, value_cells, gene_counts, grad_cells, log_totals)
    )
    proj_grads = jnp.stack(
        [
            query_grads.reshape(group, local_width),
            key_grads.reshape(group, local_width),
            value_grads.reshape(group, local_width),
        ]
    )
    grad_in = jnp.einsum("td,cte->cde", normed_all, proj_grads, preferred_element_type=jnp.float32)
    piece = proj_grads
    normed_grad = lax.psum_scatter(
        jnp.einsum("cte,cde->td", piece, in_proj, preferred_element_type=jnp.float32),
        "tensor",
        scatter_dimension=0,
        tiled=True,
    )
    resid_grad, gain_first, bias_first = first_back(normed_grad)
    input_grad = (mid_total + resid_grad).astype(jnp.bfloat16)
    grad_gains, grad_biases = lax.psum(
        (jnp.stack([gain_first, gain_second]), jnp.stack([bias_first, bias_second])),
        ("dp", "tensor"),
    )
    grad_in_part, grad_out_part, grad_up_part, grad_down_part = (
        lax.psum_scatter(grad_in, "dp", scatter_dimension=1, tiled=True),
        lax.psum_scatter(grad_out, "dp", scatter_dimension=1, tiled=True),
        lax.psum_scatter(grad_up, "dp", scatter_dimension=0, tiled=True),
        lax.psum_scatter(grad_down, "dp", scatter_dimension=1, tiled=True),
    )
    return (
        block_out,
        input_grad,
        grad_in_part,
        grad_out_part,
        grad_up_part,
        grad_down_part,
        grad_gains,
        grad_biases,
    )


def solution(mesh):
    placed = (
        P(("dp", "tensor"), None),
        P("dp"),
        P(None, None, "tensor"),
        P("tensor", None),
        P(None, "tensor"),
        P("tensor", None),
        P(),
        P(),
        P(("dp", "tensor"), None),
    )
    halves = mesh.shape["dp"] == 8 and mesh.shape["tensor"] == 4
    return jax.shard_map(
        fused if halves else per_device,
        mesh=mesh,
        in_specs=placed,
        out_specs=(
            P(("dp", "tensor"), None),
            P(("dp", "tensor"), None),
            P(None, "dp", "tensor"),
            P("tensor", "dp"),
            P("dp", "tensor"),
            P("tensor", "dp"),
            P(),
            P(),
        ),
        check_vma=False,
    )
```

```python
import itertools
import math

import jax
import jax.numpy as jnp
from jax import lax
from jax.experimental import pallas as pl
from jax.experimental.pallas import tpu as pltpu
from jax.sharding import PartitionSpec as P

HEAD_DIM = 64
EPS = 1e-05
NEG = -1e30
F32 = jnp.float32
BF16 = jnp.bfloat16
MESH = pl.DeviceIdType.MESH
LOG2E = math.log2(math.e)
LN2 = math.log(2.0)
ROWS = 512
WIDTH = 768
PART = 192
CHUNK = 96
SLAB = 256
THIRD = 32
ORDERS = ("xylh", "ylxh", "lxyh")
WEIGHT = {"x": 8, "y": 4, "l": 2, "h": 1}
BOX = (0, 16, 24, 28, 30)
SEMAPHORES = 146


def dot_nn(left, right):
    return lax.dot_general(left, right, (((1,), (0,)), ((), ())), preferred_element_type=F32)


def dot_nt(left, right):
    return lax.dot_general(left, right, (((1,), (1,)), ((), ())), preferred_element_type=F32)


def dot_tn(left, right):
    return lax.dot_general(left, right, (((0,), (0,)), ((), ())), preferred_element_type=F32)


def span(start, size):
    return pl.ds(pl.multiple_of(start, size), size)


def normalize(values):
    center = values - jnp.mean(values, axis=-1, keepdims=True)
    spread = jnp.mean(center * center, axis=-1, keepdims=True)
    rstd = lax.rsqrt(spread + EPS)
    return center * rstd, rstd


def pieces(values):
    high = values.astype(BF16)
    rest = values - high.astype(F32)
    middle = rest.astype(BF16)
    low = (rest - middle.astype(F32)).astype(BF16)
    return high, middle, low


class Mover:
    def __init__(self, where, sems):
        self.where, self.sems, self.count = where, sems, 0

    def slot(self):
        self.count += 1
        assert self.count <= SEMAPHORES
        return self.count - 1

    def remote(self, source, target, sent, arrived, to):
        copy = pltpu.make_async_remote_copy(
            src_ref=source,
            dst_ref=target,
            send_sem=self.sems.at[sent],
            recv_sem=self.sems.at[arrived],
            device_id=self.where[to],
            device_id_type=MESH,
        )
        copy.start()
        return copy

    def local(self, source, target):
        copy = pltpu.make_async_copy(source, target, self.sems.at[self.slot()])
        copy.start()
        return copy

    def wait(self, slot, like):
        pltpu.make_async_copy(like, like, self.sems.at[slot]).wait()


class Gather:
    def __init__(self, mover, place, shard, full, view, halves):
        self.m, self.p, self.shard, self.full, self.view = mover, place, shard, full, view
        self.halves = halves
        forward = ("yf", "zf") if halves else ("x1",)
        self.slots = {k: mover.slot() for k in ("x0", "y", "z", "own", "core", *forward)}
        self.sent = mover.slot()
        self.copies = {}
        self.quarter = {k: place[k] for k in ("q", "qy", "qz", "qd")}

    def go(self, key, source, target, to):
        arrived = self.slots["core" if key[0] == "c" else key]
        self.copies[key] = self.m.remote(source, target, self.sent, arrived, to)

    def start_own(self):
        p = self.p
        mine = self.view(self.full, p["t"], 0, 4)
        self.load = self.m.local(self.view(self.shard, None, 0, 4), mine)
        self.go("own", self.view(self.shard, None, 0, 4), mine, "c")

    def start_x(self, key="x0", quarter="q"):
        p = self.p
        self.go(key, self.view(self.shard, None, p[quarter], 1), self.view(self.full, p["t"], p[quarter], 1), "x")

    def start_x1(self):
        self.start_x("x1", "qd")

    def pass_on(self, key, quarter, to, half=None):
        part = self.view(self.full, self.p["t2"], self.quarter[quarter], 1, half)
        self.go(key, part, part, to)

    def step1(self):
        self.copies["x0"].wait_recv()
        self.pass_on("y", "q", "y")
        self.pass_on("z", "q", "l")
        self.pass_on("c0", "q", "c")

    def step2(self):
        self.copies["y"].wait_recv()
        if self.halves:
            self.pass_on("zf", "qy", "l", 0)
        self.pass_on("c1", "qy", "c")
        self.copies["z"].wait_recv()
        if self.halves:
            self.pass_on("yf", "qz", "y", 1)
        self.pass_on("c2", "qz", "c")

    def step3(self):
        if self.halves:
            self.copies["zf"].wait_recv()
            self.copies["yf"].wait_recv()
        else:
            self.copies["x1"].wait_recv()
        self.pass_on("c3", "qd", "c")

    def finish(self):
        self.m.wait(self.sent, self.view(self.full, 0, 0, 12))

    def ready(self, i):
        if i == 0:
            self.load.wait()
        if i == 1:
            self.copies["own"].wait_recv()
        if i == 3:
            self.m.wait(self.slots["core"], self.view(self.full, self.p["t"], 0, 4))


class Reduce:
    def __init__(self, mover, place, own, away, inbox, result):
        self.m, self.p, self.own, self.away = mover, place, own, away
        self.inbox, self.result = inbox, result
        self.slots = {key: mover.slot() for key in ("near", "far", "last")}
        self.slots |= {(third, stage): mover.slot() for third in range(3) for stage in (1, 2, 3)}
        self.sent, self.core_sent = mover.slot(), mover.slot()

    def at(self, place, third, chunk, count):
        ref, half = place
        start = third * 32 * THIRD + half * 16 * THIRD + chunk * THIRD
        return ref.at[pl.ds(pl.multiple_of(start, THIRD), count * THIRD), :]

    def box(self, third, at, count):
        return pl.ds((third * 31 + at) * THIRD, count * THIRD)

    def put(self, value, first, x, away):
        for k in range(value.shape[0] // CHUNK):
            r = first + k
            chunk = 8 * x + 4 * (r % 2) + 2 * ((r // 2) % 2) + r // 4
            for third in range(3):
                start = k * CHUNK + third * THIRD
                target = self.at(self.away if away else self.own, third, chunk, 1)
                target[...] = value[start : start + THIRD, :].astype(BF16)

    def go(self, slot, third, source, at, count, to):
        self.m.remote(
            source,
            self.inbox.at[self.box(third, at, count), :],
            self.core_sent if to == "c" else self.sent,
            self.slots[slot],
            to,
        )

    def arrived(self, slot, count):
        self.m.wait(self.slots[slot], self.inbox.at[pl.ds(0, count * THIRD), :])

    def finish_core(self):
        self.m.wait(self.core_sent, self.inbox.at[pl.ds(0, 48 * THIRD), :])

    def finish(self):
        self.m.wait(self.sent, self.inbox.at[pl.ds(0, 45 * THIRD), :])

    def halves(self, side):
        return (self.p["x"], 0) if side == "near" else (1 - self.p["x"], 8)

    def send_core(self, side):
        x, at = self.halves(side)
        for third in range(3):
            self.go(side, third, self.at(self.away, third, 8 * x, 8), at, 8, "c")

    def add(self, third, chunk, count, at):
        here = self.at(self.own, third, chunk, count)
        here[...] = here[...] + self.inbox[self.box(third, at, count), :]

    def add_core(self, side):
        x, at = self.halves(side)
        self.arrived(side, 24)
        for third in range(3):
            self.add(third, 8 * x, 8, at)
            self.send(third, 1, side)

    def runs(self, third, stage):
        order = ORDERS[third]
        dim, fixed = order[stage - 1], order[: stage - 1]
        rest, count = list("xylh"), 1
        while rest and rest[-1] != dim and rest[-1] not in fixed:
            rest.pop()
            count *= 2
        free = [name for name in rest if name != dim and name not in fixed]
        found = []
        for values in itertools.product((0, 1), repeat=len(free)):
            flip = dict(zip(free, values))
            base = 0
            for name in rest:
                if name != dim:
                    own = self.p[name]
                    base = base + WEIGHT[name] * (1 - own if flip.get(name) else own)
            own = WEIGHT[dim] * self.p[dim]
            side = "far" if flip.get("x", dim == "x") else "near"
            found.append((base + own, base + WEIGHT[dim] - own, count, BOX[stage] + len(found) * count, side))
        return found

    def send(self, third, stage, side=None):
        slot = (third, stage) if stage < 4 else "last"
        for _, away, count, at, where in self.runs(third, stage):
            if side in (None, where):
                source = self.at(self.own, third, away, count)
                self.go(slot, third, source, at, count, ORDERS[third][stage - 1])

    def step(self, third, stage):
        self.arrived((third, stage), 16 >> stage)
        for keep, _, count, at, _ in self.runs(third, stage):
            self.add(third, keep, count, at)
        self.send(third, stage + 1)

    def last(self):
        self.arrived("last", 3)
        for third in range(3):
            ((keep, _, _, at, _),) = self.runs(third, 4)
            total = self.at(self.own, third, keep, 1)[...].astype(F32) + self.inbox[
                self.box(third, at, 1), :
            ].astype(F32)
            self.result[third * THIRD : (third + 1) * THIRD, :] = total


def kernel(
    counts,
    tokens_in,
    cot_in,
    win_in,
    wout_in,
    wup_in,
    wdown_in,
    gains,
    biases,
    block_out,
    input_grad,
    grad_in,
    grad_up,
    grad_down,
    grad_out,
    grad_norm,
    tokens,
    normed,
    cot,
    win,
    wout,
    wup,
    wdown,
    qs,
    kvs,
    key_tail,
    att,
    mid,
    mid_low,
    stage,
    act,
    hid_grad,
    acc_b,
    acc_c,
    dkvs,
    g_down,
    g_up,
    in_down,
    in_up,
    res_io,
    res_ff,
    res_in,
    res_out,
    norm_box,
    norm_sum,
    free,
    sems,
):
    d = lax.axis_index("dp")
    t = lax.axis_index("tensor")
    x = lax.div(t, 2)
    c = t - 2 * x
    y = lax.rem(d, 2)
    l = lax.rem(lax.div(d, 2), 2)
    h = lax.div(d, 4)
    where = {
        "c": (d, t + 1 - 2 * c),
        "x": (d, t + 2 - 4 * x),
        "y": (d + 1 - 2 * y, t),
        "l": (d + 2 - 4 * l, t),
        "h": (d + 4 - 8 * h, t),
        "xc": (d, 3 - t),
        "lh": (d + 2 - 4 * l + 4 - 8 * h, t),
    }
    place = {"x": x, "c": c, "y": y, "l": l, "h": h, "t": t, "t2": t + 2 - 4 * x}
    place["q"] = 2 * l + y
    place["qy"] = 2 * l + 1 - y
    place["qz"] = 2 * (1 - l) + y
    place["qd"] = 2 * (1 - l) + 1 - y
    m = Mover(where, sems)
    own_rows = span(c * ROWS, ROWS)
    other_rows = span((1 - c) * ROWS, ROWS)

    def view_in(lane):
        def view(ref, dev, first, parts, half=None):
            start, size = first * 48, parts * 48
            if half is not None:
                size = 32 if half == lane else 16
                start = start + (48 - size if half else 0)
            start = start if dev is None else dev * PART + start
            return ref.at[:, pl.ds(pl.multiple_of(start, 16), size), pl.ds(lane * 384, 384)]

        return view

    def view_out(ref, dev, first, parts, half=None):
        start = first * 48
        rows = pl.ds(pl.multiple_of(start if dev is None else dev * PART + start, 48), parts * 48)
        return ref.at[rows, :]

    def view_up(lane):
        def view(ref, dev, first, parts, half=None):
            start, size = first * PART, parts * PART
            if half is not None:
                start, size = start + half * CHUNK, CHUNK
            start = start if dev is None else dev * WIDTH + start
            return ref.at[pl.ds(pl.multiple_of(start, CHUNK), size), pl.ds(lane * 384, 384)]

        return view

    barrier = pltpu.get_barrier_semaphore()
    for to in where:
        pl.semaphore_signal(barrier, inc=1, device_id=where[to], device_id_type=MESH)
    tok_load = m.local(tokens_in, tokens)
    pl.semaphore_wait(barrier, len(where))
    gat_in = [Gather(m, place, win_in, win, view_in(k), True) for k in range(2)]
    gat_out = Gather(m, place, wout_in, wout, view_out, False)
    gat_up = [Gather(m, place, wup_in, wup, view_up(k), True) for k in range(2)]
    gat_down = [Gather(m, place, wdown_in, wdown, view_up(k), False) for k in range(2)]
    ff_weights = [*gat_up, *gat_down]
    for gat in gat_in:
        gat.start_x()
    core_sent = m.slot()
    tok_copy = m.remote(tokens_in, mid_low, core_sent, m.slot(), "c")
    for gat in gat_in:
        gat.start_own()
    gat_out.start_x()
    gat_out.start_x1()
    for gat in ff_weights:
        gat.start_x()
    for gat in gat_down:
        gat.start_x1()
    cot_load = m.local(cot_in, cot)
    for gat in (gat_out, *ff_weights):
        gat.start_own()

    gain0, bias0 = gains[0:1, :], biases[0:1, :]
    gain1, bias1 = gains[1:2, :], biases[1:2, :]

    def norm_rows(source, first):
        @pl.loop(0, ROWS // 64, unroll=2)
        def _(k):
            hat, _ = normalize(source[span(k * 64, 64), :].astype(F32))
            normed[span(first + k * 64, 64), :] = (hat * gain0 + bias0).astype(BF16)

    tok_load.wait()
    norm_rows(tokens, c * ROWS)
    tok_copy.wait_recv()
    norm_rows(mid_low, (1 - c) * ROWS)

    count = counts[x]
    lane = lax.broadcasted_iota(jnp.int32, (1, 2 * HEAD_DIM), 1)
    low_lane = lane < HEAD_DIM

    @pl.loop(0, 2 * ROWS // 128)
    def _(k):
        at = k * 128 + lax.broadcasted_iota(jnp.int32, (128, 2 * HEAD_DIM), 0)
        column = lax.broadcasted_iota(jnp.int32, (128, 2 * HEAD_DIM), 1)
        key_tail[span(k * 128, 128), :] = jnp.where(
            column == HEAD_DIM,
            jnp.where(at < count, 0.0, NEG),
            jnp.where(column < HEAD_DIM + 4, 1.0, 0.0),
        ).astype(BF16)

    value_tail = jnp.where(lane < 3, 1.0, 0.0).astype(BF16)
    query_tail = jnp.where(lane[:, :HEAD_DIM] == 0, 1.0, 0.0).astype(BF16)

    def keys_of(head):
        return jnp.where(low_lane, kvs[head], key_tail[...])

    def values_of(head):
        return jnp.where(low_lane, value_tail, kvs[head])

    def peer(i):
        xi = x if i < 2 else 1 - x
        ci = c if i % 2 == 0 else 1 - c
        return xi, ci, 2 * xi + ci

    def key_value_weights(ti, lanes):
        parts = []
        for j in range(3):
            rows = pl.ds(pl.multiple_of(ti * PART + j * HEAD_DIM, HEAD_DIM), HEAD_DIM)
            parts += [win[1, rows, lanes], win[2, rows, lanes]]
        return jnp.concatenate(parts, axis=0)

    def project(i):
        _, _, ti = peer(i)
        part = span(ti * PART, PART)
        q = dot_nt(normed[own_rows, :], win[0, part, :]) * (HEAD_DIM ** (-0.5) * LOG2E)
        q = q.astype(BF16)
        kv = dot_nt(normed[...], key_value_weights(ti, slice(None))).astype(BF16)
        for j in range(3):
            lanes = slice(j * HEAD_DIM, (j + 1) * HEAD_DIM)
            qs[3 * i + j] = jnp.concatenate(
                [q[:, lanes], jnp.broadcast_to(query_tail, (ROWS, HEAD_DIM))], axis=1
            )
            kvs[3 * i + j] = kv[:, j * 128 : (j + 1) * 128]

    items = [(i, j, b) for i in range(4) for j in range(3) for b in range(2)]
    hooks = {
        0: [lambda: gat_in[0].ready(0), lambda: gat_in[1].ready(0)],
        1: [gat_in[0].step1],
        3: [gat_in[1].step1],
        6: [lambda: gat_in[0].ready(1), lambda: gat_in[1].ready(1)],
        7: [gat_in[0].step2],
        9: [gat_in[1].step2, gat_out.step1],
        12: [gat_in[0].step3, gat_in[1].step3, gat_up[0].step1],
        13: [gat_out.step2, gat_out.step3],
        15: [gat_up[1].step1],
        18: [gat_up[0].step2, lambda: gat_in[0].ready(3), lambda: gat_in[1].ready(3)],
        19: [gat_down[0].step1],
        22: [gat_up[1].step2, gat_down[1].step1],
        25: [gat_up[0].step3],
    }
    scores, tops, expos, keys = {}, {}, {}, None
    for n in range(len(items) + 2):
        for hook in hooks.get(n, ()):
            hook()
        if n < len(items):
            i, j, b = items[n]
            if n % 6 == 0:
                project(i)
            if b == 0:
                keys = keys_of(3 * i + j)
            scores[n] = dot_nt(qs[3 * i + j, b * SLAB : (b + 1) * SLAB, :], keys)
        if n >= 2:
            i, j, b = items[n - 2]
            head, rows = 3 * i + j, slice(b * SLAB, (b + 1) * SLAB)
            mixed = dot_nn(expos.pop(n - 2), values_of(head))
            total = mixed[:, 0:1]
            att[i, rows, j * HEAD_DIM : (j + 1) * HEAD_DIM] = (mixed * (1.0 / total))[
                :, HEAD_DIM:
            ].astype(BF16)
            high, middle, low = pieces(-(tops.pop(n - 2) + jnp.log2(total)))
            qs[head, rows, :] = jnp.where(
                lane == HEAD_DIM + 1,
                high,
                jnp.where(
                    lane == HEAD_DIM + 2,
                    middle,
                    jnp.where(lane == HEAD_DIM + 3, low, qs[head, rows, :]),
                ),
            )
        if 1 <= n <= len(items):
            score = scores.pop(n - 1)
            tops[n - 1] = jnp.max(score, axis=-1, keepdims=True)
            expos[n - 1] = jnp.exp2(score - tops[n - 1]).astype(BF16)
    for i in (0, 1, 3):
        gat_out.ready(i)
    for b in range(2):
        at = slice(b * SLAB, (b + 1) * SLAB)
        total = tokens[at, :].astype(F32)
        for i in range(4):
            _, _, ti = peer(i)
            total = total + dot_nn(att[i, at, :PART], wout[span(ti * PART, PART), :])
        mid[at, :] = total
        hat, _ = normalize(total)
        mid_low[at, :] = (hat * gain1 + bias1).astype(BF16)
    cot_load.wait()

    red_down = Reduce(m, place, (g_down, c), (g_down, 1 - c), in_down, res_ff)
    red_up = Reduce(m, place, (g_up, c), (g_up, 1 - c), in_up, res_ff)
    red_io = []
    for j in range(3):
        lanes = slice(j * SLAB, (j + 1) * SLAB)
        red_io.append(
            Reduce(
                m, place, (g_down.at[:, lanes], 1 - c), (g_up.at[:, lanes], 1 - c), wup.at[:, lanes], res_io
            )
        )

    def feed_forward(i, hooks):
        xi, _, ti = peer(i)
        for f in range(3):
            if f in hooks:
                hooks[f]()
            lanes = slice(f * SLAB, (f + 1) * SLAB)
            hidden = dot_nn(mid_low[...], wup[span(ti * WIDTH, WIDTH), lanes])
            back = dot_nt(cot[...], wdown[span(ti * WIDTH + f * SLAB, SLAB), :])
            cdf = 0.5 + 0.5 * lax.erf(hidden * math.sqrt(0.5))
            pdf = jnp.exp2(hidden * hidden * (-0.5 * LOG2E)) * (1.0 / math.sqrt(2.0 * math.pi))
            act[i, :, lanes] = (hidden * cdf).astype(BF16)
            hid_grad[:, lanes] = (back * (cdf + hidden * pdf)).astype(BF16)
        for s in range(3):
            lanes = slice(s * SLAB, (s + 1) * SLAB)
            up = dot_nt(hid_grad[...], wup[span(ti * WIDTH + s * SLAB, SLAB), :])
            if i == 1:
                acc_b[:, lanes] = up
            else:
                acc_b[:, lanes] += up
        for b in range(2):
            lanes = slice(b * 384, (b + 1) * 384)
            red_down.put(dot_tn(cot[:, lanes], act[i]), 4 * b, xi, i % 2)
            red_up.put(dot_tn(mid_low[:, lanes], hid_grad[...]), 4 * b, xi, i % 2)

    for gat in ff_weights:
        gat.ready(0)
        gat.ready(1)
    feed_forward(1, {})
    red_down.send_core("near")
    red_up.send_core("near")
    feed_forward(0, {1: gat_down[0].step2, 2: gat_down[1].step2})
    for gat in gat_down:
        gat.step3()
    gat_up[1].step3()
    red_down.add_core("near")
    red_up.add_core("near")
    for gat in ff_weights:
        gat.ready(3)
    feed_forward(3, {})
    red_down.send_core("far")
    red_up.send_core("far")
    feed_forward(2, {})
    for gat in ff_weights:
        gat.finish()
    pl.semaphore_signal(free, inc=1, device_id=where["c"], device_id_type=MESH)
    red_down.add_core("far")

    def finish_block(s):
        lanes = slice(s * SLAB, (s + 1) * SLAB)
        for b in range(2):
            rows = slice(b * SLAB, (b + 1) * SLAB)
            total = None
            for i in range(4):
                _, _, ti = peer(i)
                part = dot_nn(act[i, rows, :], wdown[span(ti * WIDTH, WIDTH), lanes])
                total = part if i == 0 else total + part
            stage[rows, lanes] = (mid[rows, lanes] + total).astype(BF16)

    def norm_back(grad, hat, rstd, gain):
        e = grad * gain
        mean_e = jnp.mean(e, axis=-1, keepdims=True)
        mean_eh = jnp.mean(e * hat, axis=-1, keepdims=True)
        return rstd * (e - mean_e - hat * mean_eh)

    def column_sum(values):
        return jnp.sum(values, axis=0, keepdims=True)

    gain_sum = jnp.zeros((1, WIDTH), F32)
    bias_sum = jnp.zeros((1, WIDTH), F32)
    for b in range(4):
        at = slice(b * 128, (b + 1) * 128)
        grad = acc_b[at, :]
        hat, rstd = normalize(mid[at, :])
        total = cot[at, :].astype(F32) + norm_back(grad, hat, rstd, gain1)
        gain_sum = gain_sum + column_sum(grad * hat)
        bias_sum = bias_sum + column_sum(grad)
        acc_b[at, :] = total
        mid_low[at, :] = total.astype(BF16)
    red_up.add_core("far")
    norm_sum[...] = jnp.zeros((8, WIDTH), F32)
    norm_sum[1:2, :] = gain_sum
    norm_sum[3:4, :] = bias_sum

    for i in range(4):
        _, _, ti = peer(i)
        hid_grad[:, i * PART : (i + 1) * PART] = dot_nt(
            mid_low[...], wout[span(ti * PART, PART), :]
        ).astype(BF16)

    def grads_of(i, j, rows):
        lanes = slice(j * HEAD_DIM, (j + 1) * HEAD_DIM)
        grad = hid_grad[rows, i * PART + j * HEAD_DIM : i * PART + (j + 1) * HEAD_DIM]
        inner = jnp.sum(grad.astype(F32) * att[i, rows, lanes].astype(F32), axis=-1, keepdims=True)
        high, middle, low = pieces(-inner)
        both = jnp.concatenate([grad, grad], axis=1)
        head_lanes = jnp.where(
            lane == 0,
            high,
            jnp.where(lane == 1, middle, jnp.where(lane == 2, low, jnp.zeros_like(both))),
        )
        return jnp.where(low_lane, head_lanes, both)

    def projection_grads(j, groups):
        def lanes_of(first):
            return [att[i, :, first : first + HEAD_DIM] for i in groups]

        query = jnp.concatenate(lanes_of(PART + j * HEAD_DIM), axis=1)
        mixed = jnp.concatenate(lanes_of(j * HEAD_DIM), axis=1)
        both = jnp.concatenate([dkvs[i, :, j * 128 : (j + 1) * 128] for i in groups], axis=1)
        for b in range(2):
            lanes = slice(b * 384, (b + 1) * 384)
            qs_grad = dot_tn(normed[own_rows, lanes], query)
            out_grad = dot_tn(mid_low[:, lanes], mixed)
            kv = dot_tn(normed[:, lanes], both)
            for n, i in enumerate(groups):
                pair = slice(n // 2 * 128, n // 2 * 128 + 128)
                q, o = qs_grad[:, pair], out_grad[:, pair]
                if n % 2 == 0:
                    qo = jnp.where(low_lane, q, pltpu.roll(o, HEAD_DIM, 1))
                else:
                    qo = jnp.where(low_lane, pltpu.roll(q, HEAD_DIM, 1), o)
                xi, _, _ = peer(i)
                value = jnp.concatenate([qo, kv[:, n * 128 : (n + 1) * 128]], axis=1)
                red_io[j].put(value, 4 * b, xi, i % 2)

    def far(j):
        projection_grads(j, (3, 2))
        red_io[j].send_core("far")

    def near(j):
        projection_grads(j, (1, 0))
        red_io[j].send_core("near")

    def both_sides(j):
        if j == 0:
            red_down.finish_core()
            red_up.finish_core()
            pl.semaphore_wait(free, 1)
        projection_grads(j, (3, 2, 1, 0))
        red_io[j].send_core("far")
        red_io[j].send_core("near")

    def add_both(j):
        red_io[j].add_core("far")
        red_io[j].add_core("near")

    def step(red, *what):
        for third, stage in what:
            red.step(third, stage)

    plan = {
        3: [lambda: finish_block(0)],
        4: [lambda: step(red_down, (1, 1), (2, 1))],
        8: [lambda: step(red_down, (0, 1))],
        9: [lambda: both_sides(0)],
        10: [lambda: step(red_up, (1, 1), (2, 1)), lambda: finish_block(1)],
        11: [lambda: add_both(0)],
        13: [lambda: step(red_down, (1, 2), (0, 2))],
        15: [lambda: step(red_up, (0, 1))],
        16: [lambda: step(red_up, (1, 2))],
        17: [lambda: both_sides(1)],
        18: [lambda: step(red_down, (2, 2)), lambda: finish_block(2)],
        19: [lambda: add_both(1)],
        20: [lambda: step(red_up, (0, 2)), lambda: step(red_down, (0, 3))],
        21: [lambda: far(2)],
        22: [lambda: step(red_up, (2, 2)), lambda: step(red_down, (1, 3))],
        23: [lambda: red_io[2].add_core("far"), lambda: step(red_io[0], (1, 1), (2, 1))],
        25: [lambda: near(2), lambda: step(red_down, (2, 3))],
    }
    items = [(i, j, b) for j in range(3) for i in (3, 2, 1, 0) for b in range(2)]
    raw, ready, sums = {}, {}, None
    for n in range(len(items) + 2):
        if n < len(items):
            i, j, b = items[n]
            head, rows = 3 * i + j, slice(b * SLAB, (b + 1) * SLAB)
            both = grads_of(i, j, rows)
            raw[n] = dot_nt(qs[head, rows, :], keys_of(head)), dot_nt(both, values_of(head)), both
        if n >= 2:
            i, j, b = items[n - 2]
            head, rows = 3 * i + j, slice(b * SLAB, (b + 1) * SLAB)
            probs, score_grads, both = ready.pop(n - 2)
            att[i, rows, PART + j * HEAD_DIM : PART + (j + 1) * HEAD_DIM] = (
                dot_nn(score_grads, keys_of(head))[:, :HEAD_DIM] * HEAD_DIM ** (-0.5)
            ).astype(BF16)
            key_part = dot_tn(score_grads, qs[head, rows, :])
            value_part = dot_tn(probs, both)
            if b == 0:
                sums = key_part, value_part
            else:
                dkvs[i, :, j * 128 : (j + 1) * 128] = jnp.where(
                    low_lane, (sums[0] + key_part) * LN2, sums[1] + value_part
                ).astype(BF16)
        if 1 <= n <= len(items):
            score, prob_grad, both = raw.pop(n - 1)
            probs = jnp.exp2(score)
            ready[n - 1] = probs.astype(BF16), (probs * prob_grad).astype(BF16), both
        for event in plan.get(n, ()):
            event()

    def share_rows(n):
        lanes = slice(n * SLAB, (n + 1) * SLAB)
        total = None
        for i in range(4):
            _, _, ti = peer(i)
            part = dot_nn(dkvs[i, other_rows, :], key_value_weights(ti, lanes))
            total = part if i == 0 else total + part
        mid_low[:, lanes] = total.astype(BF16)

    block_store = m.local(stage, block_out)
    share_rows(0)
    red_io[2].add_core("near")
    step(red_io[2], (0, 1))
    step(red_io[0], (0, 1))
    share_rows(1)
    step(red_io[1], (1, 1), (2, 1))
    step(red_up, (0, 3), (1, 3))
    share_rows(2)
    dn_copy = m.remote(mid_low, cot, core_sent, m.slot(), "c")
    step(red_io[1], (0, 1))

    def own_grads(n):
        lanes = slice(n * SLAB, (n + 1) * SLAB)
        total = None
        for i in range(4):
            _, _, ti = peer(i)
            part = dot_nn(att[i, :, PART:], win[0, span(ti * PART, PART), lanes]) + dot_nn(
                dkvs[i, own_rows, :], key_value_weights(ti, lanes)
            )
            total = part if i == 0 else total + part
        acc_c[:, lanes] = total

    sums = [jnp.zeros((1, WIDTH), F32), jnp.zeros((1, WIDTH), F32)]

    def finish_rows(b):
        at = slice(b * 128, (b + 1) * 128)
        grad = acc_c[at, :] + cot[at, :].astype(F32)
        hat, rstd = normalize(tokens[at, :].astype(F32))
        hid_grad[at, :] = (acc_b[at, :] + norm_back(grad, hat, rstd, gain0)).astype(BF16)
        sums[0] = sums[0] + column_sum(grad * hat)
        sums[1] = sums[1] + column_sum(grad)

    own_grads(0)
    step(red_up, (2, 3))
    step(red_io[0], (1, 2))
    own_grads(1)
    step(red_io[2], (1, 1), (2, 1))
    step(red_io[0], (0, 2), (2, 2))
    own_grads(2)
    step(red_io[1], (1, 2), (0, 2))
    dn_copy.wait_recv()
    finish_rows(0)
    finish_rows(1)
    step(red_io[2], (0, 2))
    finish_rows(2)
    finish_rows(3)
    norm_sum[0:1, :] = sums[0]
    norm_sum[2:3, :] = sums[1]
    share_sent = m.slot()
    rounds = (
        (0, 4, t, ("c", "x", "xc"), m.slot()),
        (4, 2, y, ("y",), m.slot()),
        (6, 4, 2 * h + l, ("l", "h", "lh"), m.slot()),
    )

    def share(n):
        if n > 0:
            first, size, _, peers, slot = rounds[n - 1]
            m.wait(slot, norm_box.at[pl.ds(0, len(peers))])
            total = norm_box[first]
            for k in range(1, size):
                total = total + norm_box[first + k]
            norm_sum[...] = total
        if n < 3:
            first, _, mine, peers, slot = rounds[n]
            norm_box[first + mine] = norm_sum[...]
            for to in peers:
                m.remote(norm_box.at[first + mine], norm_box.at[first + mine], share_sent, slot, to)

    share(0)
    stores = [block_store, m.local(hid_grad, input_grad)]
    red_down.last()
    down_store = m.local(res_ff, grad_down)
    step(red_io[0], (0, 3), (1, 3), (2, 3))
    step(red_io[2], (1, 2), (2, 2))
    step(red_io[1], (2, 2))
    share(1)
    step(red_io[1], (0, 3), (1, 3))
    step(red_io[2], (0, 3))
    step(red_io[1], (2, 3))
    step(red_io[2], (1, 3))
    share(2)
    step(red_io[2], (2, 3))
    down_store.wait()
    red_up.last()
    stores.append(m.local(res_ff, grad_up))
    for j in range(3):
        red_io[j].last()
        lanes = slice(j * HEAD_DIM, (j + 1) * HEAD_DIM)
        block = res_io[...]
        for k, part in enumerate((0, 2, 3)):
            res_in[k, :, lanes] = block[:, part * HEAD_DIM : (part + 1) * HEAD_DIM]
        res_out[:, lanes] = block[:, HEAD_DIM : 2 * HEAD_DIM]
        if j == 1:
            share(3)
            stores.append(m.local(norm_sum, grad_norm))
    stores.append(m.local(res_in, grad_in))
    stores.append(m.local(res_out, grad_out))
    gat_out.finish()
    for gat in gat_in:
        gat.finish()
    for red in red_io:
        red.finish_core()
    for red in (red_down, red_up, *red_io):
        red.finish()
    m.wait(share_sent, norm_box.at[pl.ds(0, 7)])
    m.wait(core_sent, normed)
    for store in stores:
        store.wait()


def write_results(*refs):
    sources, targets, stages = refs[:7], refs[7:15], refs[15:22]
    out, gains, biases, sems = refs[22], refs[23], refs[24], refs[25]
    loads = [pltpu.make_async_copy(a, b, sems.at[k]) for k, (a, b) in enumerate(zip(sources, stages))]
    for copy in loads:
        copy.start()
    loads[5].wait()
    out[...] = stages[5][...].T
    loads[6].wait()
    gains[...] = stages[6][0:2, :]
    biases[...] = stages[6][2:4, :]
    done = [*stages[:5], out, gains, biases]
    stores = [pltpu.make_async_copy(a, b, sems.at[7 + k]) for k, (a, b) in enumerate(zip(done, targets))]
    for k in (5, 6, 7):
        stores[k].start()
    for k in range(5):
        loads[k].wait()
        stores[k].start()
    for copy in stores:
        copy.wait()


def fused(tokens, gene_counts, in_proj, out_proj, up_proj, down_proj, gains, biases, cotangent):
    vmem = pl.BlockSpec(memory_space=pltpu.VMEM)
    hbm = pl.BlockSpec(memory_space=pl.ANY)
    shape = jax.ShapeDtypeStruct
    outs = pl.pallas_call(
        kernel,
        out_shape=(
            shape((ROWS, WIDTH), BF16),
            shape((ROWS, WIDTH), BF16),
            shape((3, CHUNK, PART), F32),
            shape((CHUNK, WIDTH), F32),
            shape((CHUNK, WIDTH), F32),
            shape((CHUNK, PART), F32),
            shape((8, WIDTH), F32),
        ),
        in_specs=[pl.BlockSpec(memory_space=pltpu.SMEM)] + [hbm] * 6 + [vmem] * 2,
        out_specs=[hbm] * 7,
        scratch_shapes=[
            pltpu.VMEM((ROWS, WIDTH), BF16),
            pltpu.VMEM((2 * ROWS, WIDTH), BF16),
            pltpu.VMEM((ROWS, WIDTH), BF16),
            pltpu.VMEM((3, WIDTH, WIDTH), BF16),
            pltpu.VMEM((WIDTH, WIDTH), BF16),
            pltpu.VMEM((4 * WIDTH, WIDTH), BF16),
            pltpu.VMEM((4 * WIDTH, WIDTH), BF16),
            pltpu.VMEM((12, ROWS, 2 * HEAD_DIM), BF16),
            pltpu.VMEM((12, 2 * ROWS, 2 * HEAD_DIM), BF16),
            pltpu.VMEM((2 * ROWS, 2 * HEAD_DIM), BF16),
            pltpu.VMEM((4, ROWS, 2 * PART), BF16),
            pltpu.VMEM((ROWS, WIDTH), F32),
            pltpu.VMEM((ROWS, WIDTH), BF16),
            pltpu.VMEM((ROWS, WIDTH), BF16),
            pltpu.VMEM((4, ROWS, WIDTH), BF16),
            pltpu.VMEM((ROWS, WIDTH), BF16),
            pltpu.VMEM((ROWS, WIDTH), F32),
            pltpu.VMEM((ROWS, WIDTH), F32),
            pltpu.VMEM((4, 2 * ROWS, 2 * PART), BF16),
            pltpu.VMEM((4 * WIDTH, WIDTH), BF16),
            pltpu.VMEM((4 * WIDTH, WIDTH), BF16),
            pltpu.VMEM((31 * CHUNK, WIDTH), BF16),
            pltpu.VMEM((31 * CHUNK, WIDTH), BF16),
            pltpu.VMEM((CHUNK, SLAB), F32),
            pltpu.VMEM((CHUNK, WIDTH), F32),
            pltpu.VMEM((3, CHUNK, PART), F32),
            pltpu.VMEM((CHUNK, PART), F32),
            pltpu.VMEM((10, 8, WIDTH), F32),
            pltpu.VMEM((8, WIDTH), F32),
            pltpu.SemaphoreType.REGULAR,
            pltpu.SemaphoreType.DMA((SEMAPHORES,)),
        ],
        compiler_params=pltpu.CompilerParams(
            collective_id=0, has_side_effects=True, vmem_limit_bytes=64 * 2**20
        ),
    )(
        gene_counts,
        tokens,
        cotangent,
        jnp.swapaxes(in_proj, 1, 2),
        out_proj,
        up_proj,
        down_proj,
        gains,
        biases,
    )
    results = pl.pallas_call(
        write_results,
        out_shape=(
            *(shape(o.shape, o.dtype) for o in outs[:5]),
            shape((PART, CHUNK), F32),
            shape((2, WIDTH), F32),
            shape((2, WIDTH), F32),
        ),
        in_specs=[hbm] * 7,
        out_specs=[hbm] * 8,
        scratch_shapes=[
            *(pltpu.VMEM(o.shape, o.dtype) for o in outs),
            pltpu.VMEM((PART, CHUNK), F32),
            pltpu.VMEM((2, WIDTH), F32),
            pltpu.VMEM((2, WIDTH), F32),
            pltpu.SemaphoreType.DMA((15,)),
        ],
    )(*outs)
    block_out, input_grad, grad_in, grad_up, grad_down, grad_out, grad_gains, grad_biases = results
    return (
        block_out,
        input_grad,
        grad_in,
        grad_out,
        grad_up,
        grad_down.T,
        grad_gains,
        grad_biases,
    )


def layer_norm(values, gain, offset):
    center = values - jnp.mean(values, axis=-1, keepdims=True)
    spread = jnp.mean(center * center, axis=-1, keepdims=True)
    return center * lax.rsqrt(spread + EPS) * gain + offset


def gelu_exact(values):
    return jax.nn.gelu(values, approximate=False)


def per_device(
    tokens, gene_counts, in_proj, out_proj, up_proj, down_proj, gains, biases, cotangent
):
    rows = tokens.shape[0]
    cells = gene_counts.shape[0]
    group = rows * lax.axis_size("tensor")
    length = group // cells
    local_width = out_proj.shape[0]
    heads = local_width // HEAD_DIM
    block = min(length, 512)
    blocks = length // block
    scale = HEAD_DIM ** (-0.5)
    positions = jnp.arange(length, dtype=jnp.int32)
    resid = tokens.astype(jnp.float32)
    normed, first_back = jax.vjp(layer_norm, resid, gains[0], biases[0])
    normed_all = lax.all_gather(normed.astype(jnp.bfloat16), "tensor", axis=0, tiled=True)
    projected = jnp.einsum(
        "td,cde->cte", normed_all, in_proj, preferred_element_type=jnp.float32
    ).astype(jnp.bfloat16)
    query_cells = projected[0].reshape(cells, blocks, block, local_width)
    key_cells = projected[1].reshape(cells, length, local_width)
    value_cells = projected[2].reshape(cells, length, local_width)

    def block_scores(query_block, key_rows, count):
        query_heads = query_block.reshape(block, heads, HEAD_DIM)
        key_heads = key_rows.reshape(length, heads, HEAD_DIM)
        scores = (
            jnp.einsum("qhd,khd->hqk", query_heads, key_heads, preferred_element_type=jnp.float32)
            * scale
        )
        return jnp.where((positions < count)[None, None, :], scores, NEG)

    def cell_forward(item):
        queries, key_rows, value_rows, count = item
        value_heads = value_rows.reshape(length, heads, HEAD_DIM)

        def one_block(query_block):
            scores = block_scores(query_block, key_rows, count)
            top = jnp.max(scores, axis=-1, keepdims=True)
            expo = jnp.exp(scores - top)
            total = jnp.sum(expo, axis=-1, keepdims=True)
            probs = (expo / total).astype(jnp.bfloat16)
            result = jnp.einsum(
                "hqk,khd->qhd", probs, value_heads, preferred_element_type=jnp.float32
            )
            return (
                result.reshape(block, local_width).astype(jnp.bfloat16),
                (top + jnp.log(total))[..., 0],
            )

        return lax.map(one_block, queries)

    attended, log_totals = lax.map(cell_forward, (query_cells, key_cells, value_cells, gene_counts))
    attended = attended.reshape(group, local_width)
    piece = attended
    mid = resid + lax.psum_scatter(
        jnp.dot(piece, out_proj, preferred_element_type=jnp.float32),
        "tensor",
        scatter_dimension=0,
        tiled=True,
    )
    normed_mid, second_back = jax.vjp(layer_norm, mid, gains[1], biases[1])
    mid_low = normed_mid.astype(jnp.bfloat16)
    mid_all = lax.all_gather(mid_low, "tensor", axis=0, tiled=True)
    hidden = jnp.dot(mid_all, up_proj, preferred_element_type=jnp.float32)
    active = gelu_exact(hidden).astype(jnp.bfloat16)
    piece = active
    block_out = (
        mid
        + lax.psum_scatter(
            jnp.dot(piece, down_proj, preferred_element_type=jnp.float32).astype(jnp.bfloat16),
            "tensor",
            scatter_dimension=0,
            tiled=True,
        ).astype(jnp.float32)
    ).astype(jnp.bfloat16)
    out_grads = lax.all_gather(cotangent, "tensor", axis=0, tiled=True)
    _, gelu_back = jax.vjp(gelu_exact, hidden)
    active_grad = jnp.einsum("td,fd->tf", out_grads, down_proj, preferred_element_type=jnp.float32)
    hidden_grad = gelu_back(active_grad)[0].astype(jnp.bfloat16)
    grad_down = jnp.einsum("tf,td->fd", active, out_grads, preferred_element_type=jnp.float32)
    grad_up = jnp.einsum("td,tf->df", mid_all, hidden_grad, preferred_element_type=jnp.float32)
    piece = hidden_grad
    mid_grad = lax.psum_scatter(
        jnp.einsum("tf,df->td", piece, up_proj, preferred_element_type=jnp.float32),
        "tensor",
        scatter_dimension=0,
        tiled=True,
    )
    resid_part, gain_second, bias_second = second_back(mid_grad)
    mid_total = cotangent.astype(jnp.float32) + resid_part
    branch_all = lax.all_gather(mid_total.astype(jnp.bfloat16), "tensor", axis=0, tiled=True)
    attended_grad = jnp.einsum(
        "td,ed->te", branch_all, out_proj, preferred_element_type=jnp.float32
    ).astype(jnp.bfloat16)
    grad_out = jnp.einsum("te,td->ed", attended, branch_all, preferred_element_type=jnp.float32)

    def cell_backward(item):
        queries, key_rows, value_rows, count, grad_rows, totals = item
        key_heads = key_rows.reshape(length, heads, HEAD_DIM)
        value_heads = value_rows.reshape(length, heads, HEAD_DIM)

        def one_block(carry, part):
            key_sum, value_sum = carry
            query_block, grad_block, total_block = part
            scores = block_scores(query_block, key_rows, count)
            probs = jnp.exp(scores - total_block[..., None])
            grad_heads = grad_block.reshape(block, heads, HEAD_DIM)
            query_heads = query_block.reshape(block, heads, HEAD_DIM)
            prob_grads = jnp.einsum(
                "qhd,khd->hqk", grad_heads, value_heads, preferred_element_type=jnp.float32
            )
            inner = jnp.sum(probs * prob_grads, axis=-1, keepdims=True)
            score_grads = (probs * (prob_grads - inner)).astype(jnp.bfloat16)
            query_grad = (
                jnp.einsum(
                    "hqk,khd->qhd", score_grads, key_heads, preferred_element_type=jnp.float32
                )
                * scale
            )
            key_sum = (
                key_sum
                + jnp.einsum(
                    "hqk,qhd->khd", score_grads, query_heads, preferred_element_type=jnp.float32
                )
                * scale
            )
            value_sum = value_sum + jnp.einsum(
                "hqk,qhd->khd",
                probs.astype(jnp.bfloat16),
                grad_heads,
                preferred_element_type=jnp.float32,
            )
            return (
                (key_sum, value_sum),
                query_grad.reshape(block, local_width).astype(jnp.bfloat16),
            )

        zeros = jnp.zeros((length, heads, HEAD_DIM), jnp.float32)
        (key_sum, value_sum), query_grads = lax.scan(
            one_block, (zeros, zeros), (queries, grad_rows, totals)
        )
        return (
            query_grads.reshape(length, local_width),
            key_sum.reshape(length, local_width).astype(jnp.bfloat16),
            value_sum.reshape(length, local_width).astype(jnp.bfloat16),
        )

    grad_cells = attended_grad.reshape(cells, blocks, block, local_width)
    query_grads, key_grads, value_grads = lax.map(
        cell_backward, (query_cells, key_cells, value_cells, gene_counts, grad_cells, log_totals)
    )
    proj_grads = jnp.stack(
        [
            query_grads.reshape(group, local_width),
            key_grads.reshape(group, local_width),
            value_grads.reshape(group, local_width),
        ]
    )
    grad_in = jnp.einsum("td,cte->cde", normed_all, proj_grads, preferred_element_type=jnp.float32)
    piece = proj_grads
    normed_grad = lax.psum_scatter(
        jnp.einsum("cte,cde->td", piece, in_proj, preferred_element_type=jnp.float32),
        "tensor",
        scatter_dimension=0,
        tiled=True,
    )
    resid_grad, gain_first, bias_first = first_back(normed_grad)
    input_grad = (mid_total + resid_grad).astype(jnp.bfloat16)
    grad_gains, grad_biases = lax.psum(
        (jnp.stack([gain_first, gain_second]), jnp.stack([bias_first, bias_second])),
        ("dp", "tensor"),
    )
    grad_in_part, grad_out_part, grad_up_part, grad_down_part = (
        lax.psum_scatter(grad_in, "dp", scatter_dimension=1, tiled=True),
        lax.psum_scatter(grad_out, "dp", scatter_dimension=1, tiled=True),
        lax.psum_scatter(grad_up, "dp", scatter_dimension=0, tiled=True),
        lax.psum_scatter(grad_down, "dp", scatter_dimension=1, tiled=True),
    )
    return (
        block_out,
        input_grad,
        grad_in_part,
        grad_out_part,
        grad_up_part,
        grad_down_part,
        grad_gains,
        grad_biases,
    )


def solution(mesh):
    placed = (
        P(("dp", "tensor"), None),
        P("dp"),
        P(None, None, "tensor"),
        P("tensor", None),
        P(None, "tensor"),
        P("tensor", None),
        P(),
        P(),
        P(("dp", "tensor"), None),
    )
    halves = mesh.shape["dp"] == 8 and mesh.shape["tensor"] == 4
    return jax.shard_map(
        fused if halves else per_device,
        mesh=mesh,
        in_specs=placed,
        out_specs=(
            P(("dp", "tensor"), None),
            P(("dp", "tensor"), None),
            P(None, "dp", "tensor"),
            P("tensor", "dp"),
            P("dp", "tensor"),
            P("tensor", "dp"),
            P(),
            P(),
        ),
        check_vma=False,
    )
```

```python
import itertools
import math

import jax
import jax.numpy as jnp
from jax import lax
from jax.experimental import pallas as pl
from jax.experimental.pallas import tpu as pltpu
from jax.sharding import PartitionSpec as P

HEAD_DIM = 64
EPS = 1e-05
NEG = -1e30
F32 = jnp.float32
BF16 = jnp.bfloat16
MESH = pl.DeviceIdType.MESH
LOG2E = math.log2(math.e)
LN2 = math.log(2.0)
ROWS = 512
WIDTH = 768
PART = 192
CHUNK = 96
SLAB = 256
THIRD = 32
ORDERS = ("xylh", "ylxh", "lxyh")
WEIGHT = {"x": 8, "y": 4, "l": 2, "h": 1}
BOX = (0, 16, 24, 28, 30)
SEMAPHORES = 148


def dot_nn(left, right):
    return lax.dot_general(left, right, (((1,), (0,)), ((), ())), preferred_element_type=F32)


def dot_nt(left, right):
    return lax.dot_general(left, right, (((1,), (1,)), ((), ())), preferred_element_type=F32)


def dot_tn(left, right):
    return lax.dot_general(left, right, (((0,), (0,)), ((), ())), preferred_element_type=F32)


def span(start, size):
    return pl.ds(pl.multiple_of(start, size), size)


def normalize(values):
    center = values - jnp.mean(values, axis=-1, keepdims=True)
    spread = jnp.mean(center * center, axis=-1, keepdims=True)
    rstd = lax.rsqrt(spread + EPS)
    return center * rstd, rstd


def pieces(values):
    high = values.astype(BF16)
    rest = values - high.astype(F32)
    middle = rest.astype(BF16)
    low = (rest - middle.astype(F32)).astype(BF16)
    return high, middle, low


class Mover:
    def __init__(self, where, sems):
        self.where, self.sems, self.count = where, sems, 0

    def slot(self):
        self.count += 1
        assert self.count <= SEMAPHORES
        return self.count - 1

    def remote(self, source, target, sent, arrived, to):
        copy = pltpu.make_async_remote_copy(
            src_ref=source,
            dst_ref=target,
            send_sem=self.sems.at[sent],
            recv_sem=self.sems.at[arrived],
            device_id=self.where[to],
            device_id_type=MESH,
        )
        copy.start()
        return copy

    def local(self, source, target):
        copy = pltpu.make_async_copy(source, target, self.sems.at[self.slot()])
        copy.start()
        return copy

    def wait(self, slot, like):
        pltpu.make_async_copy(like, like, self.sems.at[slot]).wait()


class Gather:
    def __init__(self, mover, place, shard, full, view, halves):
        self.m, self.p, self.shard, self.full, self.view = mover, place, shard, full, view
        self.halves = halves
        forward = ("yf", "zf") if halves else ("x1",)
        self.slots = {k: mover.slot() for k in ("x0", "y", "z", "own", "core", *forward)}
        self.sent = mover.slot()
        self.copies = {}
        self.quarter = {k: place[k] for k in ("q", "qy", "qz", "qd")}

    def go(self, key, source, target, to):
        arrived = self.slots["core" if key[0] == "c" else key]
        self.copies[key] = self.m.remote(source, target, self.sent, arrived, to)

    def start_own(self):
        p = self.p
        mine = self.view(self.full, p["t"], 0, 4)
        self.load = self.m.local(self.view(self.shard, None, 0, 4), mine)
        self.go("own", self.view(self.shard, None, 0, 4), mine, "c")

    def start_x(self, key="x0", quarter="q"):
        p = self.p
        self.go(key, self.view(self.shard, None, p[quarter], 1), self.view(self.full, p["t"], p[quarter], 1), "x")

    def start_x1(self):
        self.start_x("x1", "qd")

    def pass_on(self, key, quarter, to, half=None):
        part = self.view(self.full, self.p["t2"], self.quarter[quarter], 1, half)
        self.go(key, part, part, to)

    def step1(self):
        self.copies["x0"].wait_recv()
        self.pass_on("y", "q", "y")
        self.pass_on("z", "q", "l")
        self.pass_on("c0", "q", "c")

    def step2(self):
        self.copies["y"].wait_recv()
        if self.halves:
            self.pass_on("zf", "qy", "l", 0)
        self.pass_on("c1", "qy", "c")
        self.copies["z"].wait_recv()
        if self.halves:
            self.pass_on("yf", "qz", "y", 1)
        self.pass_on("c2", "qz", "c")

    def step3(self):
        if self.halves:
            self.copies["zf"].wait_recv()
            self.copies["yf"].wait_recv()
        else:
            self.copies["x1"].wait_recv()
        self.pass_on("c3", "qd", "c")

    def finish(self):
        self.m.wait(self.sent, self.view(self.full, 0, 0, 12))

    def ready(self, i):
        if i == 0:
            self.load.wait()
        if i == 1:
            self.copies["own"].wait_recv()
        if i == 3:
            self.m.wait(self.slots["core"], self.view(self.full, self.p["t"], 0, 4))


class Reduce:
    def __init__(self, mover, place, own, away, inbox, result):
        self.m, self.p, self.own, self.away = mover, place, own, away
        self.inbox, self.result = inbox, result
        self.slots = {key: mover.slot() for key in ("near", "far", "last")}
        self.slots |= {(third, stage): mover.slot() for third in range(3) for stage in (1, 2, 3)}
        self.sent, self.core_sent = mover.slot(), mover.slot()

    def at(self, place, third, chunk, count):
        ref, half = place
        start = third * 32 * THIRD + half * 16 * THIRD + chunk * THIRD
        return ref.at[pl.ds(pl.multiple_of(start, THIRD), count * THIRD), :]

    def box(self, third, at, count):
        return pl.ds((third * 31 + at) * THIRD, count * THIRD)

    def put(self, value, first, x, away):
        for k in range(value.shape[0] // CHUNK):
            r = first + k
            chunk = 8 * x + 4 * (r % 2) + 2 * ((r // 2) % 2) + r // 4
            for third in range(3):
                start = k * CHUNK + third * THIRD
                target = self.at(self.away if away else self.own, third, chunk, 1)
                target[...] = value[start : start + THIRD, :].astype(BF16)

    def go(self, slot, third, source, at, count, to):
        self.m.remote(
            source,
            self.inbox.at[self.box(third, at, count), :],
            self.core_sent if to == "c" else self.sent,
            self.slots[slot],
            to,
        )

    def arrived(self, slot, count):
        self.m.wait(self.slots[slot], self.inbox.at[pl.ds(0, count * THIRD), :])

    def finish_core(self):
        self.m.wait(self.core_sent, self.inbox.at[pl.ds(0, 48 * THIRD), :])

    def finish(self):
        self.m.wait(self.sent, self.inbox.at[pl.ds(0, 45 * THIRD), :])

    def halves(self, side):
        return (self.p["x"], 0) if side == "near" else (1 - self.p["x"], 8)

    def send_core(self, side):
        x, at = self.halves(side)
        for third in range(3):
            self.go(side, third, self.at(self.away, third, 8 * x, 8), at, 8, "c")

    def add(self, third, chunk, count, at):
        here = self.at(self.own, third, chunk, count)
        here[...] = here[...] + self.inbox[self.box(third, at, count), :]

    def add_core(self, side):
        x, at = self.halves(side)
        self.arrived(side, 24)
        for third in range(3):
            self.add(third, 8 * x, 8, at)
            self.send(third, 1, side)

    def runs(self, third, stage):
        order = ORDERS[third]
        dim, fixed = order[stage - 1], order[: stage - 1]
        rest, count = list("xylh"), 1
        while rest and rest[-1] != dim and rest[-1] not in fixed:
            rest.pop()
            count *= 2
        free = [name for name in rest if name != dim and name not in fixed]
        found = []
        for values in itertools.product((0, 1), repeat=len(free)):
            flip = dict(zip(free, values))
            base = 0
            for name in rest:
                if name != dim:
                    own = self.p[name]
                    base = base + WEIGHT[name] * (1 - own if flip.get(name) else own)
            own = WEIGHT[dim] * self.p[dim]
            side = "far" if flip.get("x", dim == "x") else "near"
            found.append((base + own, base + WEIGHT[dim] - own, count, BOX[stage] + len(found) * count, side))
        return found

    def send(self, third, stage, side=None):
        slot = (third, stage) if stage < 4 else "last"
        for _, away, count, at, where in self.runs(third, stage):
            if side in (None, where):
                source = self.at(self.own, third, away, count)
                self.go(slot, third, source, at, count, ORDERS[third][stage - 1])

    def step(self, third, stage):
        self.arrived((third, stage), 16 >> stage)
        for keep, _, count, at, _ in self.runs(third, stage):
            self.add(third, keep, count, at)
        self.send(third, stage + 1)

    def last(self):
        self.arrived("last", 3)
        for third in range(3):
            ((keep, _, _, at, _),) = self.runs(third, 4)
            total = self.at(self.own, third, keep, 1)[...].astype(F32) + self.inbox[
                self.box(third, at, 1), :
            ].astype(F32)
            self.result[third * THIRD : (third + 1) * THIRD, :] = total


def kernel(
    counts,
    tokens_in,
    cot_in,
    win_in,
    wout_in,
    wup_in,
    wdown_in,
    gains_in,
    biases_in,
    block_out,
    input_grad,
    grad_in,
    grad_up,
    grad_down,
    grad_out,
    grad_norm,
    gains,
    biases,
    tokens,
    normed,
    cot,
    win,
    wout,
    wup,
    wdown,
    qs,
    kvs,
    key_tail,
    att,
    mid,
    mid_low,
    stage,
    act,
    hid_grad,
    acc_b,
    acc_c,
    dkvs,
    g_down,
    g_up,
    in_down,
    in_up,
    res_io,
    res_ff,
    res_in,
    res_out,
    norm_box,
    norm_sum,
    free,
    sems,
):
    d = lax.axis_index("dp")
    t = lax.axis_index("tensor")
    x = lax.div(t, 2)
    c = t - 2 * x
    y = lax.rem(d, 2)
    l = lax.rem(lax.div(d, 2), 2)
    h = lax.div(d, 4)
    where = {
        "c": (d, t + 1 - 2 * c),
        "x": (d, t + 2 - 4 * x),
        "y": (d + 1 - 2 * y, t),
        "l": (d + 2 - 4 * l, t),
        "h": (d + 4 - 8 * h, t),
        "xc": (d, 3 - t),
        "lh": (d + 2 - 4 * l + 4 - 8 * h, t),
    }
    place = {"x": x, "c": c, "y": y, "l": l, "h": h, "t": t, "t2": t + 2 - 4 * x}
    place["q"] = 2 * l + y
    place["qy"] = 2 * l + 1 - y
    place["qz"] = 2 * (1 - l) + y
    place["qd"] = 2 * (1 - l) + 1 - y
    m = Mover(where, sems)
    own_rows = span(c * ROWS, ROWS)
    other_rows = span((1 - c) * ROWS, ROWS)

    def view_in(lane):
        def view(ref, dev, first, parts, half=None):
            start, size = first * 48, parts * 48
            if half is not None:
                start, size = start + half * 16, 32 if half else 16
            start = start if dev is None else dev * PART + start
            return ref.at[:, pl.ds(pl.multiple_of(start, 16), size), pl.ds(lane * 384, 384)]

        return view

    def view_out(ref, dev, first, parts, half=None):
        start = first * 48
        rows = pl.ds(pl.multiple_of(start if dev is None else dev * PART + start, 48), parts * 48)
        return ref.at[rows, :]

    def view_up(lane):
        def view(ref, dev, first, parts, half=None):
            start, size = first * PART, parts * PART
            if half is not None:
                start, size = start + half * CHUNK, CHUNK
            start = start if dev is None else dev * WIDTH + start
            return ref.at[pl.ds(pl.multiple_of(start, CHUNK), size), pl.ds(lane * 384, 384)]

        return view

    barrier = pltpu.get_barrier_semaphore()
    for to in where:
        pl.semaphore_signal(barrier, inc=1, device_id=where[to], device_id_type=MESH)
    tok_load = m.local(tokens_in, tokens)
    small_loads = [m.local(gains_in, gains), m.local(biases_in, biases)]
    pl.semaphore_wait(barrier, len(where))
    gat_in = [Gather(m, place, win_in, win, view_in(k), k == 0) for k in range(2)]
    gat_out = Gather(m, place, wout_in, wout, view_out, False)
    gat_up = [Gather(m, place, wup_in, wup, view_up(k), True) for k in range(2)]
    gat_down = [Gather(m, place, wdown_in, wdown, view_up(k), False) for k in range(2)]
    ff_weights = [*gat_up, *gat_down]
    for gat in gat_in:
        gat.start_x()
    gat_in[1].start_x1()
    core_sent = m.slot()
    tok_copy = m.remote(tokens_in, mid_low, core_sent, m.slot(), "c")
    for gat in gat_in:
        gat.start_own()
    gat_out.start_x()
    gat_out.start_x1()
    for gat in ff_weights:
        gat.start_x()
    for gat in gat_down:
        gat.start_x1()
    cot_load = m.local(cot_in, cot)
    for gat in (gat_out, *ff_weights):
        gat.start_own()

    for load in small_loads:
        load.wait()
    gain0, bias0 = gains[0:1, :], biases[0:1, :]
    gain1, bias1 = gains[1:2, :], biases[1:2, :]

    def norm_rows(source, first):
        @pl.loop(0, ROWS // 64, unroll=2)
        def _(k):
            hat, _ = normalize(source[span(k * 64, 64), :].astype(F32))
            normed[span(first + k * 64, 64), :] = (hat * gain0 + bias0).astype(BF16)

    tok_load.wait()
    norm_rows(tokens, c * ROWS)
    tok_copy.wait_recv()
    norm_rows(mid_low, (1 - c) * ROWS)

    count = counts[x]
    lane = lax.broadcasted_iota(jnp.int32, (1, 2 * HEAD_DIM), 1)
    low_lane = lane < HEAD_DIM

    @pl.loop(0, 2 * ROWS // 128)
    def _(k):
        at = k * 128 + lax.broadcasted_iota(jnp.int32, (128, 2 * HEAD_DIM), 0)
        column = lax.broadcasted_iota(jnp.int32, (128, 2 * HEAD_DIM), 1)
        key_tail[span(k * 128, 128), :] = jnp.where(
            column == HEAD_DIM,
            jnp.where(at < count, 0.0, NEG),
            jnp.where(column < HEAD_DIM + 4, 1.0, 0.0),
        ).astype(BF16)

    value_tail = jnp.where(lane < 3, 1.0, 0.0).astype(BF16)
    query_tail = jnp.where(lane[:, :HEAD_DIM] == 0, 1.0, 0.0).astype(BF16)

    def keys_of(head):
        return jnp.where(low_lane, kvs[head], key_tail[...])

    def values_of(head):
        return jnp.where(low_lane, value_tail, kvs[head])

    def peer(i):
        xi = x if i < 2 else 1 - x
        ci = c if i % 2 == 0 else 1 - c
        return xi, ci, 2 * xi + ci

    def key_value_weights(ti, lanes):
        parts = []
        for j in range(3):
            rows = pl.ds(pl.multiple_of(ti * PART + j * HEAD_DIM, HEAD_DIM), HEAD_DIM)
            parts += [win[1, rows, lanes], win[2, rows, lanes]]
        return jnp.concatenate(parts, axis=0)

    def project(i):
        _, _, ti = peer(i)
        part = span(ti * PART, PART)
        q = dot_nt(normed[own_rows, :], win[0, part, :]) * (HEAD_DIM ** (-0.5) * LOG2E)
        q = q.astype(BF16)
        kv = dot_nt(normed[...], key_value_weights(ti, slice(None))).astype(BF16)
        for j in range(3):
            lanes = slice(j * HEAD_DIM, (j + 1) * HEAD_DIM)
            qs[3 * i + j] = jnp.concatenate(
                [q[:, lanes], jnp.broadcast_to(query_tail, (ROWS, HEAD_DIM))], axis=1
            )
            kvs[3 * i + j] = kv[:, j * 128 : (j + 1) * 128]

    items = [(i, j, b) for i in range(4) for j in range(3) for b in range(2)]
    hooks = {
        0: [lambda: gat_in[0].ready(0), lambda: gat_in[1].ready(0)],
        1: [gat_in[0].step1],
        3: [gat_in[1].step1],
        6: [lambda: gat_in[0].ready(1), lambda: gat_in[1].ready(1)],
        7: [gat_in[0].step2],
        9: [gat_in[1].step2, gat_out.step1],
        12: [gat_in[0].step3, gat_in[1].step3],
        13: [gat_out.step2, gat_out.step3],
        14: [gat_up[0].step1],
        18: [gat_up[1].step1, lambda: gat_in[0].ready(3), lambda: gat_in[1].ready(3)],
        20: [gat_up[0].step2],
        22: [gat_down[0].step1],
        25: [gat_down[1].step1],
    }
    scores, tops, expos, keys = {}, {}, {}, None
    for n in range(len(items) + 2):
        for hook in hooks.get(n, ()):
            hook()
        if n < len(items):
            i, j, b = items[n]
            if n % 6 == 0:
                project(i)
            if b == 0:
                keys = keys_of(3 * i + j)
            scores[n] = dot_nt(qs[3 * i + j, b * SLAB : (b + 1) * SLAB, :], keys)
        if n >= 2:
            i, j, b = items[n - 2]
            head, rows = 3 * i + j, slice(b * SLAB, (b + 1) * SLAB)
            mixed = dot_nn(expos.pop(n - 2), values_of(head))
            total = mixed[:, 0:1]
            att[i, rows, j * HEAD_DIM : (j + 1) * HEAD_DIM] = (mixed * (1.0 / total))[
                :, HEAD_DIM:
            ].astype(BF16)
            high, middle, low = pieces(-(tops.pop(n - 2) + jnp.log2(total)))
            qs[head, rows, :] = jnp.where(
                lane == HEAD_DIM + 1,
                high,
                jnp.where(
                    lane == HEAD_DIM + 2,
                    middle,
                    jnp.where(lane == HEAD_DIM + 3, low, qs[head, rows, :]),
                ),
            )
        if 1 <= n <= len(items):
            score = scores.pop(n - 1)
            tops[n - 1] = jnp.max(score, axis=-1, keepdims=True)
            expos[n - 1] = jnp.exp2(score - tops[n - 1]).astype(BF16)
    for i in (0, 1, 3):
        gat_out.ready(i)
    for b in range(2):
        at = slice(b * SLAB, (b + 1) * SLAB)
        total = tokens[at, :].astype(F32)
        for i in range(4):
            _, _, ti = peer(i)
            total = total + dot_nn(att[i, at, :PART], wout[span(ti * PART, PART), :])
        mid[at, :] = total
        hat, _ = normalize(total)
        mid_low[at, :] = (hat * gain1 + bias1).astype(BF16)
    cot_load.wait()

    red_down = Reduce(m, place, (g_down, c), (g_down, 1 - c), in_down, res_ff)
    red_up = Reduce(m, place, (g_up, c), (g_up, 1 - c), in_up, res_ff)
    red_io = []
    for j in range(3):
        lanes = slice(j * SLAB, (j + 1) * SLAB)
        red_io.append(
            Reduce(
                m, place, (g_down.at[:, lanes], 1 - c), (g_up.at[:, lanes], 1 - c), wup.at[:, lanes], res_io
            )
        )

    def feed_forward(i, hooks):
        xi, _, ti = peer(i)
        for f in range(3):
            if f in hooks:
                hooks[f]()
            lanes = slice(f * SLAB, (f + 1) * SLAB)
            hidden = dot_nn(mid_low[...], wup[span(ti * WIDTH, WIDTH), lanes])
            back = dot_nt(cot[...], wdown[span(ti * WIDTH + f * SLAB, SLAB), :])
            cdf = 0.5 + 0.5 * lax.erf(hidden * math.sqrt(0.5))
            pdf = jnp.exp2(hidden * hidden * (-0.5 * LOG2E)) * (1.0 / math.sqrt(2.0 * math.pi))
            act[i, :, lanes] = (hidden * cdf).astype(BF16)
            hid_grad[:, lanes] = (back * (cdf + hidden * pdf)).astype(BF16)
        for s in range(3):
            lanes = slice(s * SLAB, (s + 1) * SLAB)
            up = dot_nt(hid_grad[...], wup[span(ti * WIDTH + s * SLAB, SLAB), :])
            if i == 1:
                acc_b[:, lanes] = up
            else:
                acc_b[:, lanes] += up
        for b in range(2):
            lanes = slice(b * 384, (b + 1) * 384)
            red_down.put(dot_tn(cot[:, lanes], act[i]), 4 * b, xi, i % 2)
            red_up.put(dot_tn(mid_low[:, lanes], hid_grad[...]), 4 * b, xi, i % 2)

    for gat in ff_weights:
        gat.ready(0)
        gat.ready(1)
    feed_forward(1, {0: gat_up[1].step2, 1: gat_up[0].step3})
    red_down.send_core("near")
    red_up.send_core("near")
    feed_forward(0, {1: gat_down[0].step2, 2: gat_down[1].step2})
    for gat in gat_down:
        gat.step3()
    gat_up[1].step3()
    red_down.add_core("near")
    red_up.add_core("near")
    for gat in ff_weights:
        gat.ready(3)
    feed_forward(3, {})
    red_down.send_core("far")
    red_up.send_core("far")
    feed_forward(2, {})
    for gat in ff_weights:
        gat.finish()
    pl.semaphore_signal(free, inc=1, device_id=where["c"], device_id_type=MESH)
    red_down.add_core("far")

    def finish_block(s):
        lanes = slice(s * SLAB, (s + 1) * SLAB)
        for b in range(2):
            rows = slice(b * SLAB, (b + 1) * SLAB)
            total = None
            for i in range(4):
                _, _, ti = peer(i)
                part = dot_nn(act[i, rows, :], wdown[span(ti * WIDTH, WIDTH), lanes])
                total = part if i == 0 else total + part
            stage[rows, lanes] = (mid[rows, lanes] + total).astype(BF16)

    def norm_back(grad, hat, rstd, gain):
        e = grad * gain
        mean_e = jnp.mean(e, axis=-1, keepdims=True)
        mean_eh = jnp.mean(e * hat, axis=-1, keepdims=True)
        return rstd * (e - mean_e - hat * mean_eh)

    def column_sum(values):
        return jnp.sum(values, axis=0, keepdims=True)

    gain_sum = jnp.zeros((1, WIDTH), F32)
    bias_sum = jnp.zeros((1, WIDTH), F32)
    for b in range(4):
        at = slice(b * 128, (b + 1) * 128)
        grad = acc_b[at, :]
        hat, rstd = normalize(mid[at, :])
        total = cot[at, :].astype(F32) + norm_back(grad, hat, rstd, gain1)
        gain_sum = gain_sum + column_sum(grad * hat)
        bias_sum = bias_sum + column_sum(grad)
        acc_b[at, :] = total
        mid_low[at, :] = total.astype(BF16)
    red_up.add_core("far")
    norm_sum[...] = jnp.zeros((8, WIDTH), F32)
    norm_sum[1:2, :] = gain_sum
    norm_sum[3:4, :] = bias_sum

    for i in range(4):
        _, _, ti = peer(i)
        hid_grad[:, i * PART : (i + 1) * PART] = dot_nt(
            mid_low[...], wout[span(ti * PART, PART), :]
        ).astype(BF16)

    def grads_of(i, j, rows):
        lanes = slice(j * HEAD_DIM, (j + 1) * HEAD_DIM)
        grad = hid_grad[rows, i * PART + j * HEAD_DIM : i * PART + (j + 1) * HEAD_DIM]
        inner = jnp.sum(grad.astype(F32) * att[i, rows, lanes].astype(F32), axis=-1, keepdims=True)
        high, middle, low = pieces(-inner)
        both = jnp.concatenate([grad, grad], axis=1)
        head_lanes = jnp.where(
            lane == 0,
            high,
            jnp.where(lane == 1, middle, jnp.where(lane == 2, low, jnp.zeros_like(both))),
        )
        return jnp.where(low_lane, head_lanes, both)

    def projection_grads(j, groups):
        def lanes_of(first):
            return [att[i, :, first : first + HEAD_DIM] for i in groups]

        query = jnp.concatenate(lanes_of(PART + j * HEAD_DIM), axis=1)
        mixed = jnp.concatenate(lanes_of(j * HEAD_DIM), axis=1)
        both = jnp.concatenate([
                dkvs[:, (3 * i + j) * 128 : (3 * i + j + 1) * 128] for i in groups
            ], axis=1)
        for b in range(2):
            lanes = slice(b * 384, (b + 1) * 384)
            qs_grad = dot_tn(normed[own_rows, lanes], query)
            out_grad = dot_tn(mid_low[:, lanes], mixed)
            kv = dot_tn(normed[:, lanes], both)
            for n, i in enumerate(groups):
                pair = slice(n // 2 * 128, n // 2 * 128 + 128)
                q, o = qs_grad[:, pair], out_grad[:, pair]
                if n % 2 == 0:
                    qo = jnp.where(low_lane, q, pltpu.roll(o, HEAD_DIM, 1))
                else:
                    qo = jnp.where(low_lane, pltpu.roll(q, HEAD_DIM, 1), o)
                xi, _, _ = peer(i)
                value = jnp.concatenate([qo, kv[:, n * 128 : (n + 1) * 128]], axis=1)
                red_io[j].put(value, 4 * b, xi, i % 2)

    def far(j):
        projection_grads(j, (3, 2))
        red_io[j].send_core("far")

    def near(j):
        projection_grads(j, (1, 0))
        red_io[j].send_core("near")

    def both_sides(j):
        if j == 0:
            red_down.finish_core()
            red_up.finish_core()
            pl.semaphore_wait(free, 1)
        projection_grads(j, (3, 2, 1, 0))
        red_io[j].send_core("far")
        red_io[j].send_core("near")

    def add_both(j):
        red_io[j].add_core("far")
        red_io[j].add_core("near")

    def step(red, *what):
        for third, stage in what:
            red.step(third, stage)

    plan = {
        3: [lambda: finish_block(0)],
        4: [lambda: step(red_down, (1, 1), (2, 1))],
        8: [lambda: step(red_down, (0, 1))],
        9: [lambda: both_sides(0)],
        10: [lambda: step(red_up, (1, 1), (2, 1))],
        11: [lambda: add_both(0)],
        13: [lambda: step(red_down, (1, 2), (0, 2))],
        15: [lambda: step(red_up, (0, 1))],
        16: [lambda: step(red_up, (1, 2))],
        17: [lambda: both_sides(1)],
        18: [lambda: step(red_down, (2, 2))],
        19: [lambda: add_both(1)],
        20: [lambda: step(red_up, (0, 2)), lambda: step(red_down, (0, 3))],
        21: [lambda: far(2)],
        22: [lambda: step(red_up, (2, 2)), lambda: step(red_down, (1, 3))],
        23: [lambda: red_io[2].add_core("far"), lambda: step(red_io[0], (1, 1), (2, 1))],
        25: [lambda: near(2), lambda: step(red_down, (2, 3))],
    }
    items = [(i, j, b) for j in range(3) for i in (3, 2, 1, 0) for b in range(2)]
    raw, ready, sums = {}, {}, None
    for n in range(len(items) + 2):
        if n < len(items):
            i, j, b = items[n]
            head, rows = 3 * i + j, slice(b * SLAB, (b + 1) * SLAB)
            both = grads_of(i, j, rows)
            raw[n] = dot_nt(qs[head, rows, :], keys_of(head)), dot_nt(both, values_of(head)), both
        if n >= 2:
            i, j, b = items[n - 2]
            head, rows = 3 * i + j, slice(b * SLAB, (b + 1) * SLAB)
            probs, score_grads, both = ready.pop(n - 2)
            att[i, rows, PART + j * HEAD_DIM : PART + (j + 1) * HEAD_DIM] = (
                dot_nn(score_grads, keys_of(head))[:, :HEAD_DIM] * HEAD_DIM ** (-0.5)
            ).astype(BF16)
            key_part = dot_tn(score_grads, qs[head, rows, :])
            value_part = dot_tn(probs, both)
            if b == 0:
                sums = key_part, value_part
            else:
                dkvs[:, head * 128 : (head + 1) * 128] = jnp.where(
                    low_lane, (sums[0] + key_part) * LN2, sums[1] + value_part
                ).astype(BF16)
        if 1 <= n <= len(items):
            score, prob_grad, both = raw.pop(n - 1)
            probs = jnp.exp2(score)
            ready[n - 1] = probs.astype(BF16), (probs * prob_grad).astype(BF16), both
        for event in plan.get(n, ()):
            event()

    def all_key_value_weights(lanes):
        return jnp.concatenate([key_value_weights(peer(i)[2], lanes) for i in range(4)], axis=0)

    def share_rows(n):
        lanes = slice(n * SLAB, (n + 1) * SLAB)
        mid_low[:, lanes] = dot_nn(dkvs[other_rows, :], all_key_value_weights(lanes)).astype(BF16)

    share_rows(0)
    red_io[2].add_core("near")
    step(red_io[0], (0, 1))
    share_rows(1)
    step(red_io[2], (0, 1))
    step(red_io[1], (1, 1), (2, 1))
    step(red_up, (0, 3), (1, 3))
    share_rows(2)
    dn_copy = m.remote(mid_low, cot, core_sent, m.slot(), "c")
    step(red_io[1], (0, 1))

    def own_grads(n):
        lanes = slice(n * SLAB, (n + 1) * SLAB)
        total = dot_nn(dkvs[own_rows, :], all_key_value_weights(lanes))
        for i in range(4):
            _, _, ti = peer(i)
            total = total + dot_nn(att[i, :, PART:], win[0, span(ti * PART, PART), lanes])
        acc_c[:, lanes] = total

    sums = [jnp.zeros((1, WIDTH), F32), jnp.zeros((1, WIDTH), F32)]

    def finish_rows(b):
        at = slice(b * 128, (b + 1) * 128)
        grad = acc_c[at, :] + cot[at, :].astype(F32)
        hat, rstd = normalize(tokens[at, :].astype(F32))
        hid_grad[at, :] = (acc_b[at, :] + norm_back(grad, hat, rstd, gain0)).astype(BF16)
        sums[0] = sums[0] + column_sum(grad * hat)
        sums[1] = sums[1] + column_sum(grad)

    own_grads(0)
    step(red_up, (2, 3))
    step(red_io[0], (1, 2))
    own_grads(1)
    step(red_io[2], (1, 1), (2, 1))
    step(red_io[0], (0, 2), (2, 2))
    own_grads(2)
    step(red_io[1], (1, 2), (0, 2))
    dn_copy.wait_recv()
    finish_rows(0)
    finish_rows(1)
    step(red_io[2], (0, 2))
    finish_rows(2)
    finish_rows(3)
    norm_sum[0:1, :] = sums[0]
    norm_sum[2:3, :] = sums[1]
    share_sent = m.slot()
    rounds = (
        (0, 4, t, ("c", "x", "xc"), m.slot()),
        (4, 2, y, ("y",), m.slot()),
        (6, 4, 2 * h + l, ("l", "h", "lh"), m.slot()),
    )

    def share(n):
        if n > 0:
            first, size, _, peers, slot = rounds[n - 1]
            m.wait(slot, norm_box.at[pl.ds(0, len(peers))])
            total = norm_box[first]
            for k in range(1, size):
                total = total + norm_box[first + k]
            norm_sum[...] = total
        if n < 3:
            first, _, mine, peers, slot = rounds[n]
            norm_box[first + mine] = norm_sum[...]
            for to in peers:
                m.remote(norm_box.at[first + mine], norm_box.at[first + mine], share_sent, slot, to)

    share(0)
    stores = [m.local(hid_grad, input_grad)]
    red_down.last()
    down_store = m.local(res_ff, grad_down)
    step(red_io[0], (1, 3))
    step(red_io[1], (2, 2))
    step(red_io[2], (2, 2), (1, 2))
    step(red_io[0], (2, 3))
    finish_block(1)
    share(1)
    step(red_io[0], (0, 3))
    step(red_io[1], (0, 3), (1, 3), (2, 3))
    step(red_io[2], (0, 3))
    share(2)
    step(red_io[2], (1, 3))
    down_store.wait()
    red_up.last()
    stores.append(m.local(res_ff, grad_up))
    step(red_io[2], (2, 3))
    finish_block(2)
    stores.append(m.local(stage, block_out))
    for j in range(3):
        red_io[j].last()
        lanes = slice(j * HEAD_DIM, (j + 1) * HEAD_DIM)
        block = res_io[...]
        for k, part in enumerate((0, 2, 3)):
            res_in[k, :, lanes] = block[:, part * HEAD_DIM : (part + 1) * HEAD_DIM]
        res_out[:, lanes] = block[:, HEAD_DIM : 2 * HEAD_DIM]
        if j == 1:
            share(3)
            stores.append(m.local(norm_sum, grad_norm))
    stores.append(m.local(res_in, grad_in))
    stores.append(m.local(res_out, grad_out))
    gat_out.finish()
    for gat in gat_in:
        gat.finish()
    for red in red_io:
        red.finish_core()
    for red in (red_down, red_up, *red_io):
        red.finish()
    m.wait(share_sent, norm_box.at[pl.ds(0, 7)])
    m.wait(core_sent, normed)
    for store in stores:
        store.wait()


def write_results(*refs):
    sources, targets, stages = refs[:7], refs[7:15], refs[15:22]
    out, gains, biases, sems = refs[22], refs[23], refs[24], refs[25]
    loads = [pltpu.make_async_copy(a, b, sems.at[k]) for k, (a, b) in enumerate(zip(sources, stages))]
    for copy in loads:
        copy.start()
    loads[5].wait()
    out[...] = stages[5][...].T
    loads[6].wait()
    gains[...] = stages[6][0:2, :]
    biases[...] = stages[6][2:4, :]
    done = [*stages[:5], out, gains, biases]
    stores = [pltpu.make_async_copy(a, b, sems.at[7 + k]) for k, (a, b) in enumerate(zip(done, targets))]
    for k in (5, 6, 7):
        stores[k].start()
    for k in range(5):
        loads[k].wait()
        stores[k].start()
    for copy in stores:
        copy.wait()


def fused(tokens, gene_counts, in_proj, out_proj, up_proj, down_proj, gains, biases, cotangent):
    hbm = pl.BlockSpec(memory_space=pl.ANY)
    shape = jax.ShapeDtypeStruct
    outs = pl.pallas_call(
        kernel,
        out_shape=(
            shape((ROWS, WIDTH), BF16),
            shape((ROWS, WIDTH), BF16),
            shape((3, CHUNK, PART), F32),
            shape((CHUNK, WIDTH), F32),
            shape((CHUNK, WIDTH), F32),
            shape((CHUNK, PART), F32),
            shape((8, WIDTH), F32),
        ),
        in_specs=[pl.BlockSpec(memory_space=pltpu.SMEM)] + [hbm] * 8,
        out_specs=[hbm] * 7,
        scratch_shapes=[
            pltpu.VMEM((2, WIDTH), F32),
            pltpu.VMEM((2, WIDTH), F32),
            pltpu.VMEM((ROWS, WIDTH), BF16),
            pltpu.VMEM((2 * ROWS, WIDTH), BF16),
            pltpu.VMEM((ROWS, WIDTH), BF16),
            pltpu.VMEM((3, WIDTH, WIDTH), BF16),
            pltpu.VMEM((WIDTH, WIDTH), BF16),
            pltpu.VMEM((4 * WIDTH, WIDTH), BF16),
            pltpu.VMEM((4 * WIDTH, WIDTH), BF16),
            pltpu.VMEM((12, ROWS, 2 * HEAD_DIM), BF16),
            pltpu.VMEM((12, 2 * ROWS, 2 * HEAD_DIM), BF16),
            pltpu.VMEM((2 * ROWS, 2 * HEAD_DIM), BF16),
            pltpu.VMEM((4, ROWS, 2 * PART), BF16),
            pltpu.VMEM((ROWS, WIDTH), F32),
            pltpu.VMEM((ROWS, WIDTH), BF16),
            pltpu.VMEM((ROWS, WIDTH), BF16),
            pltpu.VMEM((4, ROWS, WIDTH), BF16),
            pltpu.VMEM((ROWS, WIDTH), BF16),
            pltpu.VMEM((ROWS, WIDTH), F32),
            pltpu.VMEM((ROWS, WIDTH), F32),
            pltpu.VMEM((2 * ROWS, 8 * PART), BF16),
            pltpu.VMEM((4 * WIDTH, WIDTH), BF16),
            pltpu.VMEM((4 * WIDTH, WIDTH), BF16),
            pltpu.VMEM((31 * CHUNK, WIDTH), BF16),
            pltpu.VMEM((31 * CHUNK, WIDTH), BF16),
            pltpu.VMEM((CHUNK, SLAB), F32),
            pltpu.VMEM((CHUNK, WIDTH), F32),
            pltpu.VMEM((3, CHUNK, PART), F32),
            pltpu.VMEM((CHUNK, PART), F32),
            pltpu.VMEM((10, 8, WIDTH), F32),
            pltpu.VMEM((8, WIDTH), F32),
            pltpu.SemaphoreType.REGULAR,
            pltpu.SemaphoreType.DMA((SEMAPHORES,)),
        ],
        compiler_params=pltpu.CompilerParams(
            collective_id=0, has_side_effects=True, vmem_limit_bytes=64 * 2**20
        ),
    )(
        gene_counts,
        tokens,
        cotangent,
        jnp.swapaxes(in_proj, 1, 2),
        out_proj,
        up_proj,
        down_proj,
        gains,
        biases,
    )
    results = pl.pallas_call(
        write_results,
        out_shape=(
            *(shape(o.shape, o.dtype) for o in outs[:5]),
            shape((PART, CHUNK), F32),
            shape((2, WIDTH), F32),
            shape((2, WIDTH), F32),
        ),
        in_specs=[hbm] * 7,
        out_specs=[hbm] * 8,
        scratch_shapes=[
            *(pltpu.VMEM(o.shape, o.dtype) for o in outs),
            pltpu.VMEM((PART, CHUNK), F32),
            pltpu.VMEM((2, WIDTH), F32),
            pltpu.VMEM((2, WIDTH), F32),
            pltpu.SemaphoreType.DMA((15,)),
        ],
    )(*outs)
    block_out, input_grad, grad_in, grad_up, grad_down, grad_out, grad_gains, grad_biases = results
    return (
        block_out,
        input_grad,
        grad_in,
        grad_out,
        grad_up,
        grad_down.T,
        grad_gains,
        grad_biases,
    )


def layer_norm(values, gain, offset):
    center = values - jnp.mean(values, axis=-1, keepdims=True)
    spread = jnp.mean(center * center, axis=-1, keepdims=True)
    return center * lax.rsqrt(spread + EPS) * gain + offset


def gelu_exact(values):
    return jax.nn.gelu(values, approximate=False)


def per_device(
    tokens, gene_counts, in_proj, out_proj, up_proj, down_proj, gains, biases, cotangent
):
    rows = tokens.shape[0]
    cells = gene_counts.shape[0]
    group = rows * lax.axis_size("tensor")
    length = group // cells
    local_width = out_proj.shape[0]
    heads = local_width // HEAD_DIM
    block = min(length, 512)
    blocks = length // block
    scale = HEAD_DIM ** (-0.5)
    positions = jnp.arange(length, dtype=jnp.int32)
    resid = tokens.astype(jnp.float32)
    normed, first_back = jax.vjp(layer_norm, resid, gains[0], biases[0])
    normed_all = lax.all_gather(normed.astype(jnp.bfloat16), "tensor", axis=0, tiled=True)
    projected = jnp.einsum(
        "td,cde->cte", normed_all, in_proj, preferred_element_type=jnp.float32
    ).astype(jnp.bfloat16)
    query_cells = projected[0].reshape(cells, blocks, block, local_width)
    key_cells = projected[1].reshape(cells, length, local_width)
    value_cells = projected[2].reshape(cells, length, local_width)

    def block_scores(query_block, key_rows, count):
        query_heads = query_block.reshape(block, heads, HEAD_DIM)
        key_heads = key_rows.reshape(length, heads, HEAD_DIM)
        scores = (
            jnp.einsum("qhd,khd->hqk", query_heads, key_heads, preferred_element_type=jnp.float32)
            * scale
        )
        return jnp.where((positions < count)[None, None, :], scores, NEG)

    def cell_forward(item):
        queries, key_rows, value_rows, count = item
        value_heads = value_rows.reshape(length, heads, HEAD_DIM)

        def one_block(query_block):
            scores = block_scores(query_block, key_rows, count)
            top = jnp.max(scores, axis=-1, keepdims=True)
            expo = jnp.exp(scores - top)
            total = jnp.sum(expo, axis=-1, keepdims=True)
            probs = (expo / total).astype(jnp.bfloat16)
            result = jnp.einsum(
                "hqk,khd->qhd", probs, value_heads, preferred_element_type=jnp.float32
            )
            return (
                result.reshape(block, local_width).astype(jnp.bfloat16),
                (top + jnp.log(total))[..., 0],
            )

        return lax.map(one_block, queries)

    attended, log_totals = lax.map(cell_forward, (query_cells, key_cells, value_cells, gene_counts))
    attended = attended.reshape(group, local_width)
    piece = attended
    mid = resid + lax.psum_scatter(
        jnp.dot(piece, out_proj, preferred_element_type=jnp.float32),
        "tensor",
        scatter_dimension=0,
        tiled=True,
    )
    normed_mid, second_back = jax.vjp(layer_norm, mid, gains[1], biases[1])
    mid_low = normed_mid.astype(jnp.bfloat16)
    mid_all = lax.all_gather(mid_low, "tensor", axis=0, tiled=True)
    hidden = jnp.dot(mid_all, up_proj, preferred_element_type=jnp.float32)
    active = gelu_exact(hidden).astype(jnp.bfloat16)
    piece = active
    block_out = (
        mid
        + lax.psum_scatter(
            jnp.dot(piece, down_proj, preferred_element_type=jnp.float32).astype(jnp.bfloat16),
            "tensor",
            scatter_dimension=0,
            tiled=True,
        ).astype(jnp.float32)
    ).astype(jnp.bfloat16)
    out_grads = lax.all_gather(cotangent, "tensor", axis=0, tiled=True)
    _, gelu_back = jax.vjp(gelu_exact, hidden)
    active_grad = jnp.einsum("td,fd->tf", out_grads, down_proj, preferred_element_type=jnp.float32)
    hidden_grad = gelu_back(active_grad)[0].astype(jnp.bfloat16)
    grad_down = jnp.einsum("tf,td->fd", active, out_grads, preferred_element_type=jnp.float32)
    grad_up = jnp.einsum("td,tf->df", mid_all, hidden_grad, preferred_element_type=jnp.float32)
    piece = hidden_grad
    mid_grad = lax.psum_scatter(
        jnp.einsum("tf,df->td", piece, up_proj, preferred_element_type=jnp.float32),
        "tensor",
        scatter_dimension=0,
        tiled=True,
    )
    resid_part, gain_second, bias_second = second_back(mid_grad)
    mid_total = cotangent.astype(jnp.float32) + resid_part
    branch_all = lax.all_gather(mid_total.astype(jnp.bfloat16), "tensor", axis=0, tiled=True)
    attended_grad = jnp.einsum(
        "td,ed->te", branch_all, out_proj, preferred_element_type=jnp.float32
    ).astype(jnp.bfloat16)
    grad_out = jnp.einsum("te,td->ed", attended, branch_all, preferred_element_type=jnp.float32)

    def cell_backward(item):
        queries, key_rows, value_rows, count, grad_rows, totals = item
        key_heads = key_rows.reshape(length, heads, HEAD_DIM)
        value_heads = value_rows.reshape(length, heads, HEAD_DIM)

        def one_block(carry, part):
            key_sum, value_sum = carry
            query_block, grad_block, total_block = part
            scores = block_scores(query_block, key_rows, count)
            probs = jnp.exp(scores - total_block[..., None])
            grad_heads = grad_block.reshape(block, heads, HEAD_DIM)
            query_heads = query_block.reshape(block, heads, HEAD_DIM)
            prob_grads = jnp.einsum(
                "qhd,khd->hqk", grad_heads, value_heads, preferred_element_type=jnp.float32
            )
            inner = jnp.sum(probs * prob_grads, axis=-1, keepdims=True)
            score_grads = (probs * (prob_grads - inner)).astype(jnp.bfloat16)
            query_grad = (
                jnp.einsum(
                    "hqk,khd->qhd", score_grads, key_heads, preferred_element_type=jnp.float32
                )
                * scale
            )
            key_sum = (
                key_sum
                + jnp.einsum(
                    "hqk,qhd->khd", score_grads, query_heads, preferred_element_type=jnp.float32
                )
                * scale
            )
            value_sum = value_sum + jnp.einsum(
                "hqk,qhd->khd",
                probs.astype(jnp.bfloat16),
                grad_heads,
                preferred_element_type=jnp.float32,
            )
            return (
                (key_sum, value_sum),
                query_grad.reshape(block, local_width).astype(jnp.bfloat16),
            )

        zeros = jnp.zeros((length, heads, HEAD_DIM), jnp.float32)
        (key_sum, value_sum), query_grads = lax.scan(
            one_block, (zeros, zeros), (queries, grad_rows, totals)
        )
        return (
            query_grads.reshape(length, local_width),
            key_sum.reshape(length, local_width).astype(jnp.bfloat16),
            value_sum.reshape(length, local_width).astype(jnp.bfloat16),
        )

    grad_cells = attended_grad.reshape(cells, blocks, block, local_width)
    query_grads, key_grads, value_grads = lax.map(
        cell_backward, (query_cells, key_cells, value_cells, gene_counts, grad_cells, log_totals)
    )
    proj_grads = jnp.stack(
        [
            query_grads.reshape(group, local_width),
            key_grads.reshape(group, local_width),
            value_grads.reshape(group, local_width),
        ]
    )
    grad_in = jnp.einsum("td,cte->cde", normed_all, proj_grads, preferred_element_type=jnp.float32)
    piece = proj_grads
    normed_grad = lax.psum_scatter(
        jnp.einsum("cte,cde->td", piece, in_proj, preferred_element_type=jnp.float32),
        "tensor",
        scatter_dimension=0,
        tiled=True,
    )
    resid_grad, gain_first, bias_first = first_back(normed_grad)
    input_grad = (mid_total + resid_grad).astype(jnp.bfloat16)
    grad_gains, grad_biases = lax.psum(
        (jnp.stack([gain_first, gain_second]), jnp.stack([bias_first, bias_second])),
        ("dp", "tensor"),
    )
    grad_in_part, grad_out_part, grad_up_part, grad_down_part = (
        lax.psum_scatter(grad_in, "dp", scatter_dimension=1, tiled=True),
        lax.psum_scatter(grad_out, "dp", scatter_dimension=1, tiled=True),
        lax.psum_scatter(grad_up, "dp", scatter_dimension=0, tiled=True),
        lax.psum_scatter(grad_down, "dp", scatter_dimension=1, tiled=True),
    )
    return (
        block_out,
        input_grad,
        grad_in_part,
        grad_out_part,
        grad_up_part,
        grad_down_part,
        grad_gains,
        grad_biases,
    )


def solution(mesh):
    placed = (
        P(("dp", "tensor"), None),
        P("dp"),
        P(None, None, "tensor"),
        P("tensor", None),
        P(None, "tensor"),
        P("tensor", None),
        P(),
        P(),
        P(("dp", "tensor"), None),
    )
    halves = mesh.shape["dp"] == 8 and mesh.shape["tensor"] == 4
    return jax.shard_map(
        fused if halves else per_device,
        mesh=mesh,
        in_specs=placed,
        out_specs=(
            P(("dp", "tensor"), None),
            P(("dp", "tensor"), None),
            P(None, "dp", "tensor"),
            P("tensor", "dp"),
            P("dp", "tensor"),
            P("tensor", "dp"),
            P(),
            P(),
        ),
        check_vma=False,
    )
```
